32 devices in a mesh: blk: 16 (over z, y, x), grp: 2 (over core).
Axes of the slice: x: 2, y: 2, z: 4, core: 2. Of those that a mesh axis runs over, the one named last changes fastest.
Arguments:
- points: bfloat16 [64, 4096], P(None, ('blk', 'grp')), may hold values from -6 to 6
- right_side: float32 [16, 4096], P(None, ('blk', 'grp')), may hold values from -18 to 18
- lengthscale: float32 [1], replicated, may hold values from 3.3110573 to 4.0550324
- outputscale: float32 [1], replicated, may hold values from 0.6 to 1.6
- noise_level: float32 [1], replicated, may hold values from 0.4 to 1
Outputs:
- solution: float32 [16, 4096], P(None, ('blk', 'grp'))
- residual: float32 [16, 4096], P(None, ('blk', 'grp'))
- gradient: float32 [3], replicated
The draws below stay inside these ranges and needn't reach their ends.
All inputs are finite; a program needn't handle non-finite values.
Results may differ from the reference program's by a relative error of at most 0.001.
The reference program's roundings to bfloat16 on the way count: a program that leaves them out, or rounds other values in their place, can miss the bound.
Values may be sent and summed in bfloat16 or wider, within the bound.
No kernel may reach another device: no remote copies, remote signals or barrier semaphores. Data moves between devices by JAX's collectives and lax.ppermute only.
A program may use at most 64 MiB of HBM per device.

```python
import math
import jax
import jax.numpy as jnp
from jax import lax

DIMS = 64
COLS = 16
ITERS = 2
NPTS = 4096


def draw_points(key, part):
    drawn = jnp.clip(jax.random.normal(key, (DIMS, NPTS), jnp.float32), -6.0, 6.0)
    return drawn.astype(jnp.bfloat16)


def draw_right_side(key, part):
    second_key = jax.random.fold_in(key, 12)
    rising = jnp.exp(math.log(3.0) * jnp.arange(NPTS, dtype=jnp.float32) / max(NPTS - 1, 1))
    drawn = jnp.clip(jax.random.normal(second_key, (COLS, NPTS), jnp.float32), -6.0, 6.0)
    return jnp.clip(drawn * rising[None, :], -18.0, 18.0)


def draw_lengthscale(key, part):
    target = 3.177 * float(NPTS) ** 0.0927
    factor = jax.random.uniform(key, (1,), jnp.float32, 0.9, 1.1)
    return (math.sqrt(10.0 * DIMS) / target * factor).astype(jnp.float32)


def setup_inputs(seed: int = 0) -> dict:
    seeds = jax.random.split(jax.random.key(seed), 6)
    points = draw_points(jax.random.fold_in(seeds[5], 71), 0)
    right_side = draw_right_side(jax.random.fold_in(seeds[5], 71), 0)
    lengthscale = draw_lengthscale(jax.random.fold_in(seeds[5], 71), 0)
    outputscale = jnp.clip(jnp.exp(jax.random.uniform(seeds[3], (1,), jnp.float32, math.log(0.6), math.log(1.6))), 0.6, 1.6)
    noise_level = jnp.clip(jnp.exp(jax.random.uniform(seeds[4], (1,), jnp.float32, math.log(0.4), math.log(1.0))), 0.4, 1.0)
    return {"points": points, "right_side": right_side, "lengthscale": lengthscale, "outputscale": outputscale, "noise_level": noise_level}


def kernel_product(vectors, points_full, squares, scale_len, with_grad):
    rounded = lax.optimization_barrier(vectors.astype(jnp.bfloat16)).astype(jnp.float32)
    block_rows = math.gcd(NPTS, 512)
    block_count = NPTS // block_rows

    def one_block(block_index):
        offset = (block_index * block_rows).astype(jnp.int32)
        row_points = lax.dynamic_slice_in_dim(points_full, offset, block_rows, 1)
        row_squares = lax.dynamic_slice_in_dim(squares, offset, block_rows, 0)
        inner_prod = jnp.dot(row_points.T, points_full, precision=lax.Precision.HIGHEST)
        distance = jnp.maximum(row_squares[:, None] + squares[None, :] - 2.0 * inner_prod, 0.0)
        radius = jnp.sqrt(5.0 * distance) / scale_len
        damping = jnp.exp(-radius)
        kernel_tile = (1.0 + radius + radius * radius / 3.0) * damping
        kernel_tile = lax.optimization_barrier(kernel_tile.astype(jnp.bfloat16)).astype(jnp.float32)
        pieces_out = [jnp.dot(rounded, kernel_tile.T, precision=lax.Precision.HIGHEST)]
        if with_grad:
            slope_tile = radius * radius * (1.0 + radius) * damping / (3.0 * scale_len)
            slope_tile = lax.optimization_barrier(slope_tile.astype(jnp.bfloat16)).astype(jnp.float32)
            pieces_out.append(jnp.dot(rounded, slope_tile.T, precision=lax.Precision.HIGHEST))
        return jnp.concatenate(pieces_out, axis=0)
    stacked = lax.map(one_block, jnp.arange(block_count, dtype=jnp.int32))
    return jnp.moveaxis(stacked, 0, 1).reshape(stacked.shape[1], NPTS)

def reference(points, right_side, lengthscale, outputscale, noise_level):
    points_full = points.astype(jnp.float32)
    squares = lax.optimization_barrier(jnp.sum(points_full * points_full, axis=0))
    scale_len = lengthscale[0]
    amplitude = outputscale[0]
    jitter = noise_level[0]

    def system(vectors):
        return amplitude * kernel_product(vectors, points_full, squares, scale_len, False) + jitter * vectors
    solution = jnp.zeros_like(right_side)
    residual = right_side
    direction = right_side
    norm_now = lax.optimization_barrier(jnp.sum(residual * residual, axis=1))
    for iteration in range(ITERS):
        applied = system(direction)
        curvature = lax.optimization_barrier(jnp.sum(direction * applied, axis=1))
        step_size = norm_now / curvature
        solution = solution + step_size[:, None] * direction
        residual = residual - step_size[:, None] * applied
        if iteration + 1 < ITERS:
            norm_next = lax.optimization_barrier(jnp.sum(residual * residual, axis=1))
            direction = residual + (norm_next / norm_now)[:, None] * direction
            norm_now = norm_next
    products_out = kernel_product(solution, points_full, squares, scale_len, True)
    kernel_part = products_out[:COLS]
    slope_part = products_out[COLS:]
    left_side = jnp.concatenate([solution[:1], right_side[1:]], axis=0)
    weights = jnp.where(jnp.arange(COLS, dtype=jnp.int32) == 0, 1.0, -1.0 / (COLS - 1)).astype(jnp.float32)[:, None]
    local_terms = jnp.stack([jnp.sum(weights * left_side * amplitude * slope_part), jnp.sum(weights * left_side * kernel_part), jnp.sum(weights * left_side * solution)])
    gradient = 0.5 * local_terms / NPTS
    return (solution, residual, gradient)
```

```python
import functools
import math

import jax
import jax.numpy as jnp
from jax import lax
from jax.experimental import pallas as pl
from jax.experimental.pallas import tpu as pltpu
from jax.sharding import PartitionSpec as P

F32 = jnp.float32
BF16 = jnp.bfloat16
LOG2E = math.log2(math.e)
TINY = 1e-36
NT = (((1,), (1,)), ((), ()))


def _vmem(count):
    return [pl.BlockSpec(memory_space=pltpu.VMEM) for _ in range(count)]


def _smem():
    return pl.BlockSpec(memory_space=pltpu.SMEM)


def pack_kernel(points_ref, right_ref, out_ref):
    feats = points_ref.shape[0]
    cols = right_ref.shape[0]
    right = right_ref[...]
    high = right.astype(BF16)
    low = (right - high.astype(F32)).astype(BF16)
    points = points_ref[...]
    for peer in range(out_ref.shape[0]):
        out_ref[peer, 0:feats, :] = points
        out_ref[peer, feats : feats + cols, :] = high
        out_ref[peer, feats + cols : feats + 2 * cols, :] = low


def tile_kernel(part_count, pair, length_ref, points_ref, *refs):
    parts = refs[:part_count]
    tiles_ref, message_ref, first_ref = refs[part_count:]
    feats, own = points_ref.shape
    cols = first_ref.shape[0]
    scale = length_ref[0]
    per_dist = 5.0 / (scale * scale)
    slope = 1.0 / (3.0 * scale)
    own_points = points_ref[...].astype(F32).T
    own_squares = jnp.sum(own_points * own_points, axis=1, keepdims=True) * per_dist
    own_squares = jnp.broadcast_to(own_squares, (own, own))
    own_points = own_points.astype(BF16)

    total = jnp.zeros((cols, 2 * own), F32)
    base = 0
    for part in parts:
        steps = part.shape[0] // pair

        def one_pair(step, carried, part=part, base=base):
            vectors = []
            for side in range(pair):
                block = step * pair + side
                points = part[block, 0:feats, :]
                wide = points.astype(F32)
                squares = jnp.sum(wide * wide, axis=0, keepdims=True) * per_dist
                inner = jnp.dot(own_points, points, preferred_element_type=F32)
                reduced = jnp.maximum((own_squares + squares) - inner * (2.0 * per_dist), TINY)
                radius = reduced * lax.rsqrt(reduced)
                damping = jnp.exp2(radius * (-LOG2E))
                linear = 1.0 + radius
                kern = (linear + reduced * (1.0 / 3.0)) * damping
                dkern = (reduced * slope) * (linear * damping)
                lanes = pl.ds(side * own, own)
                tiles_ref[base + step, 0:own, lanes] = kern.astype(BF16)
                tiles_ref[base + step, own : 2 * own, lanes] = dkern.astype(BF16)
                vectors.append(part[block, feats : feats + cols, :])
            vectors = jnp.concatenate(vectors, axis=1) if pair > 1 else vectors[0]
            return carried + lax.dot_general(
                vectors, tiles_ref[base + step], NT, preferred_element_type=F32
            )

        total = lax.fori_loop(0, steps, one_pair, total, unroll=math.gcd(steps, 4))
        base += steps
    first_ref[...] = total
    product = total[:, 0:own]
    for peer in range(message_ref.shape[0]):
        message_ref[peer] = product


def to_lanes(column, slot):
    cols = column.shape[0]
    lanes = lax.broadcasted_iota(jnp.int32, (cols, 128), 1)
    rows = lax.broadcasted_iota(jnp.int32, (cols, 128), 0)
    return jnp.where(lanes == rows + slot * cols, jnp.broadcast_to(column, (cols, 128)), 0.0)


def from_lanes(row, slot, cols):
    lanes = lax.broadcasted_iota(jnp.int32, (cols, 128), 1)
    rows = lax.broadcasted_iota(jnp.int32, (cols, 128), 0)
    picked = jnp.where(lanes == rows + slot * cols, jnp.broadcast_to(row, (cols, 128)), 0.0)
    return jnp.sum(picked, axis=1, keepdims=True)


def lane_sum(values):
    return jnp.sum(values, axis=1, keepdims=True)


def second_kernel(part_count, pair, feats, scalars_ref, right_ref, first_ref, tiles_ref, *refs):
    vectors = refs[:part_count]
    products = refs[part_count : 2 * part_count]
    message_ref, direction_ref, residual_ref, applied_ref, columns_ref, wide_ref = refs[2 * part_count :]
    cols, own = right_ref.shape
    amplitude = scalars_ref[1]
    jitter = scalars_ref[2]
    zero = jnp.zeros((cols, own), F32)

    def right_block(part, block):
        high = vectors[part][block, feats : feats + cols, :].astype(F32)
        low = vectors[part][block, feats + cols : feats + 2 * cols, :].astype(F32)
        return high, low

    def added(sums):
        total = sums[0]
        for other in sums[1:]:
            total = [one + two for one, two in zip(total, other)]
        return [lane_sum(one) for one in total]

    sums = []
    for part in range(part_count):
        def first_pass(block, carried, part=part):
            high, low = right_block(part, block)
            right = high + low
            product = products[part][block]
            return [
                carried[0] + right * right,
                carried[1] + right * (amplitude * product + jitter * right),
                carried[2] + low * product,
            ]

        count = vectors[part].shape[0]
        sums.append(lax.fori_loop(0, count, first_pass, [zero] * 3, unroll=math.gcd(count, 4)))
    norm, curvature, low_first = added(sums)
    step = norm / curvature

    sums = []
    for part in range(part_count):
        def second_pass(block, carried, part=part):
            high, low = right_block(part, block)
            right = high + low
            product = products[part][block]
            residual = right - step * (amplitude * product + jitter * right)
            return [carried[0] + residual * residual]

        count = vectors[part].shape[0]
        sums.append(lax.fori_loop(0, count, second_pass, [zero], unroll=math.gcd(count, 4)))
    (norm_next,) = added(sums)
    turn = norm_next / norm

    sums = []
    total = jnp.zeros((cols, 2 * own), F32)
    base = 0
    for part in range(part_count):
        steps = vectors[part].shape[0] // pair

        def third_pass(index, carried, part=part, base=base):
            total, low_second, dots, squares = carried
            rounded = []
            for side in range(pair):
                block = index * pair + side
                high, low = right_block(part, block)
                right = high + low
                product = products[part][block]
                residual = right - step * (amplitude * product + jitter * right)
                direction = residual + turn * right
                narrow = direction.astype(BF16)
                rounded.append(narrow)
                wide_ref[base * pair + block] = direction
                low_second = low_second + (direction - narrow.astype(F32)) * product
                dots = dots + right * direction
                squares = squares + direction * direction
            rounded = jnp.concatenate(rounded, axis=1) if pair > 1 else rounded[0]
            total = total + lax.dot_general(
                rounded, tiles_ref[base + index], NT, preferred_element_type=F32
            )
            return total, low_second, dots, squares

        total, *rest = lax.fori_loop(
            0, steps, third_pass, (total, zero, zero, zero), unroll=math.gcd(steps, 4)
        )
        sums.append(rest)
        base += steps
    low_second, dots, squares = added(sums)

    right = right_ref[...]
    product = first_ref[:, 0:own]
    slope = first_ref[:, own : 2 * own]
    residual = right - step * (amplitude * product + jitter * right)
    direction = residual + turn * right
    product_next = total[:, 0:own]
    slope_next = total[:, own : 2 * own]
    applied = amplitude * product_next + jitter * direction
    direction_ref[...] = direction
    residual_ref[...] = residual
    applied_ref[...] = applied
    lanes = lax.broadcasted_iota(jnp.int32, (cols, 128), 1)
    kept = jnp.zeros((cols, 128), F32)
    for slot, column in enumerate([step, norm_next, norm, low_first, low_second, dots, squares]):
        kept = jnp.where(lanes == slot, jnp.broadcast_to(column, (cols, 128)), kept)
    columns_ref[...] = kept

    low = right - right.astype(BF16).astype(F32)
    low_direction = direction - direction.astype(BF16).astype(F32)
    partial = [
        direction * applied,
        low * product_next,
        right * slope,
        right * slope_next,
        direction * slope,
        direction * slope_next,
        low_direction * product_next,
    ]
    packed = jnp.zeros((cols, 128), F32)
    for slot, values in enumerate(partial):
        packed = packed + to_lanes(lane_sum(values), slot)
    packed = jnp.sum(packed, axis=0, keepdims=True)
    for peer in range(message_ref.shape[0]):
        message_ref[peer, 0:1, :] = packed
        message_ref[peer, 1:2, :] = product_next[0:1, :]


def last_kernel(
    part_count, feats, points_total, scalars_ref, place_ref, right_ref, direction_ref, residual_ref,
    applied_ref, columns_ref, wide_ref, received_ref, *refs
):
    vectors = refs[:part_count]
    products = refs[part_count : 2 * part_count]
    solution_ref, final_ref, gradient_ref = refs[2 * part_count :]
    cols, own = right_ref.shape
    amplitude = scalars_ref[1]
    device_count = received_ref.shape[0]

    def gather_sums(device, carried):
        return carried + received_ref[device, 0:1, :]

    sums = lax.fori_loop(
        0, device_count, gather_sums, jnp.zeros((1, 128), F32), unroll=math.gcd(device_count, 8)
    )
    curvature, low_next, right_slope, right_slope_next, slope_cross, slope_square, low_square = [
        from_lanes(sums, slot, cols) for slot in range(7)
    ]
    step, norm_next, norm, low_first, low_second, dots, squares = [
        columns_ref[:, slot : slot + 1] for slot in range(7)
    ]
    step_next = norm_next / curvature

    solution_ref[...] = step * right_ref[...] + step_next * direction_ref[...]
    final_ref[...] = residual_ref[...] - step_next * applied_ref[...]

    zero = jnp.zeros((cols, own), F32)
    row_zero = jnp.zeros((1, own), F32)
    sums = []
    base = 0
    for part in range(part_count):
        count = vectors[part].shape[0]

        def one_block(block, carried, part=part, base=base):
            whole, first_row = carried
            right = (
                vectors[part][block, feats : feats + cols, :].astype(F32)
                + vectors[part][block, feats + cols : feats + 2 * cols, :].astype(F32)
            )
            rounded = (step * right + step_next * wide_ref[base + block]).astype(BF16).astype(F32)
            source = block * part_count + (place_ref[0] + part) % part_count
            return (
                whole + products[part][block] * rounded,
                first_row + received_ref[source, 1:2, :] * rounded[0:1, :],
            )

        sums.append(lax.fori_loop(0, count, one_block, (zero, row_zero), unroll=math.gcd(count, 4)))
        base += count
    whole, first_row = sums[0]
    for other in sums[1:]:
        whole = whole + other[0]
        first_row = first_row + other[1]
    right_kernel = lane_sum(whole) + step * low_first + step_next * low_next
    direction_kernel = lane_sum(first_row) + (step * low_second + step_next * low_square)[0:1, :]
    right_slope_u = step * right_slope + step_next * right_slope_next
    direction_slope_u = step * slope_cross + step_next * slope_square
    right_u = step * norm + step_next * dots
    direction_u = step * dots + step_next * squares
    is_first = lax.broadcasted_iota(jnp.int32, (cols, 1), 0) == 0
    direction_kernel = jnp.broadcast_to(direction_kernel, (cols, 1))
    weight = jnp.where(is_first, 1.0, -1.0 / (cols - 1))
    forms = []
    for right_form, direction_form in (
        (amplitude * right_slope_u, amplitude * direction_slope_u),
        (right_kernel, direction_kernel),
        (right_u, direction_u),
    ):
        form = jnp.where(is_first, step * right_form + step_next * direction_form, right_form)
        forms.append(jnp.sum(weight * form, axis=0, keepdims=True) * (0.5 / points_total))
    lanes = lax.broadcasted_iota(jnp.int32, (1, 128), 1)
    gradient = jnp.zeros((1, 128), F32)
    for slot, form in enumerate(forms):
        gradient = jnp.where(lanes == slot, jnp.broadcast_to(form, (1, 128)), gradient)
    gradient_ref[...] = gradient


def spread(message, axes, mesh_shape):
    blocks = mesh_shape["blk"]
    pair = mesh_shape["grp"]
    if pair == 2:
        mine = lax.all_to_all(message, "blk", 0, 0, tiled=True)
        return [mine, lax.ppermute(mine, "grp", [(0, 1), (1, 0)])]
    return [lax.all_to_all(message, axes, 0, 0, tiled=True)]


def local(mesh_shape, points, right_side, lengthscale, outputscale, noise_level):
    axes = ("blk", "grp")
    feats, own = points.shape
    cols = right_side.shape[0]
    devices = mesh_shape["blk"] * mesh_shape["grp"]
    by_pairs = mesh_shape["grp"] == 2
    peers = mesh_shape["blk"] if by_pairs else devices
    part_count = 2 if by_pairs else 1
    pair = 2 if peers % 2 == 0 else 1
    scalars = jnp.concatenate([lengthscale, outputscale, noise_level])
    shape = jax.ShapeDtypeStruct

    message = pl.pallas_call(
        pack_kernel,
        out_shape=shape((peers, feats + 2 * cols, own), BF16),
        in_specs=_vmem(2),
        out_specs=_vmem(1)[0],
        name="pack",
    )(points, right_side)
    vectors = spread(message, axes, mesh_shape)

    tiles, message, first = pl.pallas_call(
        functools.partial(tile_kernel, part_count, pair),
        out_shape=(
            shape((devices // pair, 2 * own, pair * own), BF16),
            shape((peers, cols, own), F32),
            shape((cols, 2 * own), F32),
        ),
        in_specs=[_smem()] + _vmem(1 + part_count),
        out_specs=tuple(_vmem(3)),
        name="tiles",
    )(scalars, points, *vectors)
    products = spread(message, axes, mesh_shape)

    message, direction, residual, applied, columns, wide = pl.pallas_call(
        functools.partial(second_kernel, part_count, pair, feats),
        out_shape=(
            shape((devices, 2, own), F32),
            shape((cols, own), F32),
            shape((cols, own), F32),
            shape((cols, own), F32),
            shape((cols, 128), F32),
            shape((devices, cols, own), F32),
        ),
        in_specs=[_smem()] + _vmem(3 + 2 * part_count),
        out_specs=tuple(_vmem(6)),
        name="second",
    )(scalars, right_side, first, tiles, *vectors, *products)
    received = lax.all_to_all(message, axes, 0, 0, tiled=True)

    place = lax.axis_index("grp").astype(jnp.int32)[None]
    solution, final, gradient = pl.pallas_call(
        functools.partial(last_kernel, part_count, feats, float(own * devices)),
        out_shape=(
            shape((cols, own), F32),
            shape((cols, own), F32),
            shape((1, 128), F32),
        ),
        in_specs=[_smem(), _smem()] + _vmem(7 + 2 * part_count),
        out_specs=tuple(_vmem(3)),
        name="last",
    )(scalars, place, right_side, direction, residual, applied, columns, wide, received, *vectors, *products)
    return solution, final, gradient[0, 0:3]


def solution(mesh):
    whole = P(None, ("blk", "grp"))
    return jax.shard_map(
        functools.partial(local, dict(mesh.shape)),
        mesh=mesh,
        in_specs=(whole, whole, P(), P(), P()),
        out_specs=(whole, whole, P()),
        check_vma=False,
    )
```

```python
import functools
import math

import jax
import jax.numpy as jnp
from jax import lax
from jax.experimental import pallas as pl
from jax.experimental.pallas import tpu as pltpu
from jax.sharding import PartitionSpec as P

F32 = jnp.float32
BF16 = jnp.bfloat16
LOG2E = math.log2(math.e)
TINY = 1e-36
NT = (((1,), (1,)), ((), ()))


def _vmem(count):
    return [pl.BlockSpec(memory_space=pltpu.VMEM) for _ in range(count)]


def _smem():
    return pl.BlockSpec(memory_space=pltpu.SMEM)


def pack_kernel(points_ref, right_ref, out_ref):
    feats = points_ref.shape[0]
    cols = right_ref.shape[0]
    right = right_ref[...]
    high = right.astype(BF16)
    low = (right - high.astype(F32)).astype(BF16)
    points = points_ref[...]
    for peer in range(out_ref.shape[0]):
        out_ref[peer, 0:feats, :] = points
        out_ref[peer, feats : feats + cols, :] = high
        out_ref[peer, feats + cols : feats + 2 * cols, :] = low


def tile_kernel(part_count, pair, with_message, length_ref, points_ref, *refs):
    parts = refs[:part_count]
    tiles_ref, *outs = refs[part_count:]
    feats, own = points_ref.shape
    first_ref = outs[-1]
    cols = first_ref.shape[0]
    scale = length_ref[0]
    per_dist = 5.0 / (scale * scale)
    slope = 1.0 / (3.0 * scale)
    own_points = points_ref[...].astype(F32).T
    own_squares = jnp.sum(own_points * own_points, axis=1, keepdims=True) * per_dist
    own_squares = jnp.broadcast_to(own_squares, (own, own))
    own_points = own_points.astype(BF16)

    total = jnp.zeros((cols, own), F32)
    base = 0
    for part in parts:
        steps = part.shape[0] // pair

        def one_pair(step, carried, part=part, base=base):
            vectors = []
            for side in range(pair):
                block = step * pair + side
                points = part[block, 0:feats, :]
                wide = points.astype(F32)
                squares = jnp.sum(wide * wide, axis=0, keepdims=True) * per_dist
                inner = jnp.dot(own_points, points, preferred_element_type=F32)
                reduced = jnp.maximum((own_squares + squares) - inner * (2.0 * per_dist), TINY)
                radius = reduced * lax.rsqrt(reduced)
                damping = jnp.exp2(radius * (-LOG2E))
                linear = 1.0 + radius
                if with_message:
                    tile = (linear + reduced * (1.0 / 3.0)) * damping
                else:
                    tile = (reduced * slope) * (linear * damping)
                tiles_ref[base + step, :, pl.ds(side * own, own)] = tile.astype(BF16)
                vectors.append(part[block, feats : feats + cols, :])
            vectors = jnp.concatenate(vectors, axis=1) if pair > 1 else vectors[0]
            return carried + lax.dot_general(
                vectors, tiles_ref[base + step], NT, preferred_element_type=F32
            )

        total = lax.fori_loop(0, steps, one_pair, total, unroll=math.gcd(steps, 4))
        base += steps
    first_ref[...] = total
    if with_message:
        for peer in range(outs[0].shape[0]):
            outs[0][peer] = total


def to_lanes(column, slot):
    cols = column.shape[0]
    lanes = lax.broadcasted_iota(jnp.int32, (cols, 128), 1)
    rows = lax.broadcasted_iota(jnp.int32, (cols, 128), 0)
    return jnp.where(lanes == rows + slot * cols, jnp.broadcast_to(column, (cols, 128)), 0.0)


def from_lanes(row, slot, cols):
    lanes = lax.broadcasted_iota(jnp.int32, (cols, 128), 1)
    rows = lax.broadcasted_iota(jnp.int32, (cols, 128), 0)
    picked = jnp.where(lanes == rows + slot * cols, jnp.broadcast_to(row, (cols, 128)), 0.0)
    return jnp.sum(picked, axis=1, keepdims=True)


def lane_sum(values):
    return jnp.sum(values, axis=1, keepdims=True)


def second_kernel(
    part_count, pair, feats, amplitude_ref, jitter_ref, place_ref, right_ref, kernel_ref, slope_ref,
    kern_ref, dkern_ref, products_ref, *refs
):
    vectors = refs[:part_count]
    message_ref, direction_ref, residual_ref, applied_ref, columns_ref, wide_ref = refs[part_count:]
    cols, own = right_ref.shape
    amplitude = amplitude_ref[0]
    jitter = jitter_ref[0]
    place = place_ref[0]
    zero = jnp.zeros((cols, own), F32)

    def right_block(part, block):
        high = vectors[part][block, feats : feats + cols, :].astype(F32)
        low = vectors[part][block, feats + cols : feats + 2 * cols, :].astype(F32)
        return high, low

    def added(sums):
        total = sums[0]
        for other in sums[1:]:
            total = [one + two for one, two in zip(total, other)]
        return [lane_sum(one) for one in total]

    sums = []
    for part in range(part_count):
        def first_pass(block, carried, part=part):
            high, low = right_block(part, block)
            right = high + low
            product = products_ref[block * part_count + (place + part) % part_count]
            return [
                carried[0] + right * right,
                carried[1] + right * (amplitude * product + jitter * right),
                carried[2] + low * product,
            ]

        count = vectors[part].shape[0]
        sums.append(lax.fori_loop(0, count, first_pass, [zero] * 3, unroll=math.gcd(count, 4)))
    norm, curvature, low_first = added(sums)
    step = norm / curvature

    sums = []
    for part in range(part_count):
        def second_pass(block, carried, part=part):
            high, low = right_block(part, block)
            right = high + low
            product = products_ref[block * part_count + (place + part) % part_count]
            residual = right - step * (amplitude * product + jitter * right)
            return [carried[0] + residual * residual]

        count = vectors[part].shape[0]
        sums.append(lax.fori_loop(0, count, second_pass, [zero], unroll=math.gcd(count, 4)))
    (norm_next,) = added(sums)
    turn = norm_next / norm

    sums = []
    base = 0
    total = zero
    slopes = zero
    for part in range(part_count):
        steps = vectors[part].shape[0] // pair

        def third_pass(index, carried, part=part, base=base):
            total, slopes, low_second, dots, squares = carried
            rounded = []
            for side in range(pair):
                block = index * pair + side
                high, low = right_block(part, block)
                right = high + low
                product = products_ref[block * part_count + (place + part) % part_count]
                residual = right - step * (amplitude * product + jitter * right)
                direction = residual + turn * right
                narrow = direction.astype(BF16)
                rounded.append(narrow)
                wide_ref[base * pair + block] = direction
                low_second = low_second + (direction - narrow.astype(F32)) * product
                dots = dots + right * direction
                squares = squares + direction * direction
            rounded = jnp.concatenate(rounded, axis=1) if pair > 1 else rounded[0]
            total = total + lax.dot_general(
                rounded, kern_ref[base + index], NT, preferred_element_type=F32
            )
            slopes = slopes + lax.dot_general(
                rounded, dkern_ref[base + index], NT, preferred_element_type=F32
            )
            return total, slopes, low_second, dots, squares

        total, slopes, *rest = lax.fori_loop(
            0, steps, third_pass, (total, slopes, zero, zero, zero), unroll=math.gcd(steps, 4)
        )
        sums.append(rest)
        base += steps
    low_second, dots, squares = added(sums)

    right = right_ref[...]
    product = kernel_ref[...]
    slope = slope_ref[...]
    residual = right - step * (amplitude * product + jitter * right)
    direction = residual + turn * right
    product_next = total
    slope_next = slopes
    applied = amplitude * product_next + jitter * direction
    direction_ref[...] = direction
    residual_ref[...] = residual
    applied_ref[...] = applied
    lanes = lax.broadcasted_iota(jnp.int32, (cols, 128), 1)
    kept = jnp.zeros((cols, 128), F32)
    for slot, column in enumerate([step, norm_next, norm, low_first, low_second, dots, squares]):
        kept = jnp.where(lanes == slot, jnp.broadcast_to(column, (cols, 128)), kept)
    columns_ref[...] = kept

    low = right - right.astype(BF16).astype(F32)
    low_direction = direction - direction.astype(BF16).astype(F32)
    partial = [
        direction * applied,
        low * product_next,
        right * slope,
        right * slope_next,
        direction * slope,
        direction * slope_next,
        low_direction * product_next,
    ]
    packed = jnp.zeros((cols, 128), F32)
    for slot, values in enumerate(partial):
        packed = packed + to_lanes(lane_sum(values), slot)
    packed = jnp.sum(packed, axis=0, keepdims=True)
    for peer in range(message_ref.shape[0]):
        message_ref[peer, 0:1, :] = packed
        message_ref[peer, 1:2, :] = product_next[0:1, :]


def last_kernel(
    part_count, feats, points_total, amplitude_ref, place_ref, right_ref, direction_ref, residual_ref,
    applied_ref, columns_ref, wide_ref, received_ref, products_ref, *refs
):
    vectors = refs[:part_count]
    solution_ref, final_ref, gradient_ref = refs[part_count:]
    cols, own = right_ref.shape
    amplitude = amplitude_ref[0]
    device_count = received_ref.shape[0]

    def gather_sums(device, carried):
        return carried + received_ref[device, 0:1, :]

    sums = lax.fori_loop(
        0, device_count, gather_sums, jnp.zeros((1, 128), F32), unroll=math.gcd(device_count, 8)
    )
    curvature, low_next, right_slope, right_slope_next, slope_cross, slope_square, low_square = [
        from_lanes(sums, slot, cols) for slot in range(7)
    ]
    step, norm_next, norm, low_first, low_second, dots, squares = [
        columns_ref[:, slot : slot + 1] for slot in range(7)
    ]
    step_next = norm_next / curvature

    solution_ref[...] = step * right_ref[...] + step_next * direction_ref[...]
    final_ref[...] = residual_ref[...] - step_next * applied_ref[...]

    zero = jnp.zeros((cols, own), F32)
    row_zero = jnp.zeros((1, own), F32)
    sums = []
    base = 0
    for part in range(part_count):
        count = vectors[part].shape[0]

        def one_block(block, carried, part=part, base=base):
            whole, first_row = carried
            right = (
                vectors[part][block, feats : feats + cols, :].astype(F32)
                + vectors[part][block, feats + cols : feats + 2 * cols, :].astype(F32)
            )
            rounded = (step * right + step_next * wide_ref[base + block]).astype(BF16).astype(F32)
            source = block * part_count + (place_ref[0] + part) % part_count
            return (
                whole + products_ref[source] * rounded,
                first_row + received_ref[source, 1:2, :] * rounded[0:1, :],
            )

        sums.append(lax.fori_loop(0, count, one_block, (zero, row_zero), unroll=math.gcd(count, 4)))
        base += count
    whole, first_row = sums[0]
    for other in sums[1:]:
        whole = whole + other[0]
        first_row = first_row + other[1]
    right_kernel = lane_sum(whole) + step * low_first + step_next * low_next
    direction_kernel = lane_sum(first_row) + (step * low_second + step_next * low_square)[0:1, :]
    right_slope_u = step * right_slope + step_next * right_slope_next
    direction_slope_u = step * slope_cross + step_next * slope_square
    right_u = step * norm + step_next * dots
    direction_u = step * dots + step_next * squares
    is_first = lax.broadcasted_iota(jnp.int32, (cols, 1), 0) == 0
    direction_kernel = jnp.broadcast_to(direction_kernel, (cols, 1))
    weight = jnp.where(is_first, 1.0, -1.0 / (cols - 1))
    for slot, (right_form, direction_form) in enumerate((
        (amplitude * right_slope_u, amplitude * direction_slope_u),
        (right_kernel, direction_kernel),
        (right_u, direction_u),
    )):
        form = jnp.where(is_first, step * right_form + step_next * direction_form, right_form)
        gradient_ref[slot] = jnp.sum(weight * form) * (0.5 / points_total)


def spread(message, axes, mesh_shape):
    blocks = mesh_shape["blk"]
    pair = mesh_shape["grp"]
    if pair == 2:
        mine = lax.all_to_all(message, "blk", 0, 0, tiled=True)
        return [mine, lax.ppermute(mine, "grp", [(0, 1), (1, 0)])]
    return [lax.all_to_all(message, axes, 0, 0, tiled=True)]


def local(mesh_shape, points, right_side, lengthscale, outputscale, noise_level):
    axes = ("blk", "grp")
    feats, own = points.shape
    cols = right_side.shape[0]
    devices = mesh_shape["blk"] * mesh_shape["grp"]
    by_pairs = mesh_shape["grp"] == 2
    peers = mesh_shape["blk"] if by_pairs else devices
    part_count = 2 if by_pairs else 1
    pair = 2 if peers % 2 == 0 else 1
    params = pltpu.CompilerParams(vmem_limit_bytes=(4 << 20) + devices * (40 << 10))
    shape = pltpu.VMEM
    result = jax.ShapeDtypeStruct

    def near(*arrays):
        return [pltpu.with_memory_space_constraint(array, pltpu.VMEM) for array in arrays]

    message = pl.pallas_call(
        pack_kernel,
        out_shape=shape((peers, feats + 2 * cols, own), BF16),
        in_specs=_vmem(2),
        out_specs=_vmem(1)[0],
        name="pack",
        compiler_params=params,
    )(points, right_side)
    vectors = spread(message, axes, mesh_shape)

    tile_shape = shape((devices // pair, own, pair * own), BF16)
    kern, message, kernel_first = pl.pallas_call(
        functools.partial(tile_kernel, part_count, pair, True),
        out_shape=(tile_shape, shape((devices, cols, own), F32), shape((cols, own), F32)),
        in_specs=[_smem()] + _vmem(1 + part_count),
        out_specs=tuple(_vmem(3)),
        name="kern",
        compiler_params=params,
    )(lengthscale, points, *near(*vectors))
    products = lax.all_to_all(message, axes, 0, 0, tiled=True)
    dkern, slope_first = pl.pallas_call(
        functools.partial(tile_kernel, part_count, pair, False),
        out_shape=(tile_shape, shape((cols, own), F32)),
        in_specs=[_smem()] + _vmem(1 + part_count),
        out_specs=tuple(_vmem(2)),
        name="dkern",
        compiler_params=params,
    )(lengthscale, points, *near(*vectors))

    place = lax.axis_index("grp").astype(jnp.int32)[None]
    message, direction, residual, applied, columns, wide = pl.pallas_call(
        functools.partial(second_kernel, part_count, pair, feats),
        out_shape=(
            shape((devices, 2, own), F32),
            shape((cols, own), F32),
            shape((cols, own), F32),
            shape((cols, own), F32),
            shape((cols, 128), F32),
            shape((devices, cols, own), F32),
        ),
        in_specs=[_smem()] * 3 + _vmem(6 + part_count),
        out_specs=tuple(_vmem(6)),
        name="second",
        compiler_params=params,
    )(
        outputscale, noise_level, place, right_side,
        *near(kernel_first, slope_first, kern, dkern, products, *vectors),
    )
    received = lax.all_to_all(message, axes, 0, 0, tiled=True)

    solution, final, gradient = pl.pallas_call(
        functools.partial(last_kernel, part_count, feats, float(own * devices)),
        out_shape=(
            result((cols, own), F32),
            result((cols, own), F32),
            result((3,), F32),
        ),
        in_specs=[_smem(), _smem()] + _vmem(8 + part_count),
        out_specs=tuple(_vmem(2) + [_smem()]),
        name="last",
        compiler_params=params,
    )(
        outputscale, place, right_side,
        *near(direction, residual, applied, columns, wide, received, products, *vectors),
    )
    return solution, final, gradient


def solution(mesh):
    whole = P(None, ("blk", "grp"))
    return jax.shard_map(
        functools.partial(local, dict(mesh.shape)),
        mesh=mesh,
        in_specs=(whole, whole, P(), P(), P()),
        out_specs=(whole, whole, P()),
        check_vma=False,
    )
```

```python
import functools
import math

import jax
import jax.numpy as jnp
from jax import lax
from jax.experimental import pallas as pl
from jax.experimental.pallas import tpu as pltpu
from jax.sharding import PartitionSpec as P

F32 = jnp.float32
BF16 = jnp.bfloat16
LOG2E = math.log2(math.e)
TINY = 1e-36
NT = (((1,), (1,)), ((), ()))


def _vmem(count):
    return [pl.BlockSpec(memory_space=pltpu.VMEM) for _ in range(count)]


def _smem():
    return pl.BlockSpec(memory_space=pltpu.SMEM)


def _hbm(count):
    return [pl.BlockSpec(memory_space=pltpu.HBM) for _ in range(count)]


def lane_sum(values):
    return jnp.sum(values, axis=1, keepdims=True)


def unrolled(count, most):
    return max(divisor for divisor in range(1, most + 1) if count % divisor == 0)


def pack_kernel(points_hbm, right_hbm, out_ref, points_ref, right_ref, sems):
    feats = points_ref.shape[0]
    cols = right_ref.shape[0]
    copies = [
        pltpu.make_async_copy(right_hbm, right_ref, sems.at[0]),
        pltpu.make_async_copy(points_hbm, points_ref, sems.at[1]),
    ]
    for copy in copies:
        copy.start()
    copies[0].wait()
    right = right_ref[...]
    high = right.astype(BF16)
    low = (right - high.astype(F32)).astype(BF16)
    for peer in range(out_ref.shape[0]):
        out_ref[peer, feats : feats + cols, :] = high
        out_ref[peer, feats + cols : feats + 2 * cols, :] = low
    copies[1].wait()
    points = points_ref[...]
    for peer in range(out_ref.shape[0]):
        out_ref[peer, 0:feats, :] = points


class Distances:
    def __init__(self, length_ref, points_ref):
        scale = length_ref[0]
        self.scale = scale
        self.factor = (5.0 * LOG2E * LOG2E) / (scale * scale)
        own = points_ref.shape[1]
        points = points_ref[...].astype(F32).T
        squares = jnp.sum(points * points, axis=1, keepdims=True) * self.factor
        self.squares = jnp.broadcast_to(squares, (own, own))
        self.points = (-2.0 * points).astype(BF16)

    def __call__(self, points):
        wide = points.astype(F32)
        squares = jnp.sum(wide * wide, axis=0, keepdims=True) * self.factor
        inner = jnp.dot(self.points, points, preferred_element_type=F32)
        reduced = jnp.maximum((self.squares + squares) + inner * self.factor, TINY)
        return reduced, reduced * lax.rsqrt(reduced)


def kern_tile(reduced, root):
    shifted = root + 1.5 * LOG2E
    return (shifted * shifted + 0.75 * LOG2E * LOG2E) * jnp.exp2(-math.log2(3.0 * LOG2E * LOG2E) - root)


def kern_kernel(pair, has_before, length_ref, points_ref, part_ref, *refs):
    before = refs[0][...] if has_before else None
    tiles_ref, *outs = refs[1 if has_before else 0 :]
    feats, own = points_ref.shape
    total_ref = outs[0]
    cols = total_ref.shape[0]
    distances = Distances(length_ref, points_ref)
    steps = part_ref.shape[0] // pair
    total = before if has_before else jnp.zeros((cols, own), F32)

    def one_pair(step, total):
        vectors = []
        for side in range(pair):
            block = step * pair + side
            tile = kern_tile(*distances(part_ref[block, 0:feats, :]))
            tiles_ref[step, :, pl.ds(side * own, own)] = tile.astype(BF16)
            vectors.append(part_ref[block, feats : feats + cols, :])
        vectors = jnp.concatenate(vectors, axis=1) if pair > 1 else vectors[0]
        return total + lax.dot_general(vectors, tiles_ref[step], NT, preferred_element_type=F32)

    total = lax.fori_loop(0, steps, one_pair, total, unroll=unrolled(steps, 8))
    total_ref[...] = total
    if len(outs) > 1:
        message_ref = outs[1]
        rows = message_ref.shape[1]
        for peer in range(message_ref.shape[0]):
            first = (peer * rows) % cols
            message_ref[peer] = total[first : first + rows]


def dkern_kernel(
    part_count, pair, length_ref, amplitude_ref, jitter_ref, points_ref, *refs
):
    parts = refs[:part_count]
    tiles_ref, total_ref, wide_ref, norm_ref, scalars_ref = refs[part_count:]
    for slot, scalar in enumerate((amplitude_ref, jitter_ref)):
        scalars_ref[slot : slot + 1, :] = jnp.full((1, 128), scalar[0], F32)
    feats, own = points_ref.shape
    cols = total_ref.shape[0]
    distances = Distances(length_ref, points_ref)
    slope = 1.0 / (3.0 * LOG2E * LOG2E * LOG2E * distances.scale)
    total = jnp.zeros((cols, own), F32)
    norms = []
    base = 0
    for part in parts:
        steps = part.shape[0] // pair

        def one_pair(step, carried, part=part, base=base):
            total, norm = carried
            vectors = []
            for side in range(pair):
                block = step * pair + side
                reduced, root = distances(part[block, 0:feats, :])
                tile = (reduced * slope) * ((root + LOG2E) * jnp.exp2(-root))
                tiles_ref[base + step, :, pl.ds(side * own, own)] = tile.astype(BF16)
                high = part[block, feats : feats + cols, :]
                right = high.astype(F32) + part[block, feats + cols : feats + 2 * cols, :].astype(F32)
                wide_ref[base * pair + block] = right
                norm = norm + right * right
                vectors.append(high)
            vectors = jnp.concatenate(vectors, axis=1) if pair > 1 else vectors[0]
            total = total + lax.dot_general(
                vectors, tiles_ref[base + step], NT, preferred_element_type=F32
            )
            return total, norm

        total, norm = lax.fori_loop(
            0, steps, one_pair, (total, jnp.zeros((cols, own), F32)), unroll=unrolled(steps, 4)
        )
        norms.append(norm)
        base += steps
    total_ref[...] = total
    norm_ref[...] = jnp.broadcast_to(lane_sum(functools.reduce(jnp.add, norms)), norm_ref.shape)


def to_lanes(column, slot):
    cols = column.shape[0]
    lanes = lax.broadcasted_iota(jnp.int32, (cols, 128), 1)
    rows = lax.broadcasted_iota(jnp.int32, (cols, 128), 0)
    return jnp.where(lanes == rows + slot * cols, jnp.broadcast_to(column, (cols, 128)), 0.0)


def from_lanes(row, slot, cols):
    lanes = lax.broadcasted_iota(jnp.int32, (cols, 128), 1)
    rows = lax.broadcasted_iota(jnp.int32, (cols, 128), 0)
    picked = jnp.where(lanes == rows + slot * cols, jnp.broadcast_to(row, (cols, 128)), 0.0)
    return lane_sum(picked)


def into_columns(columns, cols):
    lanes = lax.broadcasted_iota(jnp.int32, (cols, 128), 1)
    kept = jnp.zeros((cols, 128), F32)
    for slot, column in enumerate(columns):
        kept = jnp.where(lanes == slot, jnp.broadcast_to(column, (cols, 128)), kept)
    return kept


def second_kernel(
    part_count, pair, halves, place_ref, scalars_ref, right_ref, kernel_ref, slope_ref,
    dkern_ref, wide_ref, norm_ref, *refs
):
    kerns = refs[:part_count]
    received = refs[part_count : part_count + halves]
    (
        message_ref, direction_ref, residual_ref, applied_ref, columns_ref, products_ref, turned_ref,
    ) = refs[part_count + halves :]
    cols, own = right_ref.shape
    amplitude = scalars_ref[0:1, :]
    jitter = scalars_ref[1:2, :]
    place = place_ref[0]
    zero = jnp.zeros((cols, own), F32)
    norm = norm_ref[:, 0:1]
    count = kerns[0].shape[0] * pair

    sums = []
    for part in range(part_count):
        def first_pass(block, carried, part=part):
            source = block * part_count + (place + part) % part_count
            if halves == 2:
                mine = received[0][source]
                other = received[1][source]
                product = jnp.concatenate(
                    [jnp.where(place == 0, mine, other), jnp.where(place == 0, other, mine)], axis=0
                )
            else:
                product = received[0][source]
            products_ref[part * count + block] = product
            right = wide_ref[part * count + block]
            applied = amplitude * product + jitter * right
            return carried[0] + right * applied, carried[1] + applied * applied

        sums.append(lax.fori_loop(0, count, first_pass, (zero, zero), unroll=unrolled(count, 8)))
    curvature, length = [lane_sum(functools.reduce(jnp.add, parts)) for parts in zip(*sums)]
    step = norm / curvature
    turn = (step * step * length - norm) / norm

    sums = []
    total = zero
    slopes = zero
    for part in range(part_count):
        base = part * (count // pair)

        def second_pass(index, carried, part=part, base=base):
            total, slopes, norms = carried
            rounded = []
            for side in range(pair):
                block = part * count + index * pair + side
                right = wide_ref[block]
                residual = right - step * (amplitude * products_ref[block] + jitter * right)
                direction = residual + turn * right
                turned_ref[block] = direction
                norms = norms + residual * residual
                rounded.append(direction)
            rounded = jnp.concatenate(rounded, axis=1) if pair > 1 else rounded[0]
            rounded = rounded.astype(BF16)
            total = total + lax.dot_general(
                rounded, kerns[part][index], NT, preferred_element_type=F32
            )
            slopes = slopes + lax.dot_general(
                rounded, dkern_ref[base + index], NT, preferred_element_type=F32
            )
            return total, slopes, norms

        total, slopes, norms = lax.fori_loop(
            0, count // pair, second_pass, (total, slopes, zero), unroll=unrolled(count // pair, 8)
        )
        sums.append(norms)
    norm_next = lane_sum(functools.reduce(jnp.add, sums))

    right = right_ref[...]
    residual = right - step * (amplitude * kernel_ref[...] + jitter * right)
    direction = residual + turn * right
    applied = amplitude * total + jitter * direction
    direction_ref[...] = direction
    residual_ref[...] = residual
    applied_ref[...] = applied
    columns_ref[...] = into_columns([step, norm_next, norm], cols)

    low = right - right.astype(BF16).astype(F32)
    low_direction = direction - direction.astype(BF16).astype(F32)
    slope = slope_ref[...]
    packed = jnp.zeros((cols, 128), F32)
    for slot, values in enumerate([
        direction * applied,
        low * total,
        right * slope,
        right * slopes,
        direction * slope,
        direction * slopes,
        low_direction * total,
    ]):
        packed = packed + to_lanes(lane_sum(values), slot)
    packed = jnp.sum(packed, axis=0, keepdims=True)
    for peer in range(message_ref.shape[0]):
        message_ref[peer, 0:1, :] = packed
        message_ref[peer, 1:2, :] = total[0:1, :]


def middle_kernel(part_count, wide_ref, products_ref, turned_ref, out_ref):
    blocks, cols, own = wide_ref.shape
    count = blocks // part_count
    zero = jnp.zeros((cols, own), F32)
    sums = []
    for part in range(part_count):
        def one_block(block, carried, part=part):
            block = part * count + block
            right = wide_ref[block]
            direction = turned_ref[block]
            product = products_ref[block]
            low = right - right.astype(BF16).astype(F32)
            low_direction = direction - direction.astype(BF16).astype(F32)
            return (
                carried[0] + low * product,
                carried[1] + low_direction * product,
                carried[2] + right * direction,
                carried[3] + direction * direction,
            )

        sums.append(lax.fori_loop(0, count, one_block, (zero,) * 4, unroll=unrolled(count, 4)))
    sums = [lane_sum(functools.reduce(jnp.add, parts)) for parts in zip(*sums)]
    out_ref[...] = into_columns(sums, cols)


def last_kernel(
    part_count, points_total, place_ref, scalars_ref, right_ref, direction_ref, residual_ref,
    applied_ref, columns_ref, middle_ref, wide_ref, products_ref, turned_ref, received_ref,
    solution_hbm, final_hbm, gradient_ref, solution_ref, final_ref, sems
):
    cols, own = right_ref.shape
    amplitude = scalars_ref[0:1, :]
    place = place_ref[0]
    devices = received_ref.shape[0]

    def gather_sums(device, carried):
        return carried + received_ref[device, 0:1, :]

    sums = lax.fori_loop(
        0, devices, gather_sums, jnp.zeros((1, 128), F32), unroll=unrolled(devices, 32)
    )
    step, norm_next, norm = [columns_ref[:, slot : slot + 1] for slot in range(3)]
    step_next = norm_next / from_lanes(sums, 0, cols)

    solution_ref[...] = step * right_ref[...] + step_next * direction_ref[...]
    final_ref[...] = residual_ref[...] - step_next * applied_ref[...]
    copies = [
        pltpu.make_async_copy(solution_ref, solution_hbm, sems.at[0]),
        pltpu.make_async_copy(final_ref, final_hbm, sems.at[1]),
    ]
    for copy in copies:
        copy.start()

    low_next, right_slope, right_slope_next, slope_cross, slope_square, low_square = [
        from_lanes(sums, slot, cols) for slot in range(1, 7)
    ]
    low_first, low_second, dots, squares = [middle_ref[:, slot : slot + 1] for slot in range(4)]
    count = wide_ref.shape[0] // part_count
    zero = jnp.zeros((cols, own), F32)
    row_zero = jnp.zeros((1, own), F32)
    sums = []
    for part in range(part_count):
        def one_block(index, carried, part=part):
            whole, first_row = carried
            block = part * count + index
            rounded = (step * wide_ref[block] + step_next * turned_ref[block]).astype(BF16).astype(F32)
            source = index * part_count + (place + part) % part_count
            return (
                whole + products_ref[block] * rounded,
                first_row + received_ref[source, 1:2, :] * rounded[0:1, :],
            )

        sums.append(lax.fori_loop(0, count, one_block, (zero, row_zero), unroll=unrolled(count, 8)))
    whole, first_row = [functools.reduce(jnp.add, parts) for parts in zip(*sums)]
    right_kernel = lane_sum(whole) + step * low_first + step_next * low_next
    direction_kernel = lane_sum(first_row) + (step * low_second + step_next * low_square)[0:1, :]
    is_first = lax.broadcasted_iota(jnp.int32, (cols, 1), 0) == 0
    weight = jnp.where(is_first, 1.0, -1.0 / (cols - 1))
    for slot, (right_form, direction_form) in enumerate((
        (
            amplitude[:, 0:1] * (step * right_slope + step_next * right_slope_next),
            amplitude[:, 0:1] * (step * slope_cross + step_next * slope_square),
        ),
        (right_kernel, jnp.broadcast_to(direction_kernel, (cols, 1))),
        (step * norm + step_next * dots, step * dots + step_next * squares),
    )):
        form = jnp.where(is_first, step * right_form + step_next * direction_form, right_form)
        gradient_ref[slot] = jnp.sum(weight * form) * (0.5 / points_total)
    for copy in copies:
        copy.wait()


SWAP = [(0, 1), (1, 0)]


def local(mesh_shape, points, right_side, lengthscale, outputscale, noise_level):
    axes = ("blk", "grp")
    feats, own = points.shape
    cols = right_side.shape[0]
    devices = mesh_shape["blk"] * mesh_shape["grp"]
    paired = mesh_shape["grp"] == 2
    peers = mesh_shape["blk"] if paired else devices
    part_count = 2 if paired else 1
    pair = 2 if peers % 2 == 0 else 1
    params = pltpu.CompilerParams(vmem_limit_bytes=(4 << 20) + devices * (40 << 10))
    shape = pltpu.VMEM
    result = jax.ShapeDtypeStruct

    def near(*arrays):
        return [pltpu.with_memory_space_constraint(array, pltpu.VMEM) for array in arrays]

    call = functools.partial(pl.pallas_call, compiler_params=params)
    place = lax.axis_index("grp").astype(jnp.int32)[None]

    row_shape = shape((cols, own), F32)
    message, own_points, own_right = call(
        pack_kernel,
        out_shape=(
            shape((peers, feats + 2 * cols, own), BF16), shape((feats, own), BF16), row_shape,
        ),
        in_specs=_hbm(2),
        out_specs=tuple(_vmem(3)),
        scratch_shapes=[pltpu.SemaphoreType.DMA((2,))],
        name="pack",
    )(*[pltpu.with_memory_space_constraint(array, pltpu.HBM) for array in (points, right_side)])
    vectors = [lax.all_to_all(message, "blk" if paired else axes, 0, 0, tiled=True)]
    if paired:
        vectors.append(lax.ppermute(vectors[0], "grp", SWAP))

    tile_shape = shape((peers // pair, own, pair * own), BF16)
    kerns = []
    total = []
    for part in range(part_count):
        final_part = part + 1 == part_count
        outs = [tile_shape, row_shape]
        if final_part:
            outs.append(shape((devices, cols // 2 if paired else cols, own), F32))
        tiles, *total = call(
            functools.partial(kern_kernel, pair, part > 0),
            out_shape=tuple(outs),
            in_specs=[_smem()] + _vmem(3 if part > 0 else 2),
            out_specs=tuple(_vmem(len(outs))),
            name="kern",
        )(lengthscale, *near(own_points, vectors[part], *total))
        kerns.append(tiles)
    kernel_first, message = total
    received = [lax.all_to_all(message, axes, 0, 0, tiled=True)]
    wide_shape = shape((devices, cols, own), F32)
    dkern, slope_first, wide, norm, scalars = call(
        functools.partial(dkern_kernel, part_count, pair),
        out_shape=(
            shape((devices // pair, own, pair * own), BF16), row_shape, wide_shape, row_shape,
            shape((8, 128), F32),
        ),
        in_specs=[_smem()] * 3 + _vmem(1 + part_count),
        out_specs=tuple(_vmem(5)),
        name="dkern",
    )(lengthscale, outputscale, noise_level, *near(own_points, *vectors))
    received[0], dkern = lax.optimization_barrier((received[0], dkern))
    if paired:
        received.append(lax.ppermute(received[0], "grp", SWAP))

    message, direction, residual, applied, columns, products, turned = call(
        functools.partial(second_kernel, part_count, pair, len(received)),
        out_shape=(
            shape((devices, 2, own), F32), row_shape, row_shape, row_shape, shape((cols, 128), F32),
            wide_shape, wide_shape,
        ),
        in_specs=[_smem()] + _vmem(7 + part_count + len(received)),
        out_specs=tuple(_vmem(7)),
        name="second",
    )(
        place,
        *near(scalars, own_right, kernel_first, slope_first, dkern, wide, norm, *kerns, *received),
    )
    received = lax.all_to_all(message, axes, 0, 0, tiled=True)
    middle = call(
        functools.partial(middle_kernel, part_count),
        out_shape=shape((cols, 128), F32),
        in_specs=_vmem(3),
        out_specs=_vmem(1)[0],
        name="middle",
    )(*near(wide, products, turned))

    solution, final, gradient = call(
        functools.partial(last_kernel, part_count, float(own * devices)),
        out_shape=(result((cols, own), F32), result((cols, own), F32), result((3,), F32)),
        in_specs=[_smem()] + _vmem(11),
        out_specs=tuple(_hbm(2) + [_smem()]),
        scratch_shapes=[
            pltpu.VMEM((cols, own), F32),
            pltpu.VMEM((cols, own), F32),
            pltpu.SemaphoreType.DMA((2,)),
        ],
        name="last",
    )(
        place,
        *near(scalars, own_right, direction, residual, applied, columns, middle, wide, products, turned, received),
    )
    return solution, final, gradient


def solution(mesh):
    whole = P(None, ("blk", "grp"))
    return jax.shard_map(
        functools.partial(local, dict(mesh.shape)),
        mesh=mesh,
        in_specs=(whole, whole, P(), P(), P()),
        out_specs=(whole, whole, P()),
        check_vma=False,
    )
```

```python
import functools
import math

import jax
import jax.numpy as jnp
from jax import lax
from jax.experimental import pallas as pl
from jax.experimental.pallas import tpu as pltpu
from jax.sharding import PartitionSpec as P

F32 = jnp.float32
BF16 = jnp.bfloat16
LOG2E = math.log2(math.e)
TINY = 1e-36
NT = (((1,), (1,)), ((), ()))


def _vmem(count):
    return [pl.BlockSpec(memory_space=pltpu.VMEM) for _ in range(count)]


def _smem():
    return pl.BlockSpec(memory_space=pltpu.SMEM)


def _hbm(count):
    return [pl.BlockSpec(memory_space=pltpu.HBM) for _ in range(count)]


def lane_sum(values):
    return jnp.sum(values, axis=1, keepdims=True)


def unrolled(count, most):
    return max(divisor for divisor in range(1, most + 1) if count % divisor == 0)


def pack_kernel(points_hbm, right_hbm, out_ref, points_ref, right_ref, sems):
    feats = points_ref.shape[0]
    cols = right_ref.shape[0]
    copies = [
        pltpu.make_async_copy(right_hbm, right_ref, sems.at[0]),
        pltpu.make_async_copy(points_hbm, points_ref, sems.at[1]),
    ]
    for copy in copies:
        copy.start()
    copies[0].wait()
    right = right_ref[...]
    high = right.astype(BF16)
    low = (right - high.astype(F32)).astype(BF16)
    for peer in range(out_ref.shape[0]):
        out_ref[peer, feats : feats + cols, :] = high
        out_ref[peer, feats + cols : feats + 2 * cols, :] = low
    copies[1].wait()
    points = points_ref[...]
    for peer in range(out_ref.shape[0]):
        out_ref[peer, 0:feats, :] = points


class Distances:
    def __init__(self, length_ref, points_ref):
        scale = length_ref[0]
        self.scale = scale
        self.factor = (5.0 * LOG2E * LOG2E) / (scale * scale)
        own = points_ref.shape[1]
        points = points_ref[...].astype(F32).T
        squares = jnp.sum(points * points, axis=1, keepdims=True) * self.factor
        self.squares = jnp.broadcast_to(squares, (own, own))
        self.points = (-2.0 * points).astype(BF16)

    def __call__(self, points):
        wide = points.astype(F32)
        squares = jnp.sum(wide * wide, axis=0, keepdims=True) * self.factor
        inner = jnp.dot(self.points, points, preferred_element_type=F32)
        reduced = jnp.maximum((self.squares + squares) + inner * self.factor, TINY)
        return reduced, reduced * lax.rsqrt(reduced)


def kern_tile(reduced, root):
    shifted = root + 1.5 * LOG2E
    return (shifted * shifted + 0.75 * LOG2E * LOG2E) * jnp.exp2(-math.log2(3.0 * LOG2E * LOG2E) - root)


def kern_kernel(pair, has_before, length_ref, points_ref, part_ref, *refs):
    before = refs[0][...] if has_before else None
    tiles_ref, *outs = refs[1 if has_before else 0 :]
    feats, own = points_ref.shape
    total_ref = outs[0]
    cols = total_ref.shape[0]
    distances = Distances(length_ref, points_ref)
    steps = part_ref.shape[0] // pair
    total = before if has_before else jnp.zeros((cols, own), F32)

    def one_pair(step, total):
        vectors = []
        for side in range(pair):
            block = step * pair + side
            tile = kern_tile(*distances(part_ref[block, 0:feats, :]))
            tiles_ref[step, :, pl.ds(side * own, own)] = tile.astype(BF16)
            vectors.append(part_ref[block, feats : feats + cols, :])
        vectors = jnp.concatenate(vectors, axis=1) if pair > 1 else vectors[0]
        return total + lax.dot_general(vectors, tiles_ref[step], NT, preferred_element_type=F32)

    total = lax.fori_loop(0, steps, one_pair, total, unroll=unrolled(steps, 8))
    total_ref[...] = total
    if len(outs) > 1:
        message_ref = outs[1]
        rows = message_ref.shape[1]
        for peer in range(message_ref.shape[0]):
            first = (peer * rows) % cols
            message_ref[peer] = total[first : first + rows]


def dkern_kernel(
    part_count, pair, length_ref, amplitude_ref, jitter_ref, points_ref, *refs
):
    parts = refs[:part_count]
    tiles_ref, total_ref, wide_ref, norm_ref, scalars_ref = refs[part_count:]
    for slot, scalar in enumerate((amplitude_ref, jitter_ref)):
        scalars_ref[slot : slot + 1, :] = jnp.full((1, 128), scalar[0], F32)
    feats, own = points_ref.shape
    cols = total_ref.shape[0]
    distances = Distances(length_ref, points_ref)
    slope = 1.0 / (3.0 * LOG2E * LOG2E * LOG2E * distances.scale)
    total = jnp.zeros((cols, own), F32)
    norms = []
    base = 0
    for part in parts:
        steps = part.shape[0] // pair

        def one_pair(step, carried, part=part, base=base):
            total, norm = carried
            vectors = []
            for side in range(pair):
                block = step * pair + side
                reduced, root = distances(part[block, 0:feats, :])
                tile = (reduced * slope) * ((root + LOG2E) * jnp.exp2(-root))
                tiles_ref[base + step, :, pl.ds(side * own, own)] = tile.astype(BF16)
                high = part[block, feats : feats + cols, :]
                right = high.astype(F32) + part[block, feats + cols : feats + 2 * cols, :].astype(F32)
                wide_ref[base * pair + block] = right
                norm = norm + right * right
                vectors.append(high)
            vectors = jnp.concatenate(vectors, axis=1) if pair > 1 else vectors[0]
            total = total + lax.dot_general(
                vectors, tiles_ref[base + step], NT, preferred_element_type=F32
            )
            return total, norm

        total, norm = lax.fori_loop(
            0, steps, one_pair, (total, jnp.zeros((cols, own), F32)), unroll=unrolled(steps, 4)
        )
        norms.append(norm)
        base += steps
    total_ref[...] = total
    norm_ref[...] = jnp.broadcast_to(lane_sum(functools.reduce(jnp.add, norms)), norm_ref.shape)


def from_lanes(row, first, cols):
    lanes = lax.broadcasted_iota(jnp.int32, (cols, 128), 1)
    rows = lax.broadcasted_iota(jnp.int32, (cols, 128), 0)
    picked = jnp.where(lanes == rows + first, jnp.broadcast_to(row, (cols, 128)), 0.0)
    return lane_sum(picked)


def into_columns(columns, cols):
    lanes = lax.broadcasted_iota(jnp.int32, (cols, 128), 1)
    kept = jnp.zeros((cols, 128), F32)
    for slot, column in enumerate(columns):
        kept = jnp.where(lanes == slot, jnp.broadcast_to(column, (cols, 128)), kept)
    return kept


def second_kernel(
    part_count, pair, halves, place_ref, scalars_ref, right_ref, kernel_ref, slope_ref,
    dkern_ref, wide_ref, norm_ref, *refs
):
    kerns = refs[:part_count]
    received = refs[part_count : part_count + halves]
    (
        message_ref, direction_ref, residual_ref, applied_ref, columns_ref, products_ref, turned_ref,
    ) = refs[part_count + halves :]
    cols, own = right_ref.shape
    amplitude = scalars_ref[0:1, :]
    jitter = scalars_ref[1:2, :]
    place = place_ref[0]
    zero = jnp.zeros((cols, own), F32)
    norm = norm_ref[:, 0:1]
    count = kerns[0].shape[0] * pair

    sums = []
    for part in range(part_count):
        def first_pass(block, carried, part=part):
            source = block * part_count + (place + part) % part_count
            if halves == 2:
                mine = received[0][source]
                other = received[1][source]
                product = jnp.concatenate(
                    [jnp.where(place == 0, mine, other), jnp.where(place == 0, other, mine)], axis=0
                )
            else:
                product = received[0][source]
            products_ref[part * count + block] = product
            right = wide_ref[part * count + block]
            applied = amplitude * product + jitter * right
            return carried[0] + right * applied, carried[1] + applied * applied

        sums.append(lax.fori_loop(0, count, first_pass, (zero, zero), unroll=unrolled(count, 8)))
    curvature, length = [lane_sum(functools.reduce(jnp.add, parts)) for parts in zip(*sums)]
    step = norm / curvature
    turn = (step * step * length - norm) / norm

    sums = []
    total = zero
    slopes = zero
    for part in range(part_count):
        base = part * (count // pair)

        def second_pass(index, carried, part=part, base=base):
            total, slopes, norms = carried
            rounded = []
            for side in range(pair):
                block = part * count + index * pair + side
                right = wide_ref[block]
                residual = right - step * (amplitude * products_ref[block] + jitter * right)
                direction = residual + turn * right
                turned_ref[block] = direction
                norms = norms + residual * residual
                rounded.append(direction)
            rounded = jnp.concatenate(rounded, axis=1) if pair > 1 else rounded[0]
            rounded = rounded.astype(BF16)
            total = total + lax.dot_general(
                rounded, kerns[part][index], NT, preferred_element_type=F32
            )
            slopes = slopes + lax.dot_general(
                rounded, dkern_ref[base + index], NT, preferred_element_type=F32
            )
            return total, slopes, norms

        total, slopes, norms = lax.fori_loop(
            0, count // pair, second_pass, (total, slopes, zero), unroll=unrolled(count // pair, 8)
        )
        sums.append(norms)
    norm_next = lane_sum(functools.reduce(jnp.add, sums))

    right = right_ref[...]
    residual = right - step * (amplitude * kernel_ref[...] + jitter * right)
    direction = residual + turn * right
    applied = amplitude * total + jitter * direction
    direction_ref[...] = direction
    residual_ref[...] = residual
    applied_ref[...] = applied
    columns_ref[...] = into_columns([step, norm_next, norm, turn], cols)

    low = right - right.astype(BF16).astype(F32)
    low_direction = direction - direction.astype(BF16).astype(F32)
    slope = slope_ref[...]
    lanes = lax.broadcasted_iota(jnp.int32, (cols, 128), 1)
    rows = lax.broadcasted_iota(jnp.int32, (cols, 128), 0)
    packed = jnp.zeros((cols, 128), F32)
    for slot, values in enumerate([
        direction * applied, low * total, low * kernel_ref[...], right * slope, right * slopes,
    ]):
        packed = jnp.where(lanes == rows + slot * cols, lane_sum(values), packed)
    rows = jnp.where(rows == 0, 5 * cols, 128)
    for slot, values in enumerate([
        direction * slope, direction * slopes, low_direction * kernel_ref[...], low_direction * total,
    ]):
        packed = jnp.where(lanes == rows + slot, lane_sum(values), packed)
    packed = jnp.sum(packed, axis=0, keepdims=True)
    for peer in range(message_ref.shape[0]):
        message_ref[peer, 0:1, :] = packed
        message_ref[peer, 1:2, :] = total[0:1, :]


def last_kernel(
    part_count, points_total, place_ref, scalars_ref, right_ref, direction_ref, residual_ref,
    applied_ref, columns_ref, wide_ref, products_ref, turned_ref, received_ref,
    solution_hbm, final_hbm, gradient_ref, solution_ref, final_ref, sems
):
    cols, own = right_ref.shape
    amplitude = scalars_ref[0:1, :]
    place = place_ref[0]
    devices = received_ref.shape[0]

    def gather_sums(device, carried):
        return carried + received_ref[device, 0:1, :]

    sums = lax.fori_loop(
        0, devices, gather_sums, jnp.zeros((1, 128), F32), unroll=unrolled(devices, 32)
    )
    step, norm_next, norm = [columns_ref[:, slot : slot + 1] for slot in range(3)]
    step_next = norm_next / from_lanes(sums, 0, cols)

    solution_ref[...] = step * right_ref[...] + step_next * direction_ref[...]
    final_ref[...] = residual_ref[...] - step_next * applied_ref[...]
    copies = [
        pltpu.make_async_copy(solution_ref, solution_hbm, sems.at[0]),
        pltpu.make_async_copy(final_ref, final_hbm, sems.at[1]),
    ]
    for copy in copies:
        copy.start()

    low_next, low_first, right_slope, right_slope_next = [
        from_lanes(sums, slot * cols, cols) for slot in range(1, 5)
    ]
    slope_cross, slope_square, low_second, low_square = [
        sums[:, 5 * cols + slot : 5 * cols + slot + 1] for slot in range(4)
    ]
    turn = columns_ref[:, 3:4]
    dots = turn * norm
    squares = norm_next + turn * dots
    count = wide_ref.shape[0] // part_count
    zero = jnp.zeros((cols, own), F32)
    row_zero = jnp.zeros((1, own), F32)
    sums = []
    for part in range(part_count):
        def one_block(index, carried, part=part):
            whole, first_row = carried
            block = part * count + index
            rounded = (step * wide_ref[block] + step_next * turned_ref[block]).astype(BF16).astype(F32)
            source = index * part_count + (place + part) % part_count
            return (
                whole + products_ref[block] * rounded,
                first_row + received_ref[source, 1:2, :] * rounded[0:1, :],
            )

        sums.append(lax.fori_loop(0, count, one_block, (zero, row_zero), unroll=unrolled(count, 8)))
    whole, first_row = [functools.reduce(jnp.add, parts) for parts in zip(*sums)]
    right_kernel = lane_sum(whole) + step * low_first + step_next * low_next
    first_step, second_step = step[0:1], step_next[0:1]
    direction_kernel = lane_sum(first_row) + first_step * low_second + second_step * low_square
    direction_slope = first_step * slope_cross + second_step * slope_square
    is_first = lax.broadcasted_iota(jnp.int32, (cols, 1), 0) == 0
    weight = jnp.where(is_first, 1.0, -1.0 / (cols - 1))
    for slot, (right_form, direction_form) in enumerate((
        (
            amplitude[:, 0:1] * (step * right_slope + step_next * right_slope_next),
            amplitude[:, 0:1] * direction_slope,
        ),
        (right_kernel, direction_kernel),
        (step * norm + step_next * dots, (step * dots + step_next * squares)[0:1]),
    )):
        form = jnp.where(is_first, step * right_form + step_next * direction_form, right_form)
        gradient_ref[slot] = jnp.sum(weight * form) * (0.5 / points_total)
    for copy in copies:
        copy.wait()


SWAP = [(0, 1), (1, 0)]


def local(mesh_shape, points, right_side, lengthscale, outputscale, noise_level):
    axes = ("blk", "grp")
    feats, own = points.shape
    cols = right_side.shape[0]
    devices = mesh_shape["blk"] * mesh_shape["grp"]
    paired = mesh_shape["grp"] == 2
    peers = mesh_shape["blk"] if paired else devices
    part_count = 2 if paired else 1
    pair = 2 if peers % 2 == 0 else 1
    params = pltpu.CompilerParams(vmem_limit_bytes=(4 << 20) + devices * (40 << 10))
    shape = pltpu.VMEM
    result = jax.ShapeDtypeStruct

    def near(*arrays):
        return [pltpu.with_memory_space_constraint(array, pltpu.VMEM) for array in arrays]

    call = functools.partial(pl.pallas_call, compiler_params=params)
    place = lax.axis_index("grp").astype(jnp.int32)[None]

    row_shape = shape((cols, own), F32)
    message, own_points, own_right = call(
        pack_kernel,
        out_shape=(
            shape((peers, feats + 2 * cols, own), BF16), shape((feats, own), BF16), row_shape,
        ),
        in_specs=_hbm(2),
        out_specs=tuple(_vmem(3)),
        scratch_shapes=[pltpu.SemaphoreType.DMA((2,))],
        name="pack",
    )(*[pltpu.with_memory_space_constraint(array, pltpu.HBM) for array in (points, right_side)])
    vectors = [lax.all_to_all(message, "blk" if paired else axes, 0, 0, tiled=True)]
    if paired:
        vectors.append(lax.ppermute(vectors[0], "grp", SWAP))

    tile_shape = shape((peers // pair, own, pair * own), BF16)
    kerns = []
    total = []
    for part in range(part_count):
        final_part = part + 1 == part_count
        outs = [tile_shape, row_shape]
        if final_part:
            outs.append(shape((devices, cols // 2 if paired else cols, own), F32))
        tiles, *total = call(
            functools.partial(kern_kernel, pair, part > 0),
            out_shape=tuple(outs),
            in_specs=[_smem()] + _vmem(3 if part > 0 else 2),
            out_specs=tuple(_vmem(len(outs))),
            name="kern",
        )(lengthscale, *near(own_points, vectors[part], *total))
        kerns.append(tiles)
    kernel_first, message = total
    received = [lax.all_to_all(message, axes, 0, 0, tiled=True)]
    wide_shape = shape((devices, cols, own), F32)
    dkern, slope_first, wide, norm, scalars = call(
        functools.partial(dkern_kernel, part_count, pair),
        out_shape=(
            shape((devices // pair, own, pair * own), BF16), row_shape, wide_shape, row_shape,
            shape((8, 128), F32),
        ),
        in_specs=[_smem()] * 3 + _vmem(1 + part_count),
        out_specs=tuple(_vmem(5)),
        name="dkern",
    )(lengthscale, outputscale, noise_level, *near(own_points, *vectors))
    received[0], dkern = lax.optimization_barrier((received[0], dkern))
    if paired:
        received.append(lax.ppermute(received[0], "grp", SWAP))

    message, direction, residual, applied, columns, products, turned = call(
        functools.partial(second_kernel, part_count, pair, len(received)),
        out_shape=(
            shape((devices, 2, own), F32), row_shape, row_shape, row_shape, shape((cols, 128), F32),
            wide_shape, wide_shape,
        ),
        in_specs=[_smem()] + _vmem(7 + part_count + len(received)),
        out_specs=tuple(_vmem(7)),
        name="second",
    )(
        place,
        *near(scalars, own_right, kernel_first, slope_first, dkern, wide, norm, *kerns, *received),
    )
    received = lax.all_to_all(message, axes, 0, 0, tiled=True)

    solution, final, gradient = call(
        functools.partial(last_kernel, part_count, float(own * devices)),
        out_shape=(result((cols, own), F32), result((cols, own), F32), result((3,), F32)),
        in_specs=[_smem()] + _vmem(10),
        out_specs=tuple(_hbm(2) + [_smem()]),
        scratch_shapes=[
            pltpu.VMEM((cols, own), F32),
            pltpu.VMEM((cols, own), F32),
            pltpu.SemaphoreType.DMA((2,)),
        ],
        name="last",
    )(
        place,
        *near(scalars, own_right, direction, residual, applied, columns, wide, products, turned, received),
    )
    return solution, final, gradient


def solution(mesh):
    whole = P(None, ("blk", "grp"))
    return jax.shard_map(
        functools.partial(local, dict(mesh.shape)),
        mesh=mesh,
        in_specs=(whole, whole, P(), P(), P()),
        out_specs=(whole, whole, P()),
        check_vma=False,
    )
```

```python
import functools
import math

import jax
import jax.numpy as jnp
from jax import lax
from jax.experimental import pallas as pl
from jax.experimental.pallas import tpu as pltpu
from jax.sharding import PartitionSpec as P

F32 = jnp.float32
BF16 = jnp.bfloat16
LOG2E = math.log2(math.e)
TINY = 1e-36
NT = (((1,), (1,)), ((), ()))


def _vmem(count):
    return [pl.BlockSpec(memory_space=pltpu.VMEM) for _ in range(count)]


def _smem():
    return pl.BlockSpec(memory_space=pltpu.SMEM)


def _hbm(count):
    return [pl.BlockSpec(memory_space=pltpu.HBM) for _ in range(count)]


def lane_sum(values):
    return jnp.sum(values, axis=1, keepdims=True)


def unrolled(count, most):
    return max(divisor for divisor in range(1, most + 1) if count % divisor == 0)


def pack_kernel(points_hbm, right_hbm, out_ref, points_ref, right_ref, sems):
    feats = points_ref.shape[0]
    cols = right_ref.shape[0]
    copies = [
        pltpu.make_async_copy(right_hbm, right_ref, sems.at[0]),
        pltpu.make_async_copy(points_hbm, points_ref, sems.at[1]),
    ]
    for copy in copies:
        copy.start()
    copies[0].wait()
    right = right_ref[...]
    high = right.astype(BF16)
    out_ref[feats : feats + cols, :] = high
    out_ref[feats + cols : feats + 2 * cols, :] = (right - high.astype(F32)).astype(BF16)
    copies[1].wait()
    out_ref[0:feats, :] = points_ref[...]


def fan_kernel(length_ref, amplitude_ref, jitter_ref, *refs):
    *shards, out_ref, scalars_ref = refs
    for slot, scalar in enumerate((length_ref, amplitude_ref, jitter_ref)):
        scalars_ref[slot : slot + 1, :] = jnp.full((1, 128), scalar[0], F32)
    shards = [shard[...] for shard in shards]
    for peer in range(out_ref.shape[0]):
        for side, shard in enumerate(shards):
            out_ref[peer, side] = shard


def source_of(block_ref, core_ref, paired, steps, part, step, side):
    if not paired:
        return step * 2 + side
    core = core_ref[0] if part == 0 else 1 - core_ref[0]
    first = jnp.where((block_ref[0] < steps) == (side == 0), 0, steps)
    return (first + step) * 2 + core


def joined(sums):
    return functools.reduce(jnp.add, [functools.reduce(jnp.add, sides) for sides in sums])


class Distances:
    def __init__(self, scalars_ref, points_ref):
        scale = scalars_ref[0:1, :]
        self.scale = scale
        self.factor = (5.0 * LOG2E * LOG2E) / (scale * scale)
        own = points_ref.shape[1]
        points = points_ref[...].astype(F32).T
        squares = jnp.sum(points * points, axis=1, keepdims=True) * self.factor
        self.squares = jnp.broadcast_to(squares, (own, own))
        self.points = (-2.0 * points).astype(BF16)

    def __call__(self, points):
        wide = points.astype(F32)
        squares = jnp.sum(wide * wide, axis=0, keepdims=True) * self.factor
        inner = jnp.dot(self.points, points, preferred_element_type=F32)
        reduced = jnp.maximum((self.squares + squares) + inner * self.factor, TINY)
        return reduced, reduced * lax.rsqrt(reduced)


def kern_tile(reduced, root):
    shifted = root + 1.5 * LOG2E
    return (shifted * shifted + 0.75 * LOG2E * LOG2E) * jnp.exp2(-math.log2(3.0 * LOG2E * LOG2E) - root)


def kern_kernel(has_before, scalars_ref, points_ref, part_ref, *refs):
    before = refs[0][...] if has_before else None
    tiles_ref, *outs = refs[1 if has_before else 0 :]
    feats, own = points_ref.shape
    total_ref = outs[0]
    cols = total_ref.shape[0]
    distances = Distances(scalars_ref, points_ref)
    steps, sides = part_ref.shape[:2]
    total = before if has_before else jnp.zeros((cols, own), F32)

    def one_pair(step, total):
        vectors = []
        for side in range(sides):
            tile = kern_tile(*distances(part_ref[step, side, 0:feats, :]))
            tiles_ref[step, :, pl.ds(side * own, own)] = tile.astype(BF16)
            vectors.append(part_ref[step, side, feats : feats + cols, :])
        vectors = jnp.concatenate(vectors, axis=1)
        return total + lax.dot_general(vectors, tiles_ref[step], NT, preferred_element_type=F32)

    total = lax.fori_loop(0, steps, one_pair, total, unroll=unrolled(steps, 8))
    total_ref[...] = total
    if len(outs) > 1:
        message_ref = outs[1]
        rows = message_ref.shape[1]
        for peer in range(message_ref.shape[0]):
            first = (peer * rows) % cols
            message_ref[peer] = total[first : first + rows]


def dkern_kernel(part_count, scalars_ref, points_ref, *refs):
    parts = refs[:part_count]
    tiles_ref, total_ref, wide_ref, norm_ref = refs[part_count:]
    feats, own = points_ref.shape
    cols = total_ref.shape[0]
    distances = Distances(scalars_ref, points_ref)
    slope = 1.0 / (3.0 * LOG2E * LOG2E * LOG2E * distances.scale)
    total = jnp.zeros((cols, own), F32)
    norms = []
    base = 0
    for part in parts:
        steps, sides = part.shape[:2]

        def one_pair(step, carried, part=part, base=base):
            total, norm = carried
            norm = list(norm)
            vectors = []
            for side in range(sides):
                reduced, root = distances(part[step, side, 0:feats, :])
                tile = (reduced * slope) * ((root + LOG2E) * jnp.exp2(-root))
                tiles_ref[base + step, :, pl.ds(side * own, own)] = tile.astype(BF16)
                high = part[step, side, feats : feats + cols, :]
                low = part[step, side, feats + cols : feats + 2 * cols, :]
                right = high.astype(F32) + low.astype(F32)
                wide_ref[base + step, side] = right
                norm[side] = norm[side] + right * right
                vectors.append(high)
            vectors = jnp.concatenate(vectors, axis=1)
            total = total + lax.dot_general(
                vectors, tiles_ref[base + step], NT, preferred_element_type=F32
            )
            return total, tuple(norm)

        zeros = (jnp.zeros((cols, own), F32),) * sides
        total, norm = lax.fori_loop(0, steps, one_pair, (total, zeros), unroll=unrolled(steps, 4))
        norms.append(norm)
        base += steps
    total_ref[...] = total
    norm_ref[...] = jnp.broadcast_to(lane_sum(joined(norms)), norm_ref.shape)


def from_lanes(row, first, cols):
    lanes = lax.broadcasted_iota(jnp.int32, (cols, 128), 1)
    rows = lax.broadcasted_iota(jnp.int32, (cols, 128), 0)
    picked = jnp.where(lanes == rows + first, jnp.broadcast_to(row, (cols, 128)), 0.0)
    return lane_sum(picked)


def into_columns(columns, cols):
    lanes = lax.broadcasted_iota(jnp.int32, (cols, 128), 1)
    kept = jnp.zeros((cols, 128), F32)
    for slot, column in enumerate(columns):
        kept = jnp.where(lanes == slot, jnp.broadcast_to(column, (cols, 128)), kept)
    return kept


def second_kernel(
    part_count, paired, block_ref, core_ref, scalars_ref, right_ref, kernel_ref, slope_ref, dkern_ref, wide_ref,
    norm_ref, *refs
):
    kerns = refs[:part_count]
    received = refs[part_count : 2 * part_count]
    (
        message_ref, direction_ref, residual_ref, applied_ref, columns_ref, products_ref, turned_ref,
    ) = refs[2 * part_count :]
    cols, own = right_ref.shape
    sides = wide_ref.shape[1]
    amplitude = scalars_ref[1:2, :]
    jitter = scalars_ref[2:3, :]
    low_core = core_ref[0] == 0
    zero = jnp.zeros((cols, own), F32)
    norm = norm_ref[:, 0:1]
    steps = kerns[0].shape[0]

    sums = []
    for part in range(part_count):
        def first_pass(index, carried, part=part):
            carried = [list(sums) for sums in carried]
            for side in range(sides):
                source = source_of(block_ref, core_ref, paired, steps, part, index, side)
                product = received[0][source]
                if paired:
                    other = received[1][source]
                    product = jnp.concatenate(
                        [jnp.where(low_core, product, other), jnp.where(low_core, other, product)],
                        axis=0,
                    )
                products_ref[part * steps + index, side] = product
                right = wide_ref[part * steps + index, side]
                applied = amplitude * product + jitter * right
                carried[0][side] = carried[0][side] + right * applied
                carried[1][side] = carried[1][side] + applied * applied
            return tuple(tuple(sums) for sums in carried)

        sums.append(
            lax.fori_loop(0, steps, first_pass, ((zero,) * sides,) * 2, unroll=unrolled(steps, 4))
        )
    curvature, length = [lane_sum(joined(parts)) for parts in zip(*sums)]
    step = norm / curvature
    turn = (step * step * length - norm) / norm

    sums = []
    total = zero
    slopes = zero
    for part in range(part_count):
        def second_pass(index, carried, part=part):
            total, slopes, norms = carried
            norms = list(norms)
            rounded = []
            for side in range(sides):
                right = wide_ref[part * steps + index, side]
                product = products_ref[part * steps + index, side]
                residual = right - step * (amplitude * product + jitter * right)
                direction = residual + turn * right
                turned_ref[part * steps + index, side] = direction
                norms[side] = norms[side] + residual * residual
                rounded.append(direction)
            rounded = jnp.concatenate(rounded, axis=1).astype(BF16)
            total = total + lax.dot_general(
                rounded, kerns[part][index], NT, preferred_element_type=F32
            )
            slopes = slopes + lax.dot_general(
                rounded, dkern_ref[part * steps + index], NT, preferred_element_type=F32
            )
            return total, slopes, tuple(norms)

        total, slopes, norms = lax.fori_loop(
            0, steps, second_pass, (total, slopes, (zero,) * sides), unroll=unrolled(steps, 8)
        )
        sums.append(norms)
    norm_next = lane_sum(joined(sums))

    right = right_ref[...]
    residual = right - step * (amplitude * kernel_ref[...] + jitter * right)
    direction = residual + turn * right
    applied = amplitude * total + jitter * direction
    direction_ref[...] = direction
    residual_ref[...] = residual
    applied_ref[...] = applied
    columns_ref[...] = into_columns([step, norm_next, norm, turn], cols)

    low = right - right.astype(BF16).astype(F32)
    low_direction = direction - direction.astype(BF16).astype(F32)
    slope = slope_ref[...]
    lanes = lax.broadcasted_iota(jnp.int32, (cols, 128), 1)
    rows = lax.broadcasted_iota(jnp.int32, (cols, 128), 0)
    packed = jnp.zeros((cols, 128), F32)
    for slot, values in enumerate([
        direction * applied, low * total, low * kernel_ref[...], right * slope, right * slopes,
    ]):
        packed = jnp.where(lanes == rows + slot * cols, lane_sum(values), packed)
    rows = jnp.where(rows == 0, 5 * cols, 128)
    for slot, values in enumerate([
        direction * slope, direction * slopes, low_direction * kernel_ref[...], low_direction * total,
    ]):
        packed = jnp.where(lanes == rows + slot, lane_sum(values), packed)
    packed = jnp.sum(packed, axis=0, keepdims=True)
    for peer in range(message_ref.shape[0]):
        message_ref[peer, 0:1, :] = packed
        message_ref[peer, 1:2, :] = total[0:1, :]


def last_kernel(
    part_count, paired, points_total, block_ref, core_ref, scalars_ref, right_ref, direction_ref, residual_ref,
    applied_ref, columns_ref, wide_ref, products_ref, turned_ref, received_ref,
    solution_hbm, final_hbm, gradient_ref, solution_ref, final_ref, sems
):
    cols, own = right_ref.shape
    amplitude = scalars_ref[1:2, :]
    devices = received_ref.shape[0]

    def gather_sums(device, carried):
        return carried + received_ref[device, 0:1, :]

    sums = lax.fori_loop(
        0, devices, gather_sums, jnp.zeros((1, 128), F32), unroll=unrolled(devices, 32)
    )
    step, norm_next, norm = [columns_ref[:, slot : slot + 1] for slot in range(3)]
    step_next = norm_next / from_lanes(sums, 0, cols)

    solution_ref[...] = step * right_ref[...] + step_next * direction_ref[...]
    final_ref[...] = residual_ref[...] - step_next * applied_ref[...]
    copies = [
        pltpu.make_async_copy(solution_ref, solution_hbm, sems.at[0]),
        pltpu.make_async_copy(final_ref, final_hbm, sems.at[1]),
    ]
    for copy in copies:
        copy.start()

    low_next, low_first, right_slope, right_slope_next = [
        from_lanes(sums, slot * cols, cols) for slot in range(1, 5)
    ]
    slope_cross, slope_square, low_second, low_square = [
        sums[:, 5 * cols + slot : 5 * cols + slot + 1] for slot in range(4)
    ]
    turn = columns_ref[:, 3:4]
    dots = turn * norm
    squares = norm_next + turn * dots
    steps, sides = wide_ref.shape[0] // part_count, wide_ref.shape[1]
    zero = jnp.zeros((cols, own), F32)
    row_zero = jnp.zeros((1, own), F32)
    sums = []
    for part in range(part_count):
        def one_pair(index, carried, part=part):
            carried = [list(sums) for sums in carried]
            block = part * steps + index
            for side in range(sides):
                vector = step * wide_ref[block, side] + step_next * turned_ref[block, side]
                rounded = vector.astype(BF16).astype(F32)
                source = source_of(block_ref, core_ref, paired, steps, part, index, side)
                carried[0][side] = carried[0][side] + products_ref[block, side] * rounded
                carried[1][side] = carried[1][side] + received_ref[source, 1:2, :] * rounded[0:1, :]
            return tuple(tuple(sums) for sums in carried)

        start = ((zero,) * sides, (row_zero,) * sides)
        sums.append(lax.fori_loop(0, steps, one_pair, start, unroll=unrolled(steps, 4)))
    whole, first_row = [joined(parts) for parts in zip(*sums)]
    right_kernel = lane_sum(whole) + step * low_first + step_next * low_next
    first_step, second_step = step[0:1], step_next[0:1]
    direction_kernel = lane_sum(first_row) + first_step * low_second + second_step * low_square
    direction_slope = first_step * slope_cross + second_step * slope_square
    is_first = lax.broadcasted_iota(jnp.int32, (cols, 1), 0) == 0
    weight = jnp.where(is_first, 1.0, -1.0 / (cols - 1))
    for slot, (right_form, direction_form) in enumerate((
        (
            amplitude[:, 0:1] * (step * right_slope + step_next * right_slope_next),
            amplitude[:, 0:1] * direction_slope,
        ),
        (right_kernel, direction_kernel),
        (step * norm + step_next * dots, (step * dots + step_next * squares)[0:1]),
    )):
        form = jnp.where(is_first, step * right_form + step_next * direction_form, right_form)
        gradient_ref[slot] = jnp.sum(weight * form) * (0.5 / points_total)
    for copy in copies:
        copy.wait()


SWAP = [(0, 1), (1, 0)]


def local(mesh_shape, points, right_side, lengthscale, outputscale, noise_level):
    axes = ("blk", "grp")
    feats, own = points.shape
    cols = right_side.shape[0]
    rows = feats + 2 * cols
    blocks = mesh_shape["blk"]
    devices = blocks * mesh_shape["grp"]
    paired = mesh_shape["grp"] == 2 and blocks % 2 == 0
    part_count = 2 if paired else 1
    steps = devices // (2 * part_count)
    params = pltpu.CompilerParams(vmem_limit_bytes=(4 << 20) + devices * (40 << 10))
    shape = pltpu.VMEM
    result = jax.ShapeDtypeStruct

    def near(*arrays):
        return [pltpu.with_memory_space_constraint(array, pltpu.VMEM) for array in arrays]

    call = functools.partial(pl.pallas_call, compiler_params=params)
    place = [lax.axis_index(axis).astype(jnp.int32)[None] for axis in axes]

    row_shape = shape((cols, own), F32)
    shard, own_points, own_right = call(
        pack_kernel,
        out_shape=(shape((rows, own), BF16), shape((feats, own), BF16), row_shape),
        in_specs=_hbm(2),
        out_specs=tuple(_vmem(3)),
        scratch_shapes=[pltpu.SemaphoreType.DMA((2,))],
        name="pack",
    )(*[pltpu.with_memory_space_constraint(array, pltpu.HBM) for array in (points, right_side)])
    shards = [shard]
    if paired:
        half = blocks // 2
        shards.append(lax.ppermute(shard, "blk", [(at, (at + half) % blocks) for at in range(blocks)]))
    peers = blocks // 2 if paired else devices
    message, scalars = call(
        fan_kernel,
        out_shape=(shape((peers, len(shards), rows, own), BF16), shape((8, 128), F32)),
        in_specs=[_smem()] * 3 + _vmem(len(shards)),
        out_specs=tuple(_vmem(2)),
        name="fan",
    )(lengthscale, outputscale, noise_level, *near(*shards))
    if paired:
        groups = [
            [2 * (side * half + at) + core for at in range(half)] for side in range(2) for core in range(2)
        ]
        vectors = [lax.all_to_all(message, axes, 0, 0, tiled=True, axis_index_groups=groups)]
        vectors.append(lax.ppermute(vectors[0], "grp", SWAP))
    else:
        vectors = [lax.all_to_all(message, axes, 0, 0, tiled=True).reshape(steps, 2, rows, own)]

    kerns = []
    total = []
    for part in range(part_count):
        outs = [shape((steps, own, 2 * own), BF16), row_shape]
        if part + 1 == part_count:
            outs.append(shape((devices, cols // part_count, own), F32))
        tiles, *total = call(
            functools.partial(kern_kernel, part > 0),
            out_shape=tuple(outs),
            in_specs=_vmem(4 if part > 0 else 3),
            out_specs=tuple(_vmem(len(outs))),
            name="kern",
        )(*near(scalars, own_points, vectors[part], *total))
        kerns.append(tiles)
    kernel_first, message = total
    received = [lax.all_to_all(message, axes, 0, 0, tiled=True)]
    wide_shape = shape((devices // 2, 2, cols, own), F32)
    dkern, slope_first, wide, norm = call(
        functools.partial(dkern_kernel, part_count),
        out_shape=(
            shape((devices // 2, own, 2 * own), BF16), row_shape, wide_shape, row_shape,
        ),
        in_specs=_vmem(2 + part_count),
        out_specs=tuple(_vmem(4)),
        name="dkern",
    )(*near(scalars, own_points, *vectors))
    received[0], dkern = lax.optimization_barrier((received[0], dkern))
    if paired:
        received.append(lax.ppermute(received[0], "grp", SWAP))

    message, direction, residual, applied, columns, products, turned = call(
        functools.partial(second_kernel, part_count, paired),
        out_shape=(
            shape((devices, 2, own), F32), row_shape, row_shape, row_shape, shape((cols, 128), F32),
            wide_shape, wide_shape,
        ),
        in_specs=[_smem()] * 2 + _vmem(7 + 2 * part_count),
        out_specs=tuple(_vmem(7)),
        name="second",
    )(
        *place,
        *near(scalars, own_right, kernel_first, slope_first, dkern, wide, norm, *kerns, *received),
    )
    received = lax.all_to_all(message, axes, 0, 0, tiled=True)

    solution, final, gradient = call(
        functools.partial(last_kernel, part_count, paired, float(own * devices)),
        out_shape=(result((cols, own), F32), result((cols, own), F32), result((3,), F32)),
        in_specs=[_smem()] * 2 + _vmem(10),
        out_specs=tuple(_hbm(2) + [_smem()]),
        scratch_shapes=[
            pltpu.VMEM((cols, own), F32),
            pltpu.VMEM((cols, own), F32),
            pltpu.SemaphoreType.DMA((2,)),
        ],
        name="last",
    )(
        *place,
        *near(scalars, own_right, direction, residual, applied, columns, wide, products, turned, received),
    )
    return solution, final, gradient


def solution(mesh):
    whole = P(None, ("blk", "grp"))
    return jax.shard_map(
        functools.partial(local, dict(mesh.shape)),
        mesh=mesh,
        in_specs=(whole, whole, P(), P(), P()),
        out_specs=(whole, whole, P()),
        check_vma=False,
    )
```

```python
import functools
import math

import jax
import jax.numpy as jnp
from jax import lax
from jax.experimental import pallas as pl
from jax.experimental.pallas import tpu as pltpu
from jax.sharding import PartitionSpec as P

F32 = jnp.float32
BF16 = jnp.bfloat16
LOG2E = math.log2(math.e)
TINY = 1e-36
NT = (((1,), (1,)), ((), ()))


def _vmem(count):
    return [pl.BlockSpec(memory_space=pltpu.VMEM) for _ in range(count)]


def _smem():
    return pl.BlockSpec(memory_space=pltpu.SMEM)


def _hbm(count):
    return [pl.BlockSpec(memory_space=pltpu.HBM) for _ in range(count)]


def lane_sum(values):
    return jnp.sum(values, axis=1, keepdims=True)


def unrolled(count, most):
    return max(divisor for divisor in range(1, most + 1) if count % divisor == 0)


def pack_kernel(points_hbm, right_hbm, out_ref, points_ref, right_ref, sems):
    feats = points_ref.shape[0]
    cols = right_ref.shape[0]
    copies = [
        pltpu.make_async_copy(right_hbm, right_ref, sems.at[0]),
        pltpu.make_async_copy(points_hbm, points_ref, sems.at[1]),
    ]
    for copy in copies:
        copy.start()
    copies[0].wait()
    right = right_ref[...]
    high = right.astype(BF16)
    out_ref[feats : feats + cols, :] = high
    out_ref[feats + cols : feats + 2 * cols, :] = (right - high.astype(F32)).astype(BF16)
    copies[1].wait()
    out_ref[0:feats, :] = points_ref[...]


def fan_kernel(length_ref, amplitude_ref, jitter_ref, *refs):
    *shards, out_ref, scalars_ref = refs
    for slot, scalar in enumerate((length_ref, amplitude_ref, jitter_ref)):
        scalars_ref[slot : slot + 1, :] = jnp.full((1, 128), scalar[0], F32)
    shards = [shard[...] for shard in shards]
    for peer in range(out_ref.shape[0]):
        for side, shard in enumerate(shards):
            out_ref[peer, side] = shard


def source_of(block_ref, core_ref, paired, steps, part, step, side):
    if not paired:
        return step * 2 + side
    core = core_ref[0] if part == 0 else 1 - core_ref[0]
    first = jnp.where((block_ref[0] < steps) == (side == 0), 0, steps)
    return (first + step) * 2 + core


def joined(sums):
    return functools.reduce(jnp.add, [functools.reduce(jnp.add, sides) for sides in sums])


class Distances:
    def __init__(self, scalars_ref, points_ref):
        scale = scalars_ref[0:1, :]
        self.scale = scale
        self.factor = (5.0 * LOG2E * LOG2E) / (scale * scale)
        own = points_ref.shape[1]
        points = points_ref[...].astype(F32).T
        squares = jnp.sum(points * points, axis=1, keepdims=True) * self.factor
        self.squares = jnp.broadcast_to(squares, (own, own))
        self.points = (-2.0 * points).astype(BF16)

    def __call__(self, points):
        wide = points.astype(F32)
        squares = jnp.sum(wide * wide, axis=0, keepdims=True) * self.factor
        inner = jnp.dot(self.points, points, preferred_element_type=F32)
        reduced = jnp.maximum((self.squares + squares) + inner * self.factor, TINY)
        return reduced, reduced * lax.rsqrt(reduced)


def kern_tile(reduced, root):
    shifted = root + 1.5 * LOG2E
    return (shifted * shifted + 0.75 * LOG2E * LOG2E) * jnp.exp2(-math.log2(3.0 * LOG2E * LOG2E) - root)


def kern_kernel(has_before, scalars_ref, points_ref, part_ref, *refs):
    before = refs[0][...] if has_before else None
    tiles_ref, *outs = refs[1 if has_before else 0 :]
    feats, own = points_ref.shape
    total_ref = outs[0]
    cols = total_ref.shape[0]
    distances = Distances(scalars_ref, points_ref)
    steps, sides = part_ref.shape[:2]
    total = before if has_before else jnp.zeros((cols, own), F32)

    def one_pair(step, total):
        vectors = []
        for side in range(sides):
            tile = kern_tile(*distances(part_ref[step, side, 0:feats, :]))
            tiles_ref[step, :, pl.ds(side * own, own)] = tile.astype(BF16)
            vectors.append(part_ref[step, side, feats : feats + cols, :])
        vectors = jnp.concatenate(vectors, axis=1)
        return total + lax.dot_general(vectors, tiles_ref[step], NT, preferred_element_type=F32)

    total = lax.fori_loop(0, steps, one_pair, total, unroll=unrolled(steps, 8))
    total_ref[...] = total
    if len(outs) > 1:
        message_ref = outs[1]
        rows = message_ref.shape[1]
        for peer in range(message_ref.shape[0]):
            first = (peer * rows) % cols
            message_ref[peer] = total[first : first + rows]


def dkern_kernel(has_before, scalars_ref, points_ref, part_ref, *refs):
    before = refs[0][...] if has_before else None
    tiles_ref, wide_ref, total_ref, norm_ref = refs[1 if has_before else 0 :]
    feats, own = points_ref.shape
    cols = total_ref.shape[0]
    distances = Distances(scalars_ref, points_ref)
    slope = 1.0 / (3.0 * LOG2E * LOG2E * LOG2E * distances.scale)
    steps, sides = part_ref.shape[:2]
    zero = jnp.zeros((cols, own), F32)

    def one_pair(step, carried):
        total, norm = carried
        norm = list(norm)
        vectors = []
        for side in range(sides):
            reduced, root = distances(part_ref[step, side, 0:feats, :])
            tile = (reduced * slope) * ((root + LOG2E) * jnp.exp2(-root))
            tiles_ref[step, :, pl.ds(side * own, own)] = tile.astype(BF16)
            high = part_ref[step, side, feats : feats + cols, :]
            low = part_ref[step, side, feats + cols : feats + 2 * cols, :]
            right = high.astype(F32) + low.astype(F32)
            wide_ref[step, side] = right
            norm[side] = norm[side] + right * right
            vectors.append(high)
        vectors = jnp.concatenate(vectors, axis=1)
        total = total + lax.dot_general(vectors, tiles_ref[step], NT, preferred_element_type=F32)
        return total, tuple(norm)

    start = (before if has_before else zero, (zero,) * sides)
    total, norm = lax.fori_loop(0, steps, one_pair, start, unroll=unrolled(steps, 8))
    total_ref[...] = total
    norm_ref[...] = jnp.broadcast_to(lane_sum(functools.reduce(jnp.add, norm)), norm_ref.shape)


def from_lanes(row, first, cols):
    lanes = lax.broadcasted_iota(jnp.int32, (cols, 128), 1)
    rows = lax.broadcasted_iota(jnp.int32, (cols, 128), 0)
    picked = jnp.where(lanes == rows + first, jnp.broadcast_to(row, (cols, 128)), 0.0)
    return lane_sum(picked)


def into_columns(columns, cols):
    lanes = lax.broadcasted_iota(jnp.int32, (cols, 128), 1)
    kept = jnp.zeros((cols, 128), F32)
    for slot, column in enumerate(columns):
        kept = jnp.where(lanes == slot, jnp.broadcast_to(column, (cols, 128)), kept)
    return kept


def second_kernel(
    part_count, paired, block_ref, core_ref, scalars_ref, right_ref, kernel_ref, slope_ref,
    *refs
):
    kerns, dkerns, wides, norms, received, outs = [
        refs[group * part_count : (group + 1) * part_count] for group in range(5)
    ] + [refs[5 * part_count :]]
    (
        message_ref, direction_ref, residual_ref, applied_ref, columns_ref, products_ref, turned_ref,
    ) = outs
    cols, own = right_ref.shape
    sides = wides[0].shape[1]
    amplitude = scalars_ref[1:2, :]
    jitter = scalars_ref[2:3, :]
    low_core = core_ref[0] == 0
    zero = jnp.zeros((cols, own), F32)
    norm = functools.reduce(jnp.add, [norm_ref[:, 0:1] for norm_ref in norms])
    steps = kerns[0].shape[0]

    sums = []
    for part in range(part_count):
        def first_pass(index, carried, part=part):
            carried = [list(sums) for sums in carried]
            for side in range(sides):
                source = source_of(block_ref, core_ref, paired, steps, part, index, side)
                product = received[0][source]
                if paired:
                    other = received[1][source]
                    product = jnp.concatenate(
                        [jnp.where(low_core, product, other), jnp.where(low_core, other, product)],
                        axis=0,
                    )
                products_ref[part * steps + index, side] = product
                right = wides[part][index, side]
                applied = amplitude * product + jitter * right
                carried[0][side] = carried[0][side] + right * applied
                carried[1][side] = carried[1][side] + applied * applied
            return tuple(tuple(sums) for sums in carried)

        sums.append(
            lax.fori_loop(0, steps, first_pass, ((zero,) * sides,) * 2, unroll=unrolled(steps, 4))
        )
    curvature, length = [lane_sum(joined(parts)) for parts in zip(*sums)]
    step = norm / curvature
    turn = (step * step * length - norm) / norm

    sums = []
    total = zero
    slopes = zero
    for part in range(part_count):
        def second_pass(index, carried, part=part):
            total, slopes, lengths = carried
            lengths = list(lengths)
            rounded = []
            for side in range(sides):
                right = wides[part][index, side]
                product = products_ref[part * steps + index, side]
                residual = right - step * (amplitude * product + jitter * right)
                direction = residual + turn * right
                turned_ref[part * steps + index, side] = direction
                lengths[side] = lengths[side] + residual * residual
                rounded.append(direction)
            rounded = jnp.concatenate(rounded, axis=1).astype(BF16)
            total = total + lax.dot_general(
                rounded, kerns[part][index], NT, preferred_element_type=F32
            )
            slopes = slopes + lax.dot_general(
                rounded, dkerns[part][index], NT, preferred_element_type=F32
            )
            return total, slopes, tuple(lengths)

        total, slopes, lengths = lax.fori_loop(
            0, steps, second_pass, (total, slopes, (zero,) * sides), unroll=unrolled(steps, 8)
        )
        sums.append(lengths)
    norm_next = lane_sum(joined(sums))

    right = right_ref[...]
    residual = right - step * (amplitude * kernel_ref[...] + jitter * right)
    direction = residual + turn * right
    applied = amplitude * total + jitter * direction
    direction_ref[...] = direction
    residual_ref[...] = residual
    applied_ref[...] = applied
    columns_ref[...] = into_columns([step, norm_next, norm, turn], cols)

    low = right - right.astype(BF16).astype(F32)
    low_direction = direction - direction.astype(BF16).astype(F32)
    slope = slope_ref[...]
    lanes = lax.broadcasted_iota(jnp.int32, (cols, 128), 1)
    rows = lax.broadcasted_iota(jnp.int32, (cols, 128), 0)
    packed = jnp.zeros((cols, 128), F32)
    for slot, values in enumerate([
        direction * applied, low * total, low * kernel_ref[...], right * slope, right * slopes,
    ]):
        packed = jnp.where(lanes == rows + slot * cols, lane_sum(values), packed)
    rows = jnp.where(rows == 0, 5 * cols, 128)
    for slot, values in enumerate([
        direction * slope, direction * slopes, low_direction * kernel_ref[...], low_direction * total,
    ]):
        packed = jnp.where(lanes == rows + slot, lane_sum(values), packed)
    packed = jnp.sum(packed, axis=0, keepdims=True)
    for peer in range(message_ref.shape[0]):
        message_ref[peer, 0:1, :] = packed
        message_ref[peer, 1:2, :] = total[0:1, :]


def last_kernel(
    part_count, paired, points_total, block_ref, core_ref, scalars_ref, right_ref, direction_ref,
    residual_ref, applied_ref, columns_ref, products_ref, turned_ref, received_ref, *refs
):
    wides = refs[:part_count]
    solution_hbm, final_hbm, gradient_ref, solution_ref, final_ref, sems = refs[part_count:]
    cols, own = right_ref.shape
    amplitude = scalars_ref[1:2, 0:1]
    devices = received_ref.shape[0]

    def gather_sums(device, carried):
        return carried + received_ref[device, 0:1, :]

    sums = lax.fori_loop(
        0, devices, gather_sums, jnp.zeros((1, 128), F32), unroll=unrolled(devices, 32)
    )
    step, norm_next, norm = [columns_ref[:, slot : slot + 1] for slot in range(3)]
    step_next = norm_next / from_lanes(sums, 0, cols)

    solution_ref[...] = step * right_ref[...] + step_next * direction_ref[...]
    final_ref[...] = residual_ref[...] - step_next * applied_ref[...]
    copies = [
        pltpu.make_async_copy(solution_ref, solution_hbm, sems.at[0]),
        pltpu.make_async_copy(final_ref, final_hbm, sems.at[1]),
    ]
    for copy in copies:
        copy.start()

    low_next, low_first, right_slope, right_slope_next = [
        from_lanes(sums, slot * cols, cols) for slot in range(1, 5)
    ]
    slope_cross, slope_square, low_second, low_square = [
        sums[:, 5 * cols + slot : 5 * cols + slot + 1] for slot in range(4)
    ]
    turn = columns_ref[:, 3:4]
    dots = turn * norm
    squares = norm_next + turn * dots
    steps, sides = wides[0].shape[:2]
    zero = jnp.zeros((cols, own), F32)
    row_zero = jnp.zeros((1, own), F32)
    sums = []
    for part in range(part_count):
        def one_pair(index, carried, part=part):
            carried = [list(sums) for sums in carried]
            block = part * steps + index
            for side in range(sides):
                vector = step * wides[part][index, side] + step_next * turned_ref[block, side]
                rounded = vector.astype(BF16).astype(F32)
                source = source_of(block_ref, core_ref, paired, steps, part, index, side)
                carried[0][side] = carried[0][side] + products_ref[block, side] * rounded
                carried[1][side] = carried[1][side] + received_ref[source, 1:2, :] * rounded[0:1, :]
            return tuple(tuple(sums) for sums in carried)

        start = ((zero,) * sides, (row_zero,) * sides)
        sums.append(lax.fori_loop(0, steps, one_pair, start, unroll=unrolled(steps, 4)))
    whole, first_row = [joined(parts) for parts in zip(*sums)]
    right_kernel = lane_sum(whole) + step * low_first + step_next * low_next
    first_step, second_step = step[0:1], step_next[0:1]
    direction_kernel = lane_sum(first_row) + first_step * low_second + second_step * low_square
    direction_slope = first_step * slope_cross + second_step * slope_square
    is_first = lax.broadcasted_iota(jnp.int32, (cols, 1), 0) == 0
    weight = jnp.where(is_first, 1.0, -1.0 / (cols - 1))
    for slot, (right_form, direction_form) in enumerate((
        (
            amplitude * (step * right_slope + step_next * right_slope_next),
            amplitude * direction_slope,
        ),
        (right_kernel, direction_kernel),
        (step * norm + step_next * dots, (step * dots + step_next * squares)[0:1]),
    )):
        form = jnp.where(is_first, step * right_form + step_next * direction_form, right_form)
        gradient_ref[slot] = jnp.sum(weight * form) * (0.5 / points_total)
    for copy in copies:
        copy.wait()


SWAP = [(0, 1), (1, 0)]


def local(mesh_shape, points, right_side, lengthscale, outputscale, noise_level):
    axes = ("blk", "grp")
    feats, own = points.shape
    cols = right_side.shape[0]
    rows = feats + 2 * cols
    blocks = mesh_shape["blk"]
    devices = blocks * mesh_shape["grp"]
    paired = mesh_shape["grp"] == 2 and blocks % 2 == 0
    part_count = 2 if paired else 1
    steps = devices // (2 * part_count)
    params = pltpu.CompilerParams(vmem_limit_bytes=(4 << 20) + devices * (40 << 10))
    shape = pltpu.VMEM
    result = jax.ShapeDtypeStruct

    def near(*arrays):
        return [pltpu.with_memory_space_constraint(array, pltpu.VMEM) for array in arrays]

    call = functools.partial(pl.pallas_call, compiler_params=params)
    place = [lax.axis_index(axis).astype(jnp.int32)[None] for axis in axes]

    row_shape = shape((cols, own), F32)
    shard, own_points, own_right = call(
        pack_kernel,
        out_shape=(shape((rows, own), BF16), shape((feats, own), BF16), row_shape),
        in_specs=_hbm(2),
        out_specs=tuple(_vmem(3)),
        scratch_shapes=[pltpu.SemaphoreType.DMA((2,))],
        name="pack",
    )(*[pltpu.with_memory_space_constraint(array, pltpu.HBM) for array in (points, right_side)])
    shards = [shard]
    if paired:
        half = blocks // 2
        shards.append(lax.ppermute(shard, "blk", [(at, (at + half) % blocks) for at in range(blocks)]))
    peers = blocks // 2 if paired else devices
    message, scalars = call(
        fan_kernel,
        out_shape=(shape((peers, len(shards), rows, own), BF16), shape((8, 128), F32)),
        in_specs=[_smem()] * 3 + _vmem(len(shards)),
        out_specs=tuple(_vmem(2)),
        name="fan",
    )(lengthscale, outputscale, noise_level, *near(*shards))
    if paired:
        groups = [
            [2 * (side * half + at) + core for at in range(half)] for side in range(2) for core in range(2)
        ]
        vectors = [lax.all_to_all(message, axes, 0, 0, tiled=True, axis_index_groups=groups)]
        vectors.append(lax.ppermute(vectors[0], "grp", SWAP))
    else:
        vectors = [lax.all_to_all(message, axes, 0, 0, tiled=True).reshape(steps, 2, rows, own)]

    tile_shape = shape((steps, own, 2 * own), BF16)
    wide_shape = shape((steps, 2, cols, own), F32)

    def kern_call(part, vector, *before):
        outs = [tile_shape, row_shape]
        if part + 1 == part_count:
            outs.append(shape((devices, cols // part_count, own), F32))
        return call(
            functools.partial(kern_kernel, part > 0),
            out_shape=tuple(outs),
            in_specs=_vmem(3 + len(before)),
            out_specs=tuple(_vmem(len(outs))),
            name="kern",
        )(*near(scalars, own_points, vector, *before))

    def dkern_call(vector, *before):
        return call(
            functools.partial(dkern_kernel, len(before) > 0),
            out_shape=(tile_shape, wide_shape, row_shape, row_shape),
            in_specs=_vmem(3 + len(before)),
            out_specs=tuple(_vmem(4)),
            name="dkern",
        )(*near(scalars, own_points, vector, *before))

    kerns = [kern_call(0, vectors[0])]
    dkerns = []
    if paired:
        dkerns.append(dkern_call(vectors[0]))
        vectors[1], *dkerns[0] = lax.optimization_barrier((vectors[1], *dkerns[0]))
        kerns.append(kern_call(1, vectors[1], kerns[0][1]))
    kernel_first, message = kerns[-1][1:]
    received = [lax.all_to_all(message, axes, 0, 0, tiled=True)]
    if paired:
        received[0], vectors[1] = lax.optimization_barrier((received[0], vectors[1]))
        received.append(lax.ppermute(received[0], "grp", SWAP))
        dkerns.append(dkern_call(vectors[1], dkerns[0][2]))
    else:
        dkerns.append(dkern_call(vectors[0]))
    kerns = [tiles for tiles, *rest in kerns]
    slope_first = dkerns[-1][2]
    dkerns, wides, norms = [[outs[slot] for outs in dkerns] for slot in (0, 1, 3)]

    both_shape = shape((devices // 2, 2, cols, own), F32)
    message, direction, residual, applied, columns, products, turned = call(
        functools.partial(second_kernel, part_count, paired),
        out_shape=(
            shape((devices, 2, own), F32), row_shape, row_shape, row_shape, shape((cols, 128), F32),
            both_shape, both_shape,
        ),
        in_specs=[_smem()] * 2 + _vmem(4 + 5 * part_count),
        out_specs=tuple(_vmem(7)),
        name="second",
    )(
        *place,
        *near(scalars, own_right, kernel_first, slope_first, *kerns, *dkerns, *wides, *norms, *received),
    )
    received = lax.all_to_all(message, axes, 0, 0, tiled=True)

    solution, final, gradient = call(
        functools.partial(last_kernel, part_count, paired, float(own * devices)),
        out_shape=(result((cols, own), F32), result((cols, own), F32), result((3,), F32)),
        in_specs=[_smem()] * 2 + _vmem(9 + part_count),
        out_specs=tuple(_hbm(2) + [_smem()]),
        scratch_shapes=[
            pltpu.VMEM((cols, own), F32),
            pltpu.VMEM((cols, own), F32),
            pltpu.SemaphoreType.DMA((2,)),
        ],
        name="last",
    )(
        *place,
        *near(scalars, own_right, direction, residual, applied, columns, products, turned, received, *wides),
    )
    return solution, final, gradient


def solution(mesh):
    whole = P(None, ("blk", "grp"))
    return jax.shard_map(
        functools.partial(local, dict(mesh.shape)),
        mesh=mesh,
        in_specs=(whole, whole, P(), P(), P()),
        out_specs=(whole, whole, P()),
        check_vma=False,
    )
```

```python
import functools
import math

import jax
import jax.numpy as jnp
from jax import lax
from jax.experimental import pallas as pl
from jax.experimental.pallas import tpu as pltpu
from jax.sharding import PartitionSpec as P

F32 = jnp.float32
BF16 = jnp.bfloat16
LOG2E = math.log2(math.e)
TINY = 1e-36
NT = (((1,), (1,)), ((), ()))


def _vmem(count):
    return [pl.BlockSpec(memory_space=pltpu.VMEM) for _ in range(count)]


def _smem():
    return pl.BlockSpec(memory_space=pltpu.SMEM)


def _hbm(count):
    return [pl.BlockSpec(memory_space=pltpu.HBM) for _ in range(count)]


def lane_sum(values):
    return jnp.sum(values, axis=1, keepdims=True)


def unrolled(count, most):
    return max(divisor for divisor in range(1, most + 1) if count % divisor == 0)


def pack_kernel(points_hbm, right_hbm, out_ref, points_ref, right_ref, sems):
    feats = points_ref.shape[0]
    cols = right_ref.shape[0]
    copies = [
        pltpu.make_async_copy(right_hbm, right_ref, sems.at[0]),
        pltpu.make_async_copy(points_hbm, points_ref, sems.at[1]),
    ]
    for copy in copies:
        copy.start()
    copies[0].wait()
    right = right_ref[...]
    high = right.astype(BF16)
    out_ref[feats : feats + cols, :] = high
    out_ref[feats + cols : feats + 2 * cols, :] = (right - high.astype(F32)).astype(BF16)
    copies[1].wait()
    out_ref[0:feats, :] = points_ref[...]


def fan_kernel(length_ref, amplitude_ref, jitter_ref, *refs):
    *shards, out_ref, scalars_ref = refs
    for slot, scalar in enumerate((length_ref, amplitude_ref, jitter_ref)):
        scalars_ref[slot : slot + 1, :] = jnp.full((1, 128), scalar[0], F32)
    shards = [shard[...] for shard in shards]
    for peer in range(out_ref.shape[0]):
        for side, shard in enumerate(shards):
            out_ref[peer, side] = shard


def source_of(block_ref, core_ref, paired, steps, part, step, side):
    if not paired:
        return step * 2 + side
    core = core_ref[0] if part == 0 else 1 - core_ref[0]
    first = jnp.where((block_ref[0] < steps) == (side == 0), 0, steps)
    return (first + (step ^ (step >> 1))) * 2 + core


def joined(sums):
    return functools.reduce(jnp.add, [functools.reduce(jnp.add, sides) for sides in sums])


def own_operand(points_ref, scale):
    own = points_ref.shape[1]
    points = points_ref[...].astype(F32).T
    squares = jnp.sum(points * points, axis=1, keepdims=True) * ((5.0 * LOG2E * LOG2E) / (scale * scale))
    return (-2.0 * points).astype(BF16), jnp.broadcast_to(squares, (own, own))


class Distances:
    def __init__(self, scale, points, squares):
        self.scale = scale
        self.factor = (5.0 * LOG2E * LOG2E) / (scale * scale)
        self.points = points
        self.squares = squares

    def __call__(self, points):
        wide = points.astype(F32)
        squares = jnp.sum(wide * wide, axis=0, keepdims=True) * self.factor
        inner = jnp.dot(self.points, points, preferred_element_type=F32)
        reduced = jnp.maximum((self.squares + squares) + inner * self.factor, TINY)
        return reduced, reduced * lax.rsqrt(reduced)


def kern_tile(reduced, root):
    shifted = root + 1.5 * LOG2E
    return (shifted * shifted + 0.75 * LOG2E * LOG2E) * jnp.exp2(-math.log2(3.0 * LOG2E * LOG2E) - root)


def kern_kernel(has_before, with_message, scalars_ref, points_ref, *refs):
    scale = scalars_ref[0:1, :]
    refs = list(refs)
    squares_ref = refs.pop(0) if has_before else None
    part_ref = refs.pop(0)
    before = refs.pop(0)[...] if has_before else None
    right_ref = refs.pop(0) if with_message else None
    if has_before:
        distances = Distances(scale, points_ref[...], squares_ref[...])
    else:
        operand_ref, squares_ref = refs.pop(0), refs.pop(0)
        operand, squares = own_operand(points_ref, scale)
        operand_ref[...] = operand
        squares_ref[...] = squares
        distances = Distances(scale, operand, squares)
    tiles_ref, *outs = refs
    total_ref = outs[0]
    cols, own = total_ref.shape
    feats = part_ref.shape[2] - 2 * cols
    steps, sides = part_ref.shape[:2]
    total = before if has_before else jnp.zeros((cols, own), F32)

    def one_pair(step, total):
        vectors = []
        for side in range(sides):
            tile = kern_tile(*distances(part_ref[step, side, 0:feats, :]))
            tiles_ref[step, :, pl.ds(side * own, own)] = tile.astype(BF16)
            vectors.append(part_ref[step, side, feats : feats + cols, :])
        vectors = jnp.concatenate(vectors, axis=1)
        return total + lax.dot_general(vectors, tiles_ref[step], NT, preferred_element_type=F32)

    total = lax.fori_loop(0, steps, one_pair, total, unroll=unrolled(steps, 8))
    total_ref[...] = total
    if with_message:
        right = right_ref[...]
        high = right.astype(BF16).astype(F32)
        low = (right - high).astype(BF16).astype(F32)
        lost = ((right - high) - low) / jnp.where(right == 0.0, 1.0, right)
        product = total - total * lost
        message_ref = outs[1]
        rows = message_ref.shape[1]
        for peer in range(message_ref.shape[0]):
            first = (peer * rows) % cols
            message_ref[peer] = product[first : first + rows]


def dkern_kernel(has_before, scalars_ref, operand_ref, squares_ref, part_ref, *refs):
    before = refs[0][...] if has_before else None
    tiles_ref, wide_ref, total_ref, norm_ref = refs[1 if has_before else 0 :]
    cols, own = total_ref.shape
    feats = part_ref.shape[2] - 2 * cols
    distances = Distances(scalars_ref[0:1, :], operand_ref[...], squares_ref[...])
    slope = 1.0 / (3.0 * LOG2E * LOG2E * LOG2E * distances.scale)
    steps, sides = part_ref.shape[:2]
    zero = jnp.zeros((cols, own), F32)

    def one_pair(step, carried):
        total, norm = carried
        norm = list(norm)
        vectors = []
        for side in range(sides):
            reduced, root = distances(part_ref[step, side, 0:feats, :])
            tile = (reduced * slope) * ((root + LOG2E) * jnp.exp2(-root))
            tiles_ref[step, :, pl.ds(side * own, own)] = tile.astype(BF16)
            high = part_ref[step, side, feats : feats + cols, :]
            low = part_ref[step, side, feats + cols : feats + 2 * cols, :]
            right = high.astype(F32) + low.astype(F32)
            wide_ref[step, side] = right
            norm[side] = norm[side] + right * right
            vectors.append(high)
        vectors = jnp.concatenate(vectors, axis=1)
        total = total + lax.dot_general(vectors, tiles_ref[step], NT, preferred_element_type=F32)
        return total, tuple(norm)

    start = (before if has_before else zero, (zero,) * sides)
    total, norm = lax.fori_loop(0, steps, one_pair, start, unroll=unrolled(steps, 8))
    total_ref[...] = total
    norm_ref[...] = jnp.broadcast_to(lane_sum(functools.reduce(jnp.add, norm)), norm_ref.shape)


def from_lanes(row, first, cols):
    lanes = lax.broadcasted_iota(jnp.int32, (cols, 128), 1)
    rows = lax.broadcasted_iota(jnp.int32, (cols, 128), 0)
    picked = jnp.where(lanes == rows + first, jnp.broadcast_to(row, (cols, 128)), 0.0)
    return lane_sum(picked)


def into_columns(columns, cols):
    lanes = lax.broadcasted_iota(jnp.int32, (cols, 128), 1)
    kept = jnp.zeros((cols, 128), F32)
    for slot, column in enumerate(columns):
        kept = jnp.where(lanes == slot, jnp.broadcast_to(column, (cols, 128)), kept)
    return kept


def second_kernel(
    part_count, paired, block_ref, core_ref, scalars_ref, right_ref, kernel_ref, slope_ref,
    *refs
):
    kerns, dkerns, wides, norms, received, outs = [
        refs[group * part_count : (group + 1) * part_count] for group in range(5)
    ] + [refs[5 * part_count :]]
    (
        message_ref, direction_ref, residual_ref, applied_ref, columns_ref, products_ref, turned_ref,
    ) = outs
    cols, own = right_ref.shape
    sides = wides[0].shape[1]
    amplitude = scalars_ref[1:2, :]
    jitter = scalars_ref[2:3, :]
    low_core = core_ref[0] == 0
    zero = jnp.zeros((cols, own), F32)
    norm = functools.reduce(jnp.add, [norm_ref[:, 0:1] for norm_ref in norms])
    steps = kerns[0].shape[0]

    sums = []
    for part in range(part_count):
        def first_pass(index, carried, part=part):
            carried = [list(sums) for sums in carried]
            for side in range(sides):
                source = source_of(block_ref, core_ref, paired, steps, part, index, side)
                product = received[0][source]
                if paired:
                    other = received[1][source]
                    product = jnp.concatenate(
                        [jnp.where(low_core, product, other), jnp.where(low_core, other, product)],
                        axis=0,
                    )
                products_ref[part * steps + index, side] = product
                right = wides[part][index, side]
                applied = amplitude * product + jitter * right
                carried[0][side] = carried[0][side] + right * applied
                carried[1][side] = carried[1][side] + applied * applied
            return tuple(tuple(sums) for sums in carried)

        sums.append(
            lax.fori_loop(0, steps, first_pass, ((zero,) * sides,) * 2, unroll=unrolled(steps, 8))
        )
    curvature, length = [lane_sum(joined(parts)) for parts in zip(*sums)]
    step = norm / curvature
    turn = (step * step * length - norm) / norm
    right_factor = jnp.broadcast_to(1.0 - step * jitter, (cols, own))
    product_factor = jnp.broadcast_to(step * amplitude, (cols, own))

    sums = []
    total = zero
    slopes = zero
    for part in range(part_count):
        def second_pass(index, carried, part=part):
            total, slopes, lengths = carried
            lengths = list(lengths)
            rounded = []
            for side in range(sides):
                right = wides[part][index, side]
                product = products_ref[part * steps + index, side]
                residual = right * right_factor - product * product_factor
                direction = residual + turn * right
                turned_ref[part * steps + index, side] = direction
                lengths[side] = lengths[side] + residual * residual
                rounded.append(direction)
            rounded = jnp.concatenate(rounded, axis=1).astype(BF16)
            total = total + lax.dot_general(
                rounded, kerns[part][index], NT, preferred_element_type=F32
            )
            slopes = slopes + lax.dot_general(
                rounded, dkerns[part][index], NT, preferred_element_type=F32
            )
            return total, slopes, tuple(lengths)

        total, slopes, lengths = lax.fori_loop(
            0, steps, second_pass, (total, slopes, (zero,) * sides), unroll=unrolled(steps, 8)
        )
        sums.append(lengths)
    norm_next = lane_sum(joined(sums))

    right = right_ref[...]
    residual = right * right_factor - kernel_ref[...] * product_factor
    direction = residual + turn * right
    applied = amplitude * total + jitter * direction
    direction_ref[...] = direction
    residual_ref[...] = residual
    applied_ref[...] = applied
    columns_ref[...] = into_columns([step, norm_next, norm, turn], cols)

    low = right - right.astype(BF16).astype(F32)
    low_direction = direction - direction.astype(BF16).astype(F32)
    slope = slope_ref[...]
    lanes = lax.broadcasted_iota(jnp.int32, (cols, 128), 1)
    rows = lax.broadcasted_iota(jnp.int32, (cols, 128), 0)
    packed = jnp.zeros((cols, 128), F32)
    for slot, values in enumerate([
        direction * applied, low * total, low * kernel_ref[...], right * slope, right * slopes,
    ]):
        packed = jnp.where(lanes == rows + slot * cols, lane_sum(values), packed)
    rows = jnp.where(rows == 0, 5 * cols, 128)
    for slot, values in enumerate([
        direction * slope, direction * slopes, low_direction * kernel_ref[...], low_direction * total,
    ]):
        packed = jnp.where(lanes == rows + slot, lane_sum(values), packed)
    packed = jnp.sum(packed, axis=0, keepdims=True)
    for peer in range(message_ref.shape[0]):
        message_ref[peer, 0:1, :] = packed
        message_ref[peer, 1:2, :] = total[0:1, :]


def last_kernel(
    part_count, paired, points_total, block_ref, core_ref, scalars_ref, right_ref, direction_ref,
    residual_ref, applied_ref, columns_ref, products_ref, turned_ref, received_ref, *refs
):
    wides = refs[:part_count]
    solution_hbm, final_hbm, gradient_ref, solution_ref, final_ref, sems = refs[part_count:]
    cols, own = right_ref.shape
    amplitude = scalars_ref[1:2, 0:1]
    devices = received_ref.shape[0]

    def gather_sums(device, carried):
        return carried + received_ref[device, 0:1, :]

    sums = lax.fori_loop(
        0, devices, gather_sums, jnp.zeros((1, 128), F32), unroll=unrolled(devices, 32)
    )
    step, norm_next, norm = [columns_ref[:, slot : slot + 1] for slot in range(3)]
    step_next = norm_next / from_lanes(sums, 0, cols)

    solution_ref[...] = step * right_ref[...] + step_next * direction_ref[...]
    final_ref[...] = residual_ref[...] - step_next * applied_ref[...]
    copies = [
        pltpu.make_async_copy(solution_ref, solution_hbm, sems.at[0]),
        pltpu.make_async_copy(final_ref, final_hbm, sems.at[1]),
    ]
    for copy in copies:
        copy.start()

    low_next, low_first, right_slope, right_slope_next = [
        from_lanes(sums, slot * cols, cols) for slot in range(1, 5)
    ]
    slope_cross, slope_square, low_second, low_square = [
        sums[:, 5 * cols + slot : 5 * cols + slot + 1] for slot in range(4)
    ]
    turn = columns_ref[:, 3:4]
    dots = turn * norm
    squares = norm_next + turn * dots
    steps, sides = wides[0].shape[:2]
    zero = jnp.zeros((cols, own), F32)
    row_zero = jnp.zeros((1, own), F32)
    sums = []
    for part in range(part_count):
        def one_pair(index, carried, part=part):
            carried = [list(sums) for sums in carried]
            block = part * steps + index
            for side in range(sides):
                vector = step * wides[part][index, side] + step_next * turned_ref[block, side]
                rounded = vector.astype(BF16).astype(F32)
                source = source_of(block_ref, core_ref, paired, steps, part, index, side)
                carried[0][side] = carried[0][side] + products_ref[block, side] * rounded
                carried[1][side] = carried[1][side] + received_ref[source, 1:2, :] * rounded[0:1, :]
            return tuple(tuple(sums) for sums in carried)

        start = ((zero,) * sides, (row_zero,) * sides)
        sums.append(lax.fori_loop(0, steps, one_pair, start, unroll=unrolled(steps, 4)))
    whole, first_row = [joined(parts) for parts in zip(*sums)]
    right_kernel = lane_sum(whole) + step * low_first + step_next * low_next
    first_step, second_step = step[0:1], step_next[0:1]
    direction_kernel = lane_sum(first_row) + first_step * low_second + second_step * low_square
    direction_slope = first_step * slope_cross + second_step * slope_square
    is_first = lax.broadcasted_iota(jnp.int32, (cols, 1), 0) == 0
    weight = jnp.where(is_first, 1.0, -1.0 / (cols - 1))
    for slot, (right_form, direction_form) in enumerate((
        (
            amplitude * (step * right_slope + step_next * right_slope_next),
            amplitude * direction_slope,
        ),
        (right_kernel, direction_kernel),
        (step * norm + step_next * dots, (step * dots + step_next * squares)[0:1]),
    )):
        form = jnp.where(is_first, step * right_form + step_next * direction_form, right_form)
        gradient_ref[slot] = jnp.sum(weight * form) * (0.5 / points_total)
    for copy in copies:
        copy.wait()


SWAP = [(0, 1), (1, 0)]


def local(mesh_shape, points, right_side, lengthscale, outputscale, noise_level):
    axes = ("blk", "grp")
    feats, own = points.shape
    cols = right_side.shape[0]
    rows = feats + 2 * cols
    blocks = mesh_shape["blk"]
    devices = blocks * mesh_shape["grp"]
    paired = mesh_shape["grp"] == 2 and blocks >= 2 and blocks & (blocks - 1) == 0
    part_count = 2 if paired else 1
    steps = devices // (2 * part_count)
    limit = (4 << 20) + devices * (40 << 10)
    params = pltpu.CompilerParams(vmem_limit_bytes=limit)
    shape = pltpu.VMEM
    result = jax.ShapeDtypeStruct

    def near(*arrays):
        return [pltpu.with_memory_space_constraint(array, pltpu.VMEM) for array in arrays]

    call = functools.partial(pl.pallas_call, compiler_params=params)
    place = [lax.axis_index(axis).astype(jnp.int32)[None] for axis in axes]

    row_shape = shape((cols, own), F32)
    shard, own_points, own_right = call(
        pack_kernel,
        out_shape=(shape((rows, own), BF16), shape((feats, own), BF16), row_shape),
        in_specs=_hbm(2),
        out_specs=tuple(_vmem(3)),
        scratch_shapes=[pltpu.SemaphoreType.DMA((2,))],
        name="pack",
    )(*[pltpu.with_memory_space_constraint(array, pltpu.HBM) for array in (points, right_side)])
    shards = [shard]
    if paired:
        half = blocks // 2
        shards.append(lax.ppermute(shard, "blk", [(at, (at + half) % blocks) for at in range(blocks)]))
    peers = blocks // 2 if paired else devices
    message, scalars = call(
        fan_kernel,
        out_shape=(shape((peers, len(shards), rows, own), BF16), shape((8, 128), F32)),
        in_specs=[_smem()] * 3 + _vmem(len(shards)),
        out_specs=tuple(_vmem(2)),
        name="fan",
    )(lengthscale, outputscale, noise_level, *near(*shards))
    if paired:
        groups = [
            [2 * (side * half + (at ^ (at >> 1))) + core for at in range(half)]
            for side in range(2)
            for core in range(2)
        ]
        vectors = [lax.all_to_all(message, axes, 0, 0, tiled=True, axis_index_groups=groups)]
        vectors.append(lax.ppermute(vectors[0], "grp", SWAP))
    else:
        vectors = [lax.all_to_all(message, axes, 0, 0, tiled=True).reshape(steps, 2, rows, own)]

    tile_shape = shape((steps, own, 2 * own), BF16)
    wide_shape = shape((steps, 2, cols, own), F32)

    operands = []

    def kern_call(part, vector, *before):
        outs = [tile_shape, row_shape]
        if part == 0:
            outs = [shape((own, feats), BF16), shape((own, own), F32)] + outs
        with_message = part + 1 == part_count
        if with_message:
            outs.append(shape((devices, cols // part_count, own), F32))
            before = (*before, own_right)
        results = call(
            functools.partial(kern_kernel, part > 0, with_message),
            out_shape=tuple(outs),
            in_specs=_vmem(2 + len(operands or [vector]) + len(before)),
            out_specs=tuple(_vmem(len(outs))),
            name="kern",
        )(*near(scalars, *(operands or [own_points]), vector, *before))
        if part == 0:
            operands.extend(results[:2])
            results = results[2:]
        return results

    def dkern_call(vector, *before):
        return call(
            functools.partial(dkern_kernel, len(before) > 0),
            out_shape=(tile_shape, wide_shape, row_shape, row_shape),
            in_specs=_vmem(4 + len(before)),
            out_specs=tuple(_vmem(4)),
            name="dkern",
        )(*near(scalars, *operands, vector, *before))

    kerns = [kern_call(0, vectors[0])]
    dkerns = []
    if paired:
        dkerns.append(dkern_call(vectors[0]))
        vectors[1], *dkerns[0] = lax.optimization_barrier((vectors[1], *dkerns[0]))
        kerns.append(kern_call(1, vectors[1], kerns[0][1]))
    kernel_first, message = kerns[-1][1:]
    received = [lax.all_to_all(message, axes, 0, 0, tiled=True)]
    if paired:
        received[0], vectors[1] = lax.optimization_barrier((received[0], vectors[1]))
        received.append(lax.ppermute(received[0], "grp", SWAP))
        dkerns.append(dkern_call(vectors[1], dkerns[0][2]))
    else:
        dkerns.append(dkern_call(vectors[0]))
    kerns = [tiles for tiles, *rest in kerns]
    slope_first = dkerns[-1][2]
    dkerns, wides, norms = [[outs[slot] for outs in dkerns] for slot in (0, 1, 3)]

    both_shape = shape((devices // 2, 2, cols, own), F32)
    message, direction, residual, applied, columns, products, turned = call(
        functools.partial(second_kernel, part_count, paired),
        out_shape=(
            shape((devices, 2, own), F32), row_shape, row_shape, row_shape, shape((cols, 128), F32),
            both_shape, both_shape,
        ),
        in_specs=[_smem()] * 2 + _vmem(4 + 5 * part_count),
        out_specs=tuple(_vmem(7)),
        name="second",
        compiler_params=pltpu.CompilerParams(
            vmem_limit_bytes=limit
        ),
    )(
        *place,
        *near(scalars, own_right, kernel_first, slope_first, *kerns, *dkerns, *wides, *norms, *received),
    )
    received = lax.all_to_all(message, axes, 0, 0, tiled=True)

    solution, final, gradient = call(
        functools.partial(last_kernel, part_count, paired, float(own * devices)),
        out_shape=(result((cols, own), F32), result((cols, own), F32), result((3,), F32)),
        in_specs=[_smem()] * 2 + _vmem(9 + part_count),
        out_specs=tuple(_hbm(2) + [_smem()]),
        scratch_shapes=[
            pltpu.VMEM((cols, own), F32),
            pltpu.VMEM((cols, own), F32),
            pltpu.SemaphoreType.DMA((2,)),
        ],
        name="last",
    )(
        *place,
        *near(scalars, own_right, direction, residual, applied, columns, products, turned, received, *wides),
    )
    return solution, final, gradient


def solution(mesh):
    whole = P(None, ("blk", "grp"))
    return jax.shard_map(
        functools.partial(local, dict(mesh.shape)),
        mesh=mesh,
        in_specs=(whole, whole, P(), P(), P()),
        out_specs=(whole, whole, P()),
        check_vma=False,
    )
```

```python
import functools
import math

import jax
import jax.numpy as jnp
from jax import lax
from jax.experimental import pallas as pl
from jax.experimental.pallas import tpu as pltpu
from jax.sharding import PartitionSpec as P

F32 = jnp.float32
BF16 = jnp.bfloat16
LOG2E = math.log2(math.e)
TINY = 1e-36
NT = (((1,), (1,)), ((), ()))


def _vmem(count):
    return [pl.BlockSpec(memory_space=pltpu.VMEM) for _ in range(count)]


def _smem():
    return pl.BlockSpec(memory_space=pltpu.SMEM)


def _hbm(count):
    return [pl.BlockSpec(memory_space=pltpu.HBM) for _ in range(count)]


def lane_sum(values):
    return jnp.sum(values, axis=1, keepdims=True)


def unrolled(count, most):
    return max(divisor for divisor in range(1, most + 1) if count % divisor == 0)


def pack_kernel(points_hbm, right_hbm, out_ref, points_ref, right_ref, sems):
    feats = points_ref.shape[0]
    cols = right_ref.shape[0]
    copies = [
        pltpu.make_async_copy(right_hbm, right_ref, sems.at[0]),
        pltpu.make_async_copy(points_hbm, points_ref, sems.at[1]),
    ]
    for copy in copies:
        copy.start()
    copies[0].wait()
    right = right_ref[...]
    high = right.astype(BF16)
    out_ref[feats : feats + cols, :] = high
    out_ref[feats + cols : feats + 2 * cols, :] = (right - high.astype(F32)).astype(BF16)
    copies[1].wait()
    out_ref[0:feats, :] = points_ref[...]


def fan_kernel(length_ref, amplitude_ref, jitter_ref, *refs):
    *shards, out_ref, scalars_ref = refs
    for slot, scalar in enumerate((length_ref, amplitude_ref, jitter_ref)):
        scalars_ref[slot : slot + 1, :] = jnp.full((1, 128), scalar[0], F32)
    shards = [shard[...] for shard in shards]
    for peer in range(out_ref.shape[0]):
        for side, shard in enumerate(shards):
            out_ref[peer, side] = shard


def own_place():
    return lax.axis_index("blk"), lax.axis_index("grp")


def source_of(place, paired, steps, part, step, side):
    if not paired:
        return step * 2 + side
    block, own_core = place
    core = own_core if part == 0 else 1 - own_core
    first = jnp.where((block < steps) == (side == 0), 0, steps)
    return (first + (step ^ (step >> 1))) * 2 + core


def joined(sums):
    return functools.reduce(jnp.add, [functools.reduce(jnp.add, sides) for sides in sums])


def own_operand(points_ref, scale):
    own = points_ref.shape[1]
    points = points_ref[...].astype(F32).T
    squares = jnp.sum(points * points, axis=1, keepdims=True) * ((5.0 * LOG2E * LOG2E) / (scale * scale))
    return (-2.0 * points).astype(BF16), jnp.broadcast_to(squares, (own, own))


class Distances:
    def __init__(self, scale, points, squares):
        self.scale = scale
        self.factor = (5.0 * LOG2E * LOG2E) / (scale * scale)
        self.points = points
        self.squares = squares

    def __call__(self, points):
        wide = points.astype(F32)
        squares = jnp.sum(wide * wide, axis=0, keepdims=True) * self.factor
        inner = jnp.dot(self.points, points, preferred_element_type=F32)
        reduced = jnp.maximum((self.squares + squares) + inner * self.factor, TINY)
        return reduced, reduced * lax.rsqrt(reduced)


def kern_tile(reduced, root):
    shifted = root + 1.5 * LOG2E
    return (shifted * shifted + 0.75 * LOG2E * LOG2E) * jnp.exp2(-math.log2(3.0 * LOG2E * LOG2E) - root)


def kern_kernel(has_before, with_message, scalars_ref, points_ref, *refs):
    scale = scalars_ref[0:1, :]
    refs = list(refs)
    squares_ref = refs.pop(0) if has_before else None
    part_ref = refs.pop(0)
    before = refs.pop(0)[...] if has_before else None
    right_ref = refs.pop(0) if with_message else None
    if has_before:
        distances = Distances(scale, points_ref[...], squares_ref[...])
    else:
        operand_ref, squares_ref = refs.pop(0), refs.pop(0)
        operand, squares = own_operand(points_ref, scale)
        operand_ref[...] = operand
        squares_ref[...] = squares
        distances = Distances(scale, operand, squares)
    tiles_ref, *outs = refs
    total_ref = outs[0]
    cols, own = total_ref.shape
    feats = part_ref.shape[2] - 2 * cols
    steps, sides = part_ref.shape[:2]
    total = before if has_before else jnp.zeros((cols, own), F32)

    def one_pair(step, total):
        vectors = []
        for side in range(sides):
            tile = kern_tile(*distances(part_ref[step, side, 0:feats, :]))
            tiles_ref[step, :, pl.ds(side * own, own)] = tile.astype(BF16)
            vectors.append(part_ref[step, side, feats : feats + cols, :])
        vectors = jnp.concatenate(vectors, axis=1)
        return total + lax.dot_general(vectors, tiles_ref[step], NT, preferred_element_type=F32)

    total = lax.fori_loop(0, steps, one_pair, total, unroll=unrolled(steps, 8))
    total_ref[...] = total
    if with_message:
        right = right_ref[...]
        high = right.astype(BF16).astype(F32)
        low = (right - high).astype(BF16).astype(F32)
        lost = ((right - high) - low) / jnp.where(right == 0.0, 1.0, right)
        product = total - total * lost
        message_ref = outs[1]
        rows = message_ref.shape[1]
        for peer in range(message_ref.shape[0]):
            first = (peer * rows) % cols
            message_ref[peer] = product[first : first + rows]


def dkern_kernel(has_before, scalars_ref, operand_ref, squares_ref, part_ref, *refs):
    before = refs[0][...] if has_before else None
    tiles_ref, wide_ref, total_ref, norm_ref = refs[1 if has_before else 0 :]
    cols, own = total_ref.shape
    feats = part_ref.shape[2] - 2 * cols
    distances = Distances(scalars_ref[0:1, :], operand_ref[...], squares_ref[...])
    slope = 1.0 / (3.0 * LOG2E * LOG2E * LOG2E * distances.scale)
    steps, sides = part_ref.shape[:2]
    zero = jnp.zeros((cols, own), F32)

    def one_pair(step, carried):
        total, norm = carried
        norm = list(norm)
        vectors = []
        for side in range(sides):
            reduced, root = distances(part_ref[step, side, 0:feats, :])
            tile = (reduced * slope) * ((root + LOG2E) * jnp.exp2(-root))
            tiles_ref[step, :, pl.ds(side * own, own)] = tile.astype(BF16)
            high = part_ref[step, side, feats : feats + cols, :]
            low = part_ref[step, side, feats + cols : feats + 2 * cols, :]
            right = high.astype(F32) + low.astype(F32)
            wide_ref[step, side] = right
            norm[side] = norm[side] + right * right
            vectors.append(high)
        vectors = jnp.concatenate(vectors, axis=1)
        total = total + lax.dot_general(vectors, tiles_ref[step], NT, preferred_element_type=F32)
        return total, tuple(norm)

    start = (before if has_before else zero, (zero,) * sides)
    total, norm = lax.fori_loop(0, steps, one_pair, start, unroll=unrolled(steps, 8))
    total_ref[...] = total
    norm_ref[...] = jnp.broadcast_to(lane_sum(functools.reduce(jnp.add, norm)), norm_ref.shape)


def from_lanes(row, first, cols):
    lanes = lax.broadcasted_iota(jnp.int32, (cols, 128), 1)
    rows = lax.broadcasted_iota(jnp.int32, (cols, 128), 0)
    picked = jnp.where(lanes == rows + first, jnp.broadcast_to(row, (cols, 128)), 0.0)
    return lane_sum(picked)


def into_columns(columns, cols):
    lanes = lax.broadcasted_iota(jnp.int32, (cols, 128), 1)
    kept = jnp.zeros((cols, 128), F32)
    for slot, column in enumerate(columns):
        kept = jnp.where(lanes == slot, jnp.broadcast_to(column, (cols, 128)), kept)
    return kept


def second_kernel(
    part_count, paired, scalars_ref, right_ref, kernel_ref, slope_ref,
    *refs
):
    kerns, dkerns, wides, norms, received, outs = [
        refs[group * part_count : (group + 1) * part_count] for group in range(5)
    ] + [refs[5 * part_count :]]
    (
        message_ref, direction_ref, residual_ref, applied_ref, columns_ref, products_ref, turned_ref,
    ) = outs
    cols, own = right_ref.shape
    sides = wides[0].shape[1]
    amplitude = scalars_ref[1:2, :]
    jitter = scalars_ref[2:3, :]
    place = own_place()
    low_core = place[1] == 0
    zero = jnp.zeros((cols, own), F32)
    norm = functools.reduce(jnp.add, [norm_ref[:, 0:1] for norm_ref in norms])
    steps = kerns[0].shape[0]

    sums = []
    for part in range(part_count):
        def first_pass(index, carried, part=part):
            carried = [list(sums) for sums in carried]
            for side in range(sides):
                source = source_of(place, paired, steps, part, index, side)
                product = received[0][source]
                if paired:
                    other = received[1][source]
                    product = jnp.concatenate(
                        [jnp.where(low_core, product, other), jnp.where(low_core, other, product)],
                        axis=0,
                    )
                products_ref[part * steps + index, side] = product
                right = wides[part][index, side]
                applied = amplitude * product + jitter * right
                carried[0][side] = carried[0][side] + right * applied
                carried[1][side] = carried[1][side] + applied * applied
            return tuple(tuple(sums) for sums in carried)

        sums.append(
            lax.fori_loop(0, steps, first_pass, ((zero,) * sides,) * 2, unroll=unrolled(steps, 8))
        )
    curvature, length = [lane_sum(joined(parts)) for parts in zip(*sums)]
    step = norm / curvature
    turn = (step * step * length - norm) / norm
    right_factor = jnp.broadcast_to(1.0 - step * jitter, (cols, own))
    product_factor = jnp.broadcast_to(step * amplitude, (cols, own))

    sums = []
    total = zero
    slopes = zero
    for part in range(part_count):
        def second_pass(index, carried, part=part):
            total, slopes, lengths = carried
            lengths = list(lengths)
            rounded = []
            for side in range(sides):
                right = wides[part][index, side]
                product = products_ref[part * steps + index, side]
                residual = right * right_factor - product * product_factor
                direction = residual + turn * right
                turned_ref[part * steps + index, side] = direction
                lengths[side] = lengths[side] + residual * residual
                rounded.append(direction)
            rounded = jnp.concatenate(rounded, axis=1).astype(BF16)
            total = total + lax.dot_general(
                rounded, kerns[part][index], NT, preferred_element_type=F32
            )
            slopes = slopes + lax.dot_general(
                rounded, dkerns[part][index], NT, preferred_element_type=F32
            )
            return total, slopes, tuple(lengths)

        total, slopes, lengths = lax.fori_loop(
            0, steps, second_pass, (total, slopes, (zero,) * sides), unroll=unrolled(steps, 8)
        )
        sums.append(lengths)
    norm_next = lane_sum(joined(sums))

    right = right_ref[...]
    residual = right * right_factor - kernel_ref[...] * product_factor
    direction = residual + turn * right
    applied = amplitude * total + jitter * direction
    direction_ref[...] = direction
    residual_ref[...] = residual
    applied_ref[...] = applied
    columns_ref[...] = into_columns([step, norm_next, norm, turn], cols)

    low = right - right.astype(BF16).astype(F32)
    low_direction = direction - direction.astype(BF16).astype(F32)
    slope = slope_ref[...]
    lanes = lax.broadcasted_iota(jnp.int32, (cols, 128), 1)
    rows = lax.broadcasted_iota(jnp.int32, (cols, 128), 0)
    packed = jnp.zeros((cols, 128), F32)
    for slot, values in enumerate([
        direction * applied, low * total, low * kernel_ref[...], right * slope, right * slopes,
    ]):
        packed = jnp.where(lanes == rows + slot * cols, lane_sum(values), packed)
    rows = jnp.where(rows == 0, 5 * cols, 128)
    for slot, values in enumerate([
        direction * slope, direction * slopes, low_direction * kernel_ref[...], low_direction * total,
    ]):
        packed = jnp.where(lanes == rows + slot, lane_sum(values), packed)
    packed = jnp.sum(packed, axis=0, keepdims=True)
    for peer in range(message_ref.shape[0]):
        message_ref[peer, 0:1, :] = packed
        message_ref[peer, 1:2, :] = total[0:1, :]


def last_kernel(
    part_count, paired, points_total, scalars_ref, right_ref, direction_ref,
    residual_ref, applied_ref, columns_ref, products_ref, turned_ref, received_ref, *refs
):
    wides = refs[:part_count]
    solution_hbm, final_hbm, gradient_hbm, solution_ref, final_ref, gradient_ref, sems = refs[part_count:]
    cols, own = right_ref.shape
    amplitude = scalars_ref[1:2, 0:1]
    place = own_place()
    devices = received_ref.shape[0]

    def gather_sums(device, carried):
        return carried + received_ref[device, 0:1, :]

    sums = lax.fori_loop(
        0, devices, gather_sums, jnp.zeros((1, 128), F32), unroll=unrolled(devices, 32)
    )
    step, norm_next, norm = [columns_ref[:, slot : slot + 1] for slot in range(3)]
    step_next = norm_next / from_lanes(sums, 0, cols)

    solution_ref[...] = step * right_ref[...] + step_next * direction_ref[...]
    final_ref[...] = residual_ref[...] - step_next * applied_ref[...]
    copies = [
        pltpu.make_async_copy(solution_ref, solution_hbm, sems.at[0]),
        pltpu.make_async_copy(final_ref, final_hbm, sems.at[1]),
    ]
    for copy in copies:
        copy.start()

    low_next, low_first, right_slope, right_slope_next = [
        from_lanes(sums, slot * cols, cols) for slot in range(1, 5)
    ]
    slope_cross, slope_square, low_second, low_square = [
        sums[:, 5 * cols + slot : 5 * cols + slot + 1] for slot in range(4)
    ]
    turn = columns_ref[:, 3:4]
    dots = turn * norm
    squares = norm_next + turn * dots
    steps, sides = wides[0].shape[:2]
    zero = jnp.zeros((cols, own), F32)
    row_zero = jnp.zeros((1, own), F32)
    sums = []
    for part in range(part_count):
        def one_pair(index, carried, part=part):
            carried = [list(sums) for sums in carried]
            block = part * steps + index
            for side in range(sides):
                vector = step * wides[part][index, side] + step_next * turned_ref[block, side]
                rounded = vector.astype(BF16).astype(F32)
                source = source_of(place, paired, steps, part, index, side)
                carried[0][side] = carried[0][side] + products_ref[block, side] * rounded
                carried[1][side] = carried[1][side] + received_ref[source, 1:2, :] * rounded[0:1, :]
            return tuple(tuple(sums) for sums in carried)

        start = ((zero,) * sides, (row_zero,) * sides)
        sums.append(lax.fori_loop(0, steps, one_pair, start, unroll=unrolled(steps, 4)))
    whole, first_row = [joined(parts) for parts in zip(*sums)]
    right_kernel = lane_sum(whole) + step * low_first + step_next * low_next
    first_step, second_step = step[0:1], step_next[0:1]
    direction_kernel = lane_sum(first_row) + first_step * low_second + second_step * low_square
    direction_slope = first_step * slope_cross + second_step * slope_square
    is_first = lax.broadcasted_iota(jnp.int32, (cols, 1), 0) == 0
    weight = jnp.where(is_first, 1.0, -1.0 / (cols - 1))
    for slot, (right_form, direction_form) in enumerate((
        (
            amplitude * (step * right_slope + step_next * right_slope_next),
            amplitude * direction_slope,
        ),
        (right_kernel, direction_kernel),
        (step * norm + step_next * dots, (step * dots + step_next * squares)[0:1]),
    )):
        form = jnp.where(is_first, step * right_form + step_next * direction_form, right_form)
        gradient_ref[slot] = jnp.sum(weight * form) * (0.5 / points_total)
    copies.append(pltpu.make_async_copy(gradient_ref, gradient_hbm, sems.at[2]))
    copies[2].start()
    for copy in copies:
        copy.wait()


SWAP = [(0, 1), (1, 0)]


def local(mesh_shape, points, right_side, lengthscale, outputscale, noise_level):
    axes = ("blk", "grp")
    feats, own = points.shape
    cols = right_side.shape[0]
    rows = feats + 2 * cols
    blocks = mesh_shape["blk"]
    devices = blocks * mesh_shape["grp"]
    paired = mesh_shape["grp"] == 2 and blocks >= 2 and blocks & (blocks - 1) == 0
    part_count = 2 if paired else 1
    steps = devices // (2 * part_count)
    limit = (4 << 20) + devices * (40 << 10)
    params = pltpu.CompilerParams(vmem_limit_bytes=limit)
    shape = pltpu.VMEM
    result = jax.ShapeDtypeStruct

    def near(*arrays):
        return [pltpu.with_memory_space_constraint(array, pltpu.VMEM) for array in arrays]

    call = functools.partial(pl.pallas_call, compiler_params=params)

    row_shape = shape((cols, own), F32)
    shard, own_points, own_right = call(
        pack_kernel,
        out_shape=(shape((rows, own), BF16), shape((feats, own), BF16), row_shape),
        in_specs=_hbm(2),
        out_specs=tuple(_vmem(3)),
        scratch_shapes=[pltpu.SemaphoreType.DMA((2,))],
        name="pack",
    )(*[pltpu.with_memory_space_constraint(array, pltpu.HBM) for array in (points, right_side)])
    shards = [shard]
    if paired:
        half = blocks // 2
        shards.append(lax.ppermute(shard, "blk", [(at, (at + half) % blocks) for at in range(blocks)]))
    peers = blocks // 2 if paired else devices
    message, scalars = call(
        fan_kernel,
        out_shape=(shape((peers, len(shards), rows, own), BF16), shape((8, 128), F32)),
        in_specs=[_smem()] * 3 + _vmem(len(shards)),
        out_specs=tuple(_vmem(2)),
        name="fan",
    )(lengthscale, outputscale, noise_level, *near(*shards))
    if paired:
        groups = [
            [2 * (side * half + (at ^ (at >> 1))) + core for at in range(half)]
            for side in range(2)
            for core in range(2)
        ]
        vectors = [lax.all_to_all(message, axes, 0, 0, tiled=True, axis_index_groups=groups)]
        vectors.append(lax.ppermute(vectors[0], "grp", SWAP))
    else:
        vectors = [lax.all_to_all(message, axes, 0, 0, tiled=True).reshape(steps, 2, rows, own)]

    tile_shape = shape((steps, own, 2 * own), BF16)
    wide_shape = shape((steps, 2, cols, own), F32)

    operands = []

    def kern_call(part, vector, *before):
        outs = [tile_shape, row_shape]
        if part == 0:
            outs = [shape((own, feats), BF16), shape((own, own), F32)] + outs
        with_message = part + 1 == part_count
        if with_message:
            outs.append(shape((devices, cols // part_count, own), F32))
            before = (*before, own_right)
        results = call(
            functools.partial(kern_kernel, part > 0, with_message),
            out_shape=tuple(outs),
            in_specs=_vmem(2 + len(operands or [vector]) + len(before)),
            out_specs=tuple(_vmem(len(outs))),
            name="kern",
        )(*near(scalars, *(operands or [own_points]), vector, *before))
        if part == 0:
            operands.extend(results[:2])
            results = results[2:]
        return results

    def dkern_call(vector, *before):
        return call(
            functools.partial(dkern_kernel, len(before) > 0),
            out_shape=(tile_shape, wide_shape, row_shape, row_shape),
            in_specs=_vmem(4 + len(before)),
            out_specs=tuple(_vmem(4)),
            name="dkern",
        )(*near(scalars, *operands, vector, *before))

    kerns = [kern_call(0, vectors[0])]
    dkerns = []
    if paired:
        dkerns.append(dkern_call(vectors[0]))
        vectors[1], *dkerns[0] = lax.optimization_barrier((vectors[1], *dkerns[0]))
        kerns.append(kern_call(1, vectors[1], kerns[0][1]))
    kernel_first, message = kerns[-1][1:]
    received = [lax.all_to_all(message, axes, 0, 0, tiled=True)]
    if paired:
        received[0], vectors[1] = lax.optimization_barrier((received[0], vectors[1]))
        received.append(lax.ppermute(received[0], "grp", SWAP))
        dkerns.append(dkern_call(vectors[1], dkerns[0][2]))
    else:
        dkerns.append(dkern_call(vectors[0]))
    kerns = [tiles for tiles, *rest in kerns]
    slope_first = dkerns[-1][2]
    dkerns, wides, norms = [[outs[slot] for outs in dkerns] for slot in (0, 1, 3)]

    both_shape = shape((devices // 2, 2, cols, own), F32)
    message, direction, residual, applied, columns, products, turned = call(
        functools.partial(second_kernel, part_count, paired),
        out_shape=(
            shape((devices, 2, own), F32), row_shape, row_shape, row_shape, shape((cols, 128), F32),
            both_shape, both_shape,
        ),
        in_specs=_vmem(4 + 5 * part_count),
        out_specs=tuple(_vmem(7)),
        name="second",
        compiler_params=pltpu.CompilerParams(
            vmem_limit_bytes=limit
        ),
    )(
        *near(scalars, own_right, kernel_first, slope_first, *kerns, *dkerns, *wides, *norms, *received),
    )
    received = lax.all_to_all(message, axes, 0, 0, tiled=True)

    solution, final, gradient = call(
        functools.partial(last_kernel, part_count, paired, float(own * devices)),
        out_shape=(result((cols, own), F32), result((cols, own), F32), result((3,), F32)),
        in_specs=_vmem(9 + part_count),
        out_specs=tuple(_hbm(3)),
        scratch_shapes=[
            pltpu.VMEM((cols, own), F32),
            pltpu.VMEM((cols, own), F32),
            pltpu.SMEM((3,), F32),
            pltpu.SemaphoreType.DMA((3,)),
        ],
        name="last",
    )(
        *near(scalars, own_right, direction, residual, applied, columns, products, turned, received, *wides),
    )
    return solution, final, gradient


def solution(mesh):
    whole = P(None, ("blk", "grp"))
    return jax.shard_map(
        functools.partial(local, dict(mesh.shape)),
        mesh=mesh,
        in_specs=(whole, whole, P(), P(), P()),
        out_specs=(whole, whole, P()),
        check_vma=False,
    )
```

```python
import functools
import math

import jax
import jax.numpy as jnp
from jax import lax
from jax.experimental import pallas as pl
from jax.experimental.pallas import tpu as pltpu
from jax.sharding import PartitionSpec as P

F32 = jnp.float32
BF16 = jnp.bfloat16
LOG2E = math.log2(math.e)
TINY = 1e-36
NT = (((1,), (1,)), ((), ()))


def _vmem(count):
    return [pl.BlockSpec(memory_space=pltpu.VMEM) for _ in range(count)]


def _smem():
    return pl.BlockSpec(memory_space=pltpu.SMEM)


def _hbm(count):
    return [pl.BlockSpec(memory_space=pltpu.HBM) for _ in range(count)]


def lane_sum(values):
    return jnp.sum(values, axis=1, keepdims=True)


def unrolled(count, most):
    return max(divisor for divisor in range(1, most + 1) if count % divisor == 0)


def pack_kernel(points_hbm, right_hbm, out_ref, points_ref, right_ref, sems):
    feats = points_ref.shape[0]
    cols = right_ref.shape[0]
    copies = [
        pltpu.make_async_copy(right_hbm, right_ref, sems.at[0]),
        pltpu.make_async_copy(points_hbm, points_ref, sems.at[1]),
    ]
    for copy in copies:
        copy.start()
    copies[0].wait()
    right = right_ref[...]
    high = right.astype(BF16)
    out_ref[feats : feats + cols, :] = high
    out_ref[feats + cols : feats + 2 * cols, :] = (right - high.astype(F32)).astype(BF16)
    copies[1].wait()
    out_ref[0:feats, :] = points_ref[...]


def fan_kernel(length_ref, amplitude_ref, jitter_ref, *refs):
    *shards, out_ref, scalars_ref = refs
    for slot, scalar in enumerate((length_ref, amplitude_ref, jitter_ref)):
        scalars_ref[slot : slot + 1, :] = jnp.full((1, 128), scalar[0], F32)
    shards = [shard[...] for shard in shards]
    for peer in range(out_ref.shape[0]):
        for side, shard in enumerate(shards):
            out_ref[peer, side] = shard


def own_place():
    return lax.axis_index("blk"), lax.axis_index("grp")


def source_of(place, paired, steps, part, step, side):
    if not paired:
        return step * 2 + side
    block, own_core = place
    core = own_core if part == 0 else 1 - own_core
    first = jnp.where((block < steps) == (side == 0), 0, steps)
    return (first + (step ^ (step >> 1))) * 2 + core


def joined(sums):
    return functools.reduce(jnp.add, [functools.reduce(jnp.add, sides) for sides in sums])


def own_operand(points_ref, scale):
    own = points_ref.shape[1]
    points = points_ref[...].astype(F32).T
    squares = jnp.sum(points * points, axis=1, keepdims=True) * ((5.0 * LOG2E * LOG2E) / (scale * scale))
    return (-2.0 * points).astype(BF16), jnp.broadcast_to(squares, (own, own))


class Distances:
    def __init__(self, scale, points, squares):
        self.scale = scale
        self.factor = (5.0 * LOG2E * LOG2E) / (scale * scale)
        self.points = points
        self.squares = squares

    def __call__(self, points):
        wide = points.astype(F32)
        squares = jnp.sum(wide * wide, axis=0, keepdims=True) * self.factor
        inner = jnp.dot(self.points, points, preferred_element_type=F32)
        reduced = jnp.maximum((self.squares + squares) + inner * self.factor, TINY)
        return reduced, reduced * lax.rsqrt(reduced)


def kern_tile(reduced, root):
    shifted = root + 1.5 * LOG2E
    return (shifted * shifted + 0.75 * LOG2E * LOG2E) * jnp.exp2(-math.log2(3.0 * LOG2E * LOG2E) - root)


def kern_kernel(has_before, with_message, scalars_ref, points_ref, *refs):
    scale = scalars_ref[0:1, :]
    refs = list(refs)
    squares_ref = refs.pop(0) if has_before else None
    part_ref = refs.pop(0)
    before = refs.pop(0)[...] if has_before else None
    right_ref = refs.pop(0) if with_message else None
    if has_before:
        distances = Distances(scale, points_ref[...], squares_ref[...])
    else:
        operand_ref, squares_ref = refs.pop(0), refs.pop(0)
        operand, squares = own_operand(points_ref, scale)
        operand_ref[...] = operand
        squares_ref[...] = squares
        distances = Distances(scale, operand, squares)
    tiles_ref, *outs = refs
    total_ref = outs[0]
    cols, own = total_ref.shape
    feats = part_ref.shape[2] - 2 * cols
    steps, sides = part_ref.shape[:2]
    total = before if has_before else jnp.zeros((cols, own), F32)

    def one_pair(step, total):
        vectors = []
        for side in range(sides):
            tile = kern_tile(*distances(part_ref[step, side, 0:feats, :]))
            tiles_ref[step, :, pl.ds(side * own, own)] = tile.astype(BF16)
            vectors.append(part_ref[step, side, feats : feats + cols, :])
        vectors = jnp.concatenate(vectors, axis=1)
        return total + lax.dot_general(vectors, tiles_ref[step], NT, preferred_element_type=F32)

    total = lax.fori_loop(0, steps, one_pair, total, unroll=unrolled(steps, 8))
    total_ref[...] = total
    if with_message:
        right = right_ref[...]
        high = right.astype(BF16).astype(F32)
        low = (right - high).astype(BF16).astype(F32)
        lost = ((right - high) - low) / jnp.where(right == 0.0, 1.0, right)
        product = total - total * lost
        message_ref = outs[1]
        rows = message_ref.shape[1]
        for peer in range(message_ref.shape[0]):
            first = (peer * rows) % cols
            message_ref[peer] = product[first : first + rows]


def dkern_kernel(has_before, scalars_ref, operand_ref, squares_ref, part_ref, *refs):
    before = refs[0][...] if has_before else None
    tiles_ref, wide_ref, total_ref, norm_ref = refs[1 if has_before else 0 :]
    cols, own = total_ref.shape
    feats = part_ref.shape[2] - 2 * cols
    distances = Distances(scalars_ref[0:1, :], operand_ref[...], squares_ref[...])
    slope = 1.0 / (3.0 * LOG2E * LOG2E * LOG2E * distances.scale)
    steps, sides = part_ref.shape[:2]
    zero = jnp.zeros((cols, own), F32)

    def one_pair(step, carried):
        total, norm = carried
        norm = list(norm)
        vectors = []
        for side in range(sides):
            reduced, root = distances(part_ref[step, side, 0:feats, :])
            tile = (reduced * slope) * ((root + LOG2E) * jnp.exp2(-root))
            tiles_ref[step, :, pl.ds(side * own, own)] = tile.astype(BF16)
            high = part_ref[step, side, feats : feats + cols, :]
            low = part_ref[step, side, feats + cols : feats + 2 * cols, :]
            right = high.astype(F32) + low.astype(F32)
            wide_ref[step, side] = right
            norm[side] = norm[side] + right * right
            vectors.append(high)
        vectors = jnp.concatenate(vectors, axis=1)
        total = total + lax.dot_general(vectors, tiles_ref[step], NT, preferred_element_type=F32)
        return total, tuple(norm)

    start = (before if has_before else zero, (zero,) * sides)
    total, norm = lax.fori_loop(0, steps, one_pair, start, unroll=unrolled(steps, 8))
    total_ref[...] = total
    norm_ref[...] = jnp.broadcast_to(lane_sum(functools.reduce(jnp.add, norm)), norm_ref.shape)


def from_lanes(row, first, cols):
    lanes = lax.broadcasted_iota(jnp.int32, (cols, 128), 1)
    rows = lax.broadcasted_iota(jnp.int32, (cols, 128), 0)
    picked = jnp.where(lanes == rows + first, jnp.broadcast_to(row, (cols, 128)), 0.0)
    return lane_sum(picked)


def into_columns(columns, cols):
    lanes = lax.broadcasted_iota(jnp.int32, (cols, 128), 1)
    kept = jnp.zeros((cols, 128), F32)
    for slot, column in enumerate(columns):
        kept = jnp.where(lanes == slot, jnp.broadcast_to(column, (cols, 128)), kept)
    return kept


def second_kernel(
    part_count, paired, scalars_ref, right_ref, kernel_ref, slope_ref,
    *refs
):
    kerns, dkerns, wides, norms, received, outs = [
        refs[group * part_count : (group + 1) * part_count] for group in range(5)
    ] + [refs[5 * part_count :]]
    (
        message_ref, direction_ref, residual_ref, applied_ref, columns_ref, products_ref, turned_ref,
    ) = outs
    cols, own = right_ref.shape
    sides = wides[0].shape[1]
    amplitude = scalars_ref[1:2, :]
    jitter = scalars_ref[2:3, :]
    place = own_place()
    low_core = place[1] == 0
    zero = jnp.zeros((cols, own), F32)
    norm = functools.reduce(jnp.add, [norm_ref[:, 0:1] for norm_ref in norms])
    steps = kerns[0].shape[0]

    sums = []
    for part in range(part_count):
        def first_pass(index, carried, part=part):
            carried = [list(sums) for sums in carried]
            for side in range(sides):
                source = source_of(place, paired, steps, part, index, side)
                product = received[0][source]
                if paired:
                    other = received[1][source]
                    product = jnp.concatenate(
                        [jnp.where(low_core, product, other), jnp.where(low_core, other, product)],
                        axis=0,
                    )
                products_ref[part * steps + index, side] = product
                right = wides[part][index, side]
                applied = amplitude * product + jitter * right
                carried[0][side] = carried[0][side] + right * applied
                carried[1][side] = carried[1][side] + applied * applied
            return tuple(tuple(sums) for sums in carried)

        sums.append(
            lax.fori_loop(0, steps, first_pass, ((zero,) * sides,) * 2, unroll=unrolled(steps, 8))
        )
    curvature, length = [lane_sum(joined(parts)) for parts in zip(*sums)]
    step = norm / curvature
    turn = (step * step * length - norm) / norm
    right_factor = jnp.broadcast_to(1.0 - step * jitter, (cols, own))
    product_factor = jnp.broadcast_to(step * amplitude, (cols, own))

    sums = []
    total = zero
    slopes = zero
    for part in range(part_count):
        def second_pass(index, carried, part=part):
            total, slopes, lengths = carried
            lengths = list(lengths)
            rounded = []
            for side in range(sides):
                right = wides[part][index, side]
                product = products_ref[part * steps + index, side]
                residual = right * right_factor - product * product_factor
                direction = residual + turn * right
                turned_ref[part * steps + index, side] = direction
                lengths[side] = lengths[side] + residual * residual
                rounded.append(direction)
            rounded = jnp.concatenate(rounded, axis=1).astype(BF16)
            tiles = jnp.concatenate([kerns[part][index], dkerns[part][index]], axis=0)
            both = lax.dot_general(rounded, tiles, NT, preferred_element_type=F32)
            total = total + both[:, 0:own]
            slopes = slopes + both[:, own : 2 * own]
            return total, slopes, tuple(lengths)

        total, slopes, lengths = lax.fori_loop(
            0, steps, second_pass, (total, slopes, (zero,) * sides), unroll=unrolled(steps, 8)
        )
        sums.append(lengths)
    norm_next = lane_sum(joined(sums))

    right = right_ref[...]
    residual = right * right_factor - kernel_ref[...] * product_factor
    direction = residual + turn * right
    applied = amplitude * total + jitter * direction
    direction_ref[...] = direction
    residual_ref[...] = residual
    applied_ref[...] = applied
    columns_ref[...] = into_columns([step, norm_next, norm, turn], cols)

    low = right - right.astype(BF16).astype(F32)
    low_direction = direction - direction.astype(BF16).astype(F32)
    slope = slope_ref[...]
    lanes = lax.broadcasted_iota(jnp.int32, (cols, 128), 1)
    rows = lax.broadcasted_iota(jnp.int32, (cols, 128), 0)
    packed = jnp.zeros((cols, 128), F32)
    for slot, values in enumerate([
        direction * applied, low * total, low * kernel_ref[...], right * slope, right * slopes,
    ]):
        packed = jnp.where(lanes == rows + slot * cols, lane_sum(values), packed)
    rows = jnp.where(rows == 0, 5 * cols, 128)
    for slot, values in enumerate([
        direction * slope, direction * slopes, low_direction * kernel_ref[...], low_direction * total,
    ]):
        packed = jnp.where(lanes == rows + slot, lane_sum(values), packed)
    packed = jnp.sum(packed, axis=0, keepdims=True)
    for peer in range(message_ref.shape[0]):
        message_ref[peer, 0:1, :] = packed
        message_ref[peer, 1:2, :] = total[0:1, :]


def last_kernel(
    part_count, paired, points_total, scalars_ref, right_ref, direction_ref,
    residual_ref, applied_ref, columns_ref, products_ref, turned_ref, received_ref, *refs
):
    wides = refs[:part_count]
    solution_hbm, final_hbm, gradient_hbm, solution_ref, final_ref, gradient_ref, sems = refs[part_count:]
    cols, own = right_ref.shape
    amplitude = scalars_ref[1:2, 0:1]
    place = own_place()
    devices = received_ref.shape[0]

    def gather_sums(device, carried):
        return carried + received_ref[device, 0:1, :]

    sums = lax.fori_loop(
        0, devices, gather_sums, jnp.zeros((1, 128), F32), unroll=unrolled(devices, 32)
    )
    step, norm_next, norm = [columns_ref[:, slot : slot + 1] for slot in range(3)]
    step_next = norm_next / from_lanes(sums, 0, cols)

    solution_ref[...] = step * right_ref[...] + step_next * direction_ref[...]
    final_ref[...] = residual_ref[...] - step_next * applied_ref[...]
    copies = [
        pltpu.make_async_copy(solution_ref, solution_hbm, sems.at[0]),
        pltpu.make_async_copy(final_ref, final_hbm, sems.at[1]),
    ]
    for copy in copies:
        copy.start()

    low_next, low_first, right_slope, right_slope_next = [
        from_lanes(sums, slot * cols, cols) for slot in range(1, 5)
    ]
    slope_cross, slope_square, low_second, low_square = [
        sums[:, 5 * cols + slot : 5 * cols + slot + 1] for slot in range(4)
    ]
    turn = columns_ref[:, 3:4]
    dots = turn * norm
    squares = norm_next + turn * dots
    steps, sides = wides[0].shape[:2]
    zero = jnp.zeros((cols, own), F32)
    row_zero = jnp.zeros((1, own), F32)
    sums = []
    for part in range(part_count):
        def one_pair(index, carried, part=part):
            carried = [list(sums) for sums in carried]
            block = part * steps + index
            for side in range(sides):
                vector = step * wides[part][index, side] + step_next * turned_ref[block, side]
                rounded = vector.astype(BF16).astype(F32)
                source = source_of(place, paired, steps, part, index, side)
                carried[0][side] = carried[0][side] + products_ref[block, side] * rounded
                carried[1][side] = carried[1][side] + received_ref[source, 1:2, :] * rounded[0:1, :]
            return tuple(tuple(sums) for sums in carried)

        start = ((zero,) * sides, (row_zero,) * sides)
        sums.append(lax.fori_loop(0, steps, one_pair, start, unroll=unrolled(steps, 4)))
    whole, first_row = [joined(parts) for parts in zip(*sums)]
    right_kernel = lane_sum(whole) + step * low_first + step_next * low_next
    first_step, second_step = step[0:1], step_next[0:1]
    direction_kernel = lane_sum(first_row) + first_step * low_second + second_step * low_square
    direction_slope = first_step * slope_cross + second_step * slope_square
    is_first = lax.broadcasted_iota(jnp.int32, (cols, 1), 0) == 0
    weight = jnp.where(is_first, 1.0, -1.0 / (cols - 1))
    for slot, (right_form, direction_form) in enumerate((
        (
            amplitude * (step * right_slope + step_next * right_slope_next),
            amplitude * direction_slope,
        ),
        (right_kernel, direction_kernel),
        (step * norm + step_next * dots, (step * dots + step_next * squares)[0:1]),
    )):
        form = jnp.where(is_first, step * right_form + step_next * direction_form, right_form)
        gradient_ref[slot] = jnp.sum(weight * form) * (0.5 / points_total)
    copies.append(pltpu.make_async_copy(gradient_ref, gradient_hbm, sems.at[2]))
    copies[2].start()
    for copy in copies:
        copy.wait()


SWAP = [(0, 1), (1, 0)]


def local(mesh_shape, points, right_side, lengthscale, outputscale, noise_level):
    axes = ("blk", "grp")
    feats, own = points.shape
    cols = right_side.shape[0]
    rows = feats + 2 * cols
    blocks = mesh_shape["blk"]
    devices = blocks * mesh_shape["grp"]
    paired = mesh_shape["grp"] == 2 and blocks >= 2 and blocks & (blocks - 1) == 0
    part_count = 2 if paired else 1
    steps = devices // (2 * part_count)
    params = pltpu.CompilerParams(vmem_limit_bytes=(4 << 20) + devices * (40 << 10))
    shape = pltpu.VMEM
    result = jax.ShapeDtypeStruct

    def near(*arrays):
        return [pltpu.with_memory_space_constraint(array, pltpu.VMEM) for array in arrays]

    call = functools.partial(pl.pallas_call, compiler_params=params)

    row_shape = shape((cols, own), F32)
    shard, own_points, own_right = call(
        pack_kernel,
        out_shape=(shape((rows, own), BF16), shape((feats, own), BF16), row_shape),
        in_specs=_hbm(2),
        out_specs=tuple(_vmem(3)),
        scratch_shapes=[pltpu.SemaphoreType.DMA((2,))],
        name="pack",
    )(*[pltpu.with_memory_space_constraint(array, pltpu.HBM) for array in (points, right_side)])
    shards = [shard]
    if paired:
        half = blocks // 2
        shards.append(lax.ppermute(shard, "blk", [(at, (at + half) % blocks) for at in range(blocks)]))
    peers = blocks // 2 if paired else devices
    message, scalars = call(
        fan_kernel,
        out_shape=(shape((peers, len(shards), rows, own), BF16), shape((8, 128), F32)),
        in_specs=[_smem()] * 3 + _vmem(len(shards)),
        out_specs=tuple(_vmem(2)),
        name="fan",
    )(lengthscale, outputscale, noise_level, *near(*shards))
    if paired:
        groups = [
            [2 * (side * half + (at ^ (at >> 1))) + core for at in range(half)]
            for side in range(2)
            for core in range(2)
        ]
        vectors = [lax.all_to_all(message, axes, 0, 0, tiled=True, axis_index_groups=groups)]
        vectors.append(lax.ppermute(vectors[0], "grp", SWAP))
    else:
        vectors = [lax.all_to_all(message, axes, 0, 0, tiled=True).reshape(steps, 2, rows, own)]

    tile_shape = shape((steps, own, 2 * own), BF16)
    wide_shape = shape((steps, 2, cols, own), F32)

    operands = []

    def kern_call(part, vector, *before):
        outs = [tile_shape, row_shape]
        if part == 0:
            outs = [shape((own, feats), BF16), shape((own, own), F32)] + outs
        with_message = part + 1 == part_count
        if with_message:
            outs.append(shape((devices, cols // part_count, own), F32))
            before = (*before, own_right)
        results = call(
            functools.partial(kern_kernel, part > 0, with_message),
            out_shape=tuple(outs),
            in_specs=_vmem(2 + len(operands or [vector]) + len(before)),
            out_specs=tuple(_vmem(len(outs))),
            name="kern",
        )(*near(scalars, *(operands or [own_points]), vector, *before))
        if part == 0:
            operands.extend(results[:2])
            results = results[2:]
        return results

    def dkern_call(vector, *before):
        return call(
            functools.partial(dkern_kernel, len(before) > 0),
            out_shape=(tile_shape, wide_shape, row_shape, row_shape),
            in_specs=_vmem(4 + len(before)),
            out_specs=tuple(_vmem(4)),
            name="dkern",
        )(*near(scalars, *operands, vector, *before))

    kerns = [kern_call(0, vectors[0])]
    dkerns = []
    if paired:
        dkerns.append(dkern_call(vectors[0]))
        vectors[1], *dkerns[0] = lax.optimization_barrier((vectors[1], *dkerns[0]))
        kerns.append(kern_call(1, vectors[1], kerns[0][1]))
    kernel_first, message = kerns[-1][1:]
    received = [lax.all_to_all(message, axes, 0, 0, tiled=True)]
    if paired:
        received[0], vectors[1] = lax.optimization_barrier((received[0], vectors[1]))
        received.append(lax.ppermute(received[0], "grp", SWAP))
        dkerns.append(dkern_call(vectors[1], dkerns[0][2]))
    else:
        dkerns.append(dkern_call(vectors[0]))
    kerns = [tiles for tiles, *rest in kerns]
    slope_first = dkerns[-1][2]
    dkerns, wides, norms = [[outs[slot] for outs in dkerns] for slot in (0, 1, 3)]

    both_shape = shape((devices // 2, 2, cols, own), F32)
    message, direction, residual, applied, columns, products, turned = call(
        functools.partial(second_kernel, part_count, paired),
        out_shape=(
            shape((devices, 2, own), F32), row_shape, row_shape, row_shape, shape((cols, 128), F32),
            both_shape, both_shape,
        ),
        in_specs=_vmem(4 + 5 * part_count),
        out_specs=tuple(_vmem(7)),
        name="second",
    )(
        *near(scalars, own_right, kernel_first, slope_first, *kerns, *dkerns, *wides, *norms, *received),
    )
    received = lax.all_to_all(message, axes, 0, 0, tiled=True)

    solution, final, gradient = call(
        functools.partial(last_kernel, part_count, paired, float(own * devices)),
        out_shape=(result((cols, own), F32), result((cols, own), F32), result((3,), F32)),
        in_specs=_vmem(9 + part_count),
        out_specs=tuple(_hbm(3)),
        scratch_shapes=[
            pltpu.VMEM((cols, own), F32),
            pltpu.VMEM((cols, own), F32),
            pltpu.SMEM((3,), F32),
            pltpu.SemaphoreType.DMA((3,)),
        ],
        name="last",
    )(
        *near(scalars, own_right, direction, residual, applied, columns, products, turned, received, *wides),
    )
    return solution, final, gradient


def solution(mesh):
    whole = P(None, ("blk", "grp"))
    return jax.shard_map(
        functools.partial(local, dict(mesh.shape)),
        mesh=mesh,
        in_specs=(whole, whole, P(), P(), P()),
        out_specs=(whole, whole, P()),
        check_vma=False,
    )
```

```python
import functools
import math

import jax
import jax.numpy as jnp
from jax import lax
from jax.experimental import pallas as pl
from jax.experimental.pallas import tpu as pltpu
from jax.sharding import PartitionSpec as P

F32 = jnp.float32
BF16 = jnp.bfloat16
LOG2E = math.log2(math.e)
TINY = 1e-36
NT = (((1,), (1,)), ((), ()))


def _vmem(count):
    return [pl.BlockSpec(memory_space=pltpu.VMEM) for _ in range(count)]


def _smem():
    return pl.BlockSpec(memory_space=pltpu.SMEM)


def _hbm(count):
    return [pl.BlockSpec(memory_space=pltpu.HBM) for _ in range(count)]


def lane_sum(values):
    return jnp.sum(values, axis=1, keepdims=True)


def unrolled(count, most):
    return max(divisor for divisor in range(1, most + 1) if count % divisor == 0)


def pack_kernel(points_hbm, right_hbm, out_ref, points_ref, right_ref, sems):
    feats = points_ref.shape[0]
    cols = right_ref.shape[0]
    copies = [
        pltpu.make_async_copy(right_hbm, right_ref, sems.at[0]),
        pltpu.make_async_copy(points_hbm, points_ref, sems.at[1]),
    ]
    for copy in copies:
        copy.start()
    copies[0].wait()
    right = right_ref[...]
    high = right.astype(BF16)
    out_ref[feats : feats + cols, :] = high
    out_ref[feats + cols : feats + 2 * cols, :] = (right - high.astype(F32)).astype(BF16)
    copies[1].wait()
    out_ref[0:feats, :] = points_ref[...]


def fan_kernel(length_ref, amplitude_ref, jitter_ref, *refs):
    *shards, out_ref, scalars_ref = refs
    for slot, scalar in enumerate((length_ref, amplitude_ref, jitter_ref)):
        scalars_ref[slot : slot + 1, :] = jnp.full((1, 128), scalar[0], F32)
    shards = [shard[...] for shard in shards]
    for peer in range(out_ref.shape[0]):
        for side, shard in enumerate(shards):
            out_ref[peer, side] = shard


def own_place():
    return lax.axis_index("blk"), lax.axis_index("grp")


def source_of(place, paired, steps, part, step, side):
    if not paired:
        return step * 2 + side
    block, own_core = place
    core = own_core if part == 0 else 1 - own_core
    first = jnp.where((block < steps) == (side == 0), 0, steps)
    return (first + (step ^ (step >> 1))) * 2 + core


def joined(sums):
    return functools.reduce(jnp.add, [functools.reduce(jnp.add, sides) for sides in sums])


def own_operand(points_ref, scale):
    own = points_ref.shape[1]
    points = points_ref[...].astype(F32).T
    squares = jnp.sum(points * points, axis=1, keepdims=True) * ((5.0 * LOG2E * LOG2E) / (scale * scale))
    return (-2.0 * points).astype(BF16), jnp.broadcast_to(squares, (own, own))


class Distances:
    def __init__(self, scale, points, squares):
        self.scale = scale
        self.factor = (5.0 * LOG2E * LOG2E) / (scale * scale)
        self.points = points
        self.squares = squares

    def __call__(self, points):
        wide = points.astype(F32)
        squares = jnp.sum(wide * wide, axis=0, keepdims=True) * self.factor
        inner = jnp.dot(self.points, points, preferred_element_type=F32)
        reduced = jnp.maximum((self.squares + squares) + inner * self.factor, TINY)
        return reduced, reduced * lax.rsqrt(reduced)


def kern_tile(reduced, root):
    shifted = root + 1.5 * LOG2E
    return (shifted * shifted + 0.75 * LOG2E * LOG2E) * jnp.exp2(-math.log2(3.0 * LOG2E * LOG2E) - root)


def kern_kernel(has_before, with_message, scalars_ref, points_ref, *refs):
    scale = scalars_ref[0:1, :]
    refs = list(refs)
    squares_ref = refs.pop(0) if has_before else None
    part_ref = refs.pop(0)
    before = refs.pop(0)[...] if has_before else None
    right_ref = refs.pop(0) if with_message else None
    if has_before:
        distances = Distances(scale, points_ref[...], squares_ref[...])
    else:
        operand_ref, squares_ref = refs.pop(0), refs.pop(0)
        operand, squares = own_operand(points_ref, scale)
        operand_ref[...] = operand
        squares_ref[...] = squares
        distances = Distances(scale, operand, squares)
    tiles_ref, *outs = refs
    total_ref = outs[0]
    cols, own = total_ref.shape
    feats = part_ref.shape[2] - 2 * cols
    steps, sides = part_ref.shape[:2]
    total = before if has_before else jnp.zeros((cols, own), F32)

    def one_pair(step, total):
        vectors = []
        for side in range(sides):
            tile = kern_tile(*distances(part_ref[step, side, 0:feats, :]))
            tiles_ref[step, :, pl.ds(side * own, own)] = tile.astype(BF16)
            vectors.append(part_ref[step, side, feats : feats + cols, :])
        vectors = jnp.concatenate(vectors, axis=1)
        return total + lax.dot_general(vectors, tiles_ref[step], NT, preferred_element_type=F32)

    total = lax.fori_loop(0, steps, one_pair, total, unroll=unrolled(steps, 8))
    total_ref[...] = total
    if with_message:
        right = right_ref[...]
        high = right.astype(BF16).astype(F32)
        low = (right - high).astype(BF16).astype(F32)
        lost = ((right - high) - low) / jnp.where(right == 0.0, 1.0, right)
        product = total - total * lost
        message_ref = outs[1]
        rows = message_ref.shape[1]
        for peer in range(message_ref.shape[0]):
            first = (peer * rows) % cols
            message_ref[peer] = product[first : first + rows]


def dkern_kernel(has_before, scalars_ref, operand_ref, squares_ref, part_ref, *refs):
    before = refs[0][...] if has_before else None
    tiles_ref, wide_ref, total_ref, norm_ref = refs[1 if has_before else 0 :]
    cols, own = total_ref.shape
    feats = part_ref.shape[2] - 2 * cols
    distances = Distances(scalars_ref[0:1, :], operand_ref[...], squares_ref[...])
    slope = 1.0 / (3.0 * LOG2E * LOG2E * LOG2E * distances.scale)
    steps, sides = part_ref.shape[:2]
    zero = jnp.zeros((cols, own), F32)

    def one_pair(step, carried):
        total, norm = carried
        norm = list(norm)
        vectors = []
        for side in range(sides):
            reduced, root = distances(part_ref[step, side, 0:feats, :])
            tile = (reduced * slope) * ((root + LOG2E) * jnp.exp2(-root))
            tiles_ref[step, :, pl.ds(side * own, own)] = tile.astype(BF16)
            high = part_ref[step, side, feats : feats + cols, :]
            low = part_ref[step, side, feats + cols : feats + 2 * cols, :]
            right = high.astype(F32) + low.astype(F32)
            wide_ref[step, side] = right
            norm[side] = norm[side] + right * right
            vectors.append(high)
        vectors = jnp.concatenate(vectors, axis=1)
        total = total + lax.dot_general(vectors, tiles_ref[step], NT, preferred_element_type=F32)
        return total, tuple(norm)

    start = (before if has_before else zero, (zero,) * sides)
    total, norm = lax.fori_loop(0, steps, one_pair, start, unroll=unrolled(steps, 8))
    total_ref[...] = total
    norm_ref[...] = jnp.broadcast_to(lane_sum(functools.reduce(jnp.add, norm)), norm_ref.shape)


def from_lanes(row, first, cols):
    lanes = lax.broadcasted_iota(jnp.int32, (cols, 128), 1)
    rows = lax.broadcasted_iota(jnp.int32, (cols, 128), 0)
    picked = jnp.where(lanes == rows + first, jnp.broadcast_to(row, (cols, 128)), 0.0)
    return lane_sum(picked)


def into_columns(columns, cols):
    lanes = lax.broadcasted_iota(jnp.int32, (cols, 128), 1)
    kept = jnp.zeros((cols, 128), F32)
    for slot, column in enumerate(columns):
        kept = jnp.where(lanes == slot, jnp.broadcast_to(column, (cols, 128)), kept)
    return kept


def second_kernel(
    part_count, paired, scalars_ref, right_ref, kernel_ref, slope_ref,
    *refs
):
    kerns, dkerns, wides, norms, received, outs = [
        refs[group * part_count : (group + 1) * part_count] for group in range(5)
    ] + [refs[5 * part_count :]]
    (
        message_ref, direction_ref, residual_ref, applied_ref, columns_ref, products_ref, turned_ref,
    ) = outs
    cols, own = right_ref.shape
    sides = wides[0].shape[1]
    amplitude = scalars_ref[1:2, :]
    jitter = scalars_ref[2:3, :]
    place = own_place()
    low_core = place[1] == 0
    zero = jnp.zeros((cols, own), F32)
    norm = functools.reduce(jnp.add, [norm_ref[:, 0:1] for norm_ref in norms])
    steps = kerns[0].shape[0]

    sums = []
    for part in range(part_count):
        def first_pass(index, carried, part=part):
            carried = [list(sums) for sums in carried]
            for side in range(sides):
                source = source_of(place, paired, steps, part, index, side)
                product = received[0][source]
                if paired:
                    other = received[1][source]
                    product = jnp.concatenate(
                        [jnp.where(low_core, product, other), jnp.where(low_core, other, product)],
                        axis=0,
                    )
                products_ref[part * steps + index, side] = product
                right = wides[part][index, side]
                applied = amplitude * product + jitter * right
                carried[0][side] = carried[0][side] + right * applied
                carried[1][side] = carried[1][side] + applied * applied
            return tuple(tuple(sums) for sums in carried)

        sums.append(
            lax.fori_loop(0, steps, first_pass, ((zero,) * sides,) * 2, unroll=unrolled(steps, 8))
        )
    curvature, length = [lane_sum(joined(parts)) for parts in zip(*sums)]
    step = norm / curvature
    turn = (step * step * length - norm) / norm
    right_factor = jnp.broadcast_to(1.0 - step * jitter, (cols, own))
    product_factor = jnp.broadcast_to(step * amplitude, (cols, own))

    sums = []
    total = zero
    slopes = zero
    for part in range(part_count):
        def second_pass(index, carried, part=part):
            total, slopes, lengths = carried
            lengths = list(lengths)
            rounded = []
            for side in range(sides):
                right = wides[part][index, side]
                product = products_ref[part * steps + index, side]
                residual = right * right_factor - product * product_factor
                direction = residual + turn * right
                turned_ref[part * steps + index, side] = direction
                lengths[side] = lengths[side] + residual * residual
                rounded.append(direction)
            rounded = jnp.concatenate(rounded, axis=1).astype(BF16)
            tiles = jnp.concatenate([kerns[part][index], dkerns[part][index]], axis=0)
            both = lax.dot_general(rounded, tiles, NT, preferred_element_type=F32)
            total = total + both[:, 0:own]
            slopes = slopes + both[:, own : 2 * own]
            return total, slopes, tuple(lengths)

        total, slopes, lengths = lax.fori_loop(
            0, steps, second_pass, (total, slopes, (zero,) * sides), unroll=unrolled(steps, 8)
        )
        sums.append(lengths)
    norm_next = lane_sum(joined(sums))

    right = right_ref[...]
    residual = right * right_factor - kernel_ref[...] * product_factor
    direction = residual + turn * right
    applied = amplitude * total + jitter * direction
    direction_ref[...] = direction
    residual_ref[...] = residual
    applied_ref[...] = applied
    columns_ref[...] = into_columns([step, norm_next, norm, turn], cols)

    low = right - right.astype(BF16).astype(F32)
    low_direction = direction - direction.astype(BF16).astype(F32)
    slope = slope_ref[...]
    lanes = lax.broadcasted_iota(jnp.int32, (cols, 128), 1)
    rows = lax.broadcasted_iota(jnp.int32, (cols, 128), 0)
    packed = jnp.zeros((cols, 128), F32)
    for slot, values in enumerate([
        direction * applied, low * total, low * kernel_ref[...], right * slope, right * slopes,
    ]):
        packed = jnp.where(lanes == rows + slot * cols, lane_sum(values), packed)
    rows = jnp.where(rows == 0, 5 * cols, 128)
    for slot, values in enumerate([
        direction * slope, direction * slopes, low_direction * kernel_ref[...], low_direction * total,
    ]):
        packed = jnp.where(lanes == rows + slot, lane_sum(values), packed)
    packed = jnp.sum(packed, axis=0, keepdims=True)
    for peer in range(message_ref.shape[0]):
        message_ref[peer, 0:1, :] = packed
        message_ref[peer, 1:2, :] = total[0:1, :]


def last_kernel(
    part_count, paired, points_total, scalars_ref, right_ref, direction_ref,
    residual_ref, applied_ref, columns_ref, products_ref, turned_ref, received_ref, *refs
):
    wides = refs[:part_count]
    solution_hbm, final_hbm, gradient_hbm, solution_ref, final_ref, gradient_ref, sems = refs[part_count:]
    cols, own = right_ref.shape
    amplitude = scalars_ref[1:2, 0:1]
    place = own_place()
    devices = received_ref.shape[0]

    chains = unrolled(devices, 4)

    def gather_sums(group, carried):
        return tuple(
            sums + received_ref[group * chains + chain, 0:1, :] for chain, sums in enumerate(carried)
        )

    sums = functools.reduce(
        jnp.add,
        lax.fori_loop(
            0, devices // chains, gather_sums, (jnp.zeros((1, 128), F32),) * chains,
            unroll=unrolled(devices // chains, 8),
        ),
    )
    step, norm_next, norm = [columns_ref[:, slot : slot + 1] for slot in range(3)]
    step_next = norm_next / from_lanes(sums, 0, cols)

    solution_ref[...] = step * right_ref[...] + step_next * direction_ref[...]
    final_ref[...] = residual_ref[...] - step_next * applied_ref[...]
    copies = [
        pltpu.make_async_copy(solution_ref, solution_hbm, sems.at[0]),
        pltpu.make_async_copy(final_ref, final_hbm, sems.at[1]),
    ]
    for copy in copies:
        copy.start()

    low_next, low_first, right_slope, right_slope_next = [
        from_lanes(sums, slot * cols, cols) for slot in range(1, 5)
    ]
    slope_cross, slope_square, low_second, low_square = [
        sums[:, 5 * cols + slot : 5 * cols + slot + 1] for slot in range(4)
    ]
    turn = columns_ref[:, 3:4]
    dots = turn * norm
    squares = norm_next + turn * dots
    steps, sides = wides[0].shape[:2]
    zero = jnp.zeros((cols, own), F32)
    row_zero = jnp.zeros((1, own), F32)
    sums = []
    for part in range(part_count):
        def one_pair(index, carried, part=part):
            carried = [list(sums) for sums in carried]
            block = part * steps + index
            for side in range(sides):
                vector = step * wides[part][index, side] + step_next * turned_ref[block, side]
                rounded = vector.astype(BF16).astype(F32)
                source = source_of(place, paired, steps, part, index, side)
                carried[0][side] = carried[0][side] + products_ref[block, side] * rounded
                carried[1][side] = carried[1][side] + received_ref[source, 1:2, :] * rounded[0:1, :]
            return tuple(tuple(sums) for sums in carried)

        start = ((zero,) * sides, (row_zero,) * sides)
        sums.append(lax.fori_loop(0, steps, one_pair, start, unroll=unrolled(steps, 4)))
    whole, first_row = [joined(parts) for parts in zip(*sums)]
    right_kernel = lane_sum(whole) + step * low_first + step_next * low_next
    first_step, second_step = step[0:1], step_next[0:1]
    direction_kernel = lane_sum(first_row) + first_step * low_second + second_step * low_square
    direction_slope = first_step * slope_cross + second_step * slope_square
    is_first = lax.broadcasted_iota(jnp.int32, (cols, 1), 0) == 0
    weight = jnp.where(is_first, 1.0, -1.0 / (cols - 1))
    for slot, (right_form, direction_form) in enumerate((
        (
            amplitude * (step * right_slope + step_next * right_slope_next),
            amplitude * direction_slope,
        ),
        (right_kernel, direction_kernel),
        (step * norm + step_next * dots, (step * dots + step_next * squares)[0:1]),
    )):
        form = jnp.where(is_first, step * right_form + step_next * direction_form, right_form)
        gradient_ref[slot] = jnp.sum(weight * form) * (0.5 / points_total)
    copies.append(pltpu.make_async_copy(gradient_ref, gradient_hbm, sems.at[2]))
    copies[2].start()
    for copy in copies:
        copy.wait()


SWAP = [(0, 1), (1, 0)]


def local(mesh_shape, points, right_side, lengthscale, outputscale, noise_level):
    axes = ("blk", "grp")
    feats, own = points.shape
    cols = right_side.shape[0]
    rows = feats + 2 * cols
    blocks = mesh_shape["blk"]
    devices = blocks * mesh_shape["grp"]
    paired = mesh_shape["grp"] == 2 and blocks >= 2 and blocks & (blocks - 1) == 0
    part_count = 2 if paired else 1
    steps = devices // (2 * part_count)
    params = pltpu.CompilerParams(vmem_limit_bytes=(4 << 20) + devices * (40 << 10))
    shape = pltpu.VMEM
    result = jax.ShapeDtypeStruct

    def near(*arrays):
        return [pltpu.with_memory_space_constraint(array, pltpu.VMEM) for array in arrays]

    call = functools.partial(pl.pallas_call, compiler_params=params)

    row_shape = shape((cols, own), F32)
    shard, own_points, own_right = call(
        pack_kernel,
        out_shape=(shape((rows, own), BF16), shape((feats, own), BF16), row_shape),
        in_specs=_hbm(2),
        out_specs=tuple(_vmem(3)),
        scratch_shapes=[pltpu.SemaphoreType.DMA((2,))],
        name="pack",
    )(*[pltpu.with_memory_space_constraint(array, pltpu.HBM) for array in (points, right_side)])
    shards = [shard]
    if paired:
        half = blocks // 2
        shards.append(lax.ppermute(shard, "blk", [(at, (at + half) % blocks) for at in range(blocks)]))
    peers = blocks // 2 if paired else devices
    message, scalars = call(
        fan_kernel,
        out_shape=(shape((peers, len(shards), rows, own), BF16), shape((8, 128), F32)),
        in_specs=[_smem()] * 3 + _vmem(len(shards)),
        out_specs=tuple(_vmem(2)),
        name="fan",
    )(lengthscale, outputscale, noise_level, *near(*shards))
    if paired:
        groups = [
            [2 * (side * half + (at ^ (at >> 1))) + core for at in range(half)]
            for side in range(2)
            for core in range(2)
        ]
        vectors = [lax.all_to_all(message, axes, 0, 0, tiled=True, axis_index_groups=groups)]
        vectors.append(lax.ppermute(vectors[0], "grp", SWAP))
    else:
        vectors = [lax.all_to_all(message, axes, 0, 0, tiled=True).reshape(steps, 2, rows, own)]

    tile_shape = shape((steps, own, 2 * own), BF16)
    wide_shape = shape((steps, 2, cols, own), F32)

    operands = []

    def kern_call(part, vector, *before):
        outs = [tile_shape, row_shape]
        if part == 0:
            outs = [shape((own, feats), BF16), shape((own, own), F32)] + outs
        with_message = part + 1 == part_count
        if with_message:
            outs.append(shape((devices, cols // part_count, own), F32))
            before = (*before, own_right)
        results = call(
            functools.partial(kern_kernel, part > 0, with_message),
            out_shape=tuple(outs),
            in_specs=_vmem(2 + len(operands or [vector]) + len(before)),
            out_specs=tuple(_vmem(len(outs))),
            name="kern",
        )(*near(scalars, *(operands or [own_points]), vector, *before))
        if part == 0:
            operands.extend(results[:2])
            results = results[2:]
        return results

    def dkern_call(vector, *before):
        return call(
            functools.partial(dkern_kernel, len(before) > 0),
            out_shape=(tile_shape, wide_shape, row_shape, row_shape),
            in_specs=_vmem(4 + len(before)),
            out_specs=tuple(_vmem(4)),
            name="dkern",
        )(*near(scalars, *operands, vector, *before))

    kerns = [kern_call(0, vectors[0])]
    dkerns = []
    if paired:
        dkerns.append(dkern_call(vectors[0]))
        vectors[1], *dkerns[0] = lax.optimization_barrier((vectors[1], *dkerns[0]))
        kerns.append(kern_call(1, vectors[1], kerns[0][1]))
    kernel_first, message = kerns[-1][1:]
    received = [lax.all_to_all(message, axes, 0, 0, tiled=True)]
    if paired:
        received[0], vectors[1] = lax.optimization_barrier((received[0], vectors[1]))
        received.append(lax.ppermute(received[0], "grp", SWAP))
        dkerns.append(dkern_call(vectors[1], dkerns[0][2]))
    else:
        dkerns.append(dkern_call(vectors[0]))
    kerns = [tiles for tiles, *rest in kerns]
    slope_first = dkerns[-1][2]
    dkerns, wides, norms = [[outs[slot] for outs in dkerns] for slot in (0, 1, 3)]

    both_shape = shape((devices // 2, 2, cols, own), F32)
    message, direction, residual, applied, columns, products, turned = call(
        functools.partial(second_kernel, part_count, paired),
        out_shape=(
            shape((devices, 2, own), F32), row_shape, row_shape, row_shape, shape((cols, 128), F32),
            both_shape, both_shape,
        ),
        in_specs=_vmem(4 + 5 * part_count),
        out_specs=tuple(_vmem(7)),
        name="second",
    )(
        *near(scalars, own_right, kernel_first, slope_first, *kerns, *dkerns, *wides, *norms, *received),
    )
    received = lax.all_to_all(message, axes, 0, 0, tiled=True)

    solution, final, gradient = call(
        functools.partial(last_kernel, part_count, paired, float(own * devices)),
        out_shape=(result((cols, own), F32), result((cols, own), F32), result((3,), F32)),
        in_specs=_vmem(9 + part_count),
        out_specs=tuple(_hbm(3)),
        scratch_shapes=[
            pltpu.VMEM((cols, own), F32),
            pltpu.VMEM((cols, own), F32),
            pltpu.SMEM((3,), F32),
            pltpu.SemaphoreType.DMA((3,)),
        ],
        name="last",
    )(
        *near(scalars, own_right, direction, residual, applied, columns, products, turned, received, *wides),
    )
    return solution, final, gradient


def solution(mesh):
    whole = P(None, ("blk", "grp"))
    return jax.shard_map(
        functools.partial(local, dict(mesh.shape)),
        mesh=mesh,
        in_specs=(whole, whole, P(), P(), P()),
        out_specs=(whole, whole, P()),
        check_vma=False,
    )
```

```python
import functools
import math

import jax
import jax.numpy as jnp
from jax import lax
from jax.experimental import pallas as pl
from jax.experimental.pallas import tpu as pltpu
from jax.sharding import PartitionSpec as P

F32 = jnp.float32
BF16 = jnp.bfloat16
LOG2E = math.log2(math.e)
TINY = 1e-36
NT = (((1,), (1,)), ((), ()))


def _vmem(count):
    return [pl.BlockSpec(memory_space=pltpu.VMEM) for _ in range(count)]


def _smem():
    return pl.BlockSpec(memory_space=pltpu.SMEM)


def _hbm(count):
    return [pl.BlockSpec(memory_space=pltpu.HBM) for _ in range(count)]


def lane_sum(values):
    return jnp.sum(values, axis=1, keepdims=True)


def unrolled(count, most):
    return max(divisor for divisor in range(1, most + 1) if count % divisor == 0)


def pack_kernel(points_hbm, right_hbm, out_ref, points_ref, right_ref, sems):
    feats = points_ref.shape[0]
    cols = right_ref.shape[0]
    copies = [
        pltpu.make_async_copy(right_hbm, right_ref, sems.at[0]),
        pltpu.make_async_copy(points_hbm, points_ref, sems.at[1]),
    ]
    for copy in copies:
        copy.start()
    copies[0].wait()
    right = right_ref[...]
    high = right.astype(BF16)
    out_ref[feats : feats + cols, :] = high
    out_ref[feats + cols : feats + 2 * cols, :] = (right - high.astype(F32)).astype(BF16)
    copies[1].wait()
    out_ref[0:feats, :] = points_ref[...]


def fan_kernel(length_ref, amplitude_ref, jitter_ref, *refs):
    *shards, out_ref, scalars_ref = refs
    for slot, scalar in enumerate((length_ref, amplitude_ref, jitter_ref)):
        scalars_ref[slot : slot + 1, :] = jnp.full((1, 128), scalar[0], F32)
    shards = [shard[...] for shard in shards]
    for peer in range(out_ref.shape[0]):
        for side, shard in enumerate(shards):
            out_ref[peer, side] = shard


def own_place():
    return lax.axis_index("blk"), lax.axis_index("grp")


def source_of(place, paired, steps, part, step, side):
    if not paired:
        return step * 2 + side
    block, own_core = place
    core = own_core if part == 0 else 1 - own_core
    first = jnp.where((block < steps) == (side == 0), 0, steps)
    return (first + (step ^ (step >> 1))) * 2 + core


def joined(sums):
    return functools.reduce(jnp.add, [functools.reduce(jnp.add, sides) for sides in sums])


def own_operand(points_ref, scale):
    own = points_ref.shape[1]
    points = points_ref[...].astype(F32).T
    squares = jnp.sum(points * points, axis=1, keepdims=True) * ((5.0 * LOG2E * LOG2E) / (scale * scale))
    return (-2.0 * points).astype(BF16), jnp.broadcast_to(squares, (own, own))


class Distances:
    def __init__(self, scale, points, squares):
        self.scale = scale
        self.factor = (5.0 * LOG2E * LOG2E) / (scale * scale)
        self.points = points
        self.squares = squares

    def __call__(self, points):
        wide = points.astype(F32)
        squares = jnp.sum(wide * wide, axis=0, keepdims=True) * self.factor
        inner = jnp.dot(self.points, points, preferred_element_type=F32)
        reduced = jnp.maximum((self.squares + squares) + inner * self.factor, TINY)
        return reduced, reduced * lax.rsqrt(reduced)


def kern_tile(reduced, root):
    shifted = root + 1.5 * LOG2E
    return (shifted * shifted + 0.75 * LOG2E * LOG2E) * jnp.exp2(-math.log2(3.0 * LOG2E * LOG2E) - root)


def kern_kernel(has_before, with_message, scalars_ref, points_ref, *refs):
    scale = scalars_ref[0:1, :]
    refs = list(refs)
    squares_ref = refs.pop(0) if has_before else None
    part_ref = refs.pop(0)
    before = refs.pop(0)[...] if has_before else None
    right_ref = refs.pop(0) if with_message else None
    if has_before:
        distances = Distances(scale, points_ref[...], squares_ref[...])
    else:
        operand_ref, squares_ref = refs.pop(0), refs.pop(0)
        operand, squares = own_operand(points_ref, scale)
        operand_ref[...] = operand
        squares_ref[...] = squares
        distances = Distances(scale, operand, squares)
    tiles_ref, *outs = refs
    total_ref = outs[0]
    cols, own = total_ref.shape
    feats = part_ref.shape[2] - 2 * cols
    steps, sides = part_ref.shape[:2]
    total = before if has_before else jnp.zeros((cols, own), F32)

    def one_pair(step, total):
        vectors = []
        for side in range(sides):
            tile = kern_tile(*distances(part_ref[step, side, 0:feats, :]))
            tiles_ref[step, :, pl.ds(side * own, own)] = tile.astype(BF16)
            vectors.append(part_ref[step, side, feats : feats + cols, :])
        vectors = jnp.concatenate(vectors, axis=1)
        return total + lax.dot_general(vectors, tiles_ref[step], NT, preferred_element_type=F32)

    total = lax.fori_loop(0, steps, one_pair, total, unroll=unrolled(steps, 8))
    total_ref[...] = total
    if with_message:
        right = right_ref[...]
        high = right.astype(BF16).astype(F32)
        low = (right - high).astype(BF16).astype(F32)
        lost = ((right - high) - low) / jnp.where(right == 0.0, 1.0, right)
        product = total - total * lost
        message_ref = outs[1]
        rows = message_ref.shape[1]
        for peer in range(message_ref.shape[0]):
            first = (peer * rows) % cols
            message_ref[peer] = product[first : first + rows]


def dkern_kernel(has_before, scalars_ref, operand_ref, squares_ref, part_ref, *refs):
    before = refs[0][...] if has_before else None
    tiles_ref, wide_ref, total_ref, norm_ref = refs[1 if has_before else 0 :]
    cols, own = total_ref.shape
    feats = part_ref.shape[2] - 2 * cols
    distances = Distances(scalars_ref[0:1, :], operand_ref[...], squares_ref[...])
    slope = 1.0 / (3.0 * LOG2E * LOG2E * LOG2E * distances.scale)
    steps, sides = part_ref.shape[:2]
    zero = jnp.zeros((cols, own), F32)

    def one_pair(step, carried):
        total, norm = carried
        norm = list(norm)
        vectors = []
        for side in range(sides):
            reduced, root = distances(part_ref[step, side, 0:feats, :])
            tile = (reduced * slope) * ((root + LOG2E) * jnp.exp2(-root))
            tiles_ref[step, :, pl.ds(side * own, own)] = tile.astype(BF16)
            high = part_ref[step, side, feats : feats + cols, :]
            low = part_ref[step, side, feats + cols : feats + 2 * cols, :]
            right = high.astype(F32) + low.astype(F32)
            wide_ref[step, side] = right
            norm[side] = norm[side] + right * right
            vectors.append(high)
        vectors = jnp.concatenate(vectors, axis=1)
        total = total + lax.dot_general(vectors, tiles_ref[step], NT, preferred_element_type=F32)
        return total, tuple(norm)

    start = (before if has_before else zero, (zero,) * sides)
    total, norm = lax.fori_loop(0, steps, one_pair, start, unroll=unrolled(steps, 8))
    total_ref[...] = total
    norm_ref[...] = jnp.broadcast_to(lane_sum(functools.reduce(jnp.add, norm)), norm_ref.shape)


def from_lanes(row, first, cols):
    lanes = lax.broadcasted_iota(jnp.int32, (cols, 128), 1)
    rows = lax.broadcasted_iota(jnp.int32, (cols, 128), 0)
    picked = jnp.where(lanes == rows + first, jnp.broadcast_to(row, (cols, 128)), 0.0)
    return lane_sum(picked)


def into_columns(columns, cols):
    lanes = lax.broadcasted_iota(jnp.int32, (cols, 128), 1)
    kept = jnp.zeros((cols, 128), F32)
    for slot, column in enumerate(columns):
        kept = jnp.where(lanes == slot, jnp.broadcast_to(column, (cols, 128)), kept)
    return kept


def second_kernel(
    part_count, paired, scalars_ref, right_ref, kernel_ref, slope_ref,
    *refs
):
    kerns, dkerns, wides, norms, received, outs = [
        refs[group * part_count : (group + 1) * part_count] for group in range(5)
    ] + [refs[5 * part_count :]]
    (
        message_ref, direction_ref, residual_ref, applied_ref, columns_ref, products_ref, turned_ref,
    ) = outs
    cols, own = right_ref.shape
    sides = wides[0].shape[1]
    amplitude = scalars_ref[1:2, :]
    jitter = scalars_ref[2:3, :]
    place = own_place()
    low_core = place[1] == 0
    zero = jnp.zeros((cols, own), F32)
    norm = functools.reduce(jnp.add, [norm_ref[:, 0:1] for norm_ref in norms])
    steps = kerns[0].shape[0]

    sums = []
    for part in range(part_count):
        def first_pass(index, carried, part=part):
            carried = [list(sums) for sums in carried]
            for side in range(sides):
                source = source_of(place, paired, steps, part, index, side)
                product = received[0][source]
                if paired:
                    other = received[1][source]
                    product = jnp.concatenate(
                        [jnp.where(low_core, product, other), jnp.where(low_core, other, product)],
                        axis=0,
                    )
                products_ref[part * steps + index, side] = product
                right = wides[part][index, side]
                applied = amplitude * product + jitter * right
                carried[0][side] = carried[0][side] + right * applied
                carried[1][side] = carried[1][side] + applied * applied
            return tuple(tuple(sums) for sums in carried)

        sums.append(
            lax.fori_loop(0, steps, first_pass, ((zero,) * sides,) * 2, unroll=unrolled(steps, 8))
        )
    curvature, length = [lane_sum(joined(parts)) for parts in zip(*sums)]
    step = norm / curvature
    turn = (step * step * length - norm) / norm
    right_factor = jnp.broadcast_to(1.0 - step * jitter, (cols, own))
    product_factor = jnp.broadcast_to(step * amplitude, (cols, own))

    sums = []
    total = zero
    slopes = zero
    for part in range(part_count):
        def second_pass(index, carried, part=part):
            total, slopes, lengths = carried
            lengths = list(lengths)
            rounded = []
            for side in range(sides):
                right = wides[part][index, side]
                product = products_ref[part * steps + index, side]
                residual = right * right_factor - product * product_factor
                direction = residual + turn * right
                turned_ref[part * steps + index, side] = direction
                lengths[side] = lengths[side] + residual * residual
                rounded.append(direction)
            rounded = jnp.concatenate(rounded, axis=1).astype(BF16)
            tiles = jnp.concatenate([kerns[part][index], dkerns[part][index]], axis=0)
            both = lax.dot_general(rounded, tiles, NT, preferred_element_type=F32)
            total = total + both[:, 0:own]
            slopes = slopes + both[:, own : 2 * own]
            return total, slopes, tuple(lengths)

        total, slopes, lengths = lax.fori_loop(
            0, steps, second_pass, (total, slopes, (zero,) * sides), unroll=unrolled(steps, 8)
        )
        sums.append(lengths)
    norm_next = lane_sum(joined(sums))

    right = right_ref[...]
    residual = right * right_factor - kernel_ref[...] * product_factor
    direction = residual + turn * right
    applied = amplitude * total + jitter * direction
    direction_ref[...] = direction
    residual_ref[...] = residual
    applied_ref[...] = applied
    columns_ref[...] = into_columns([step, norm_next, norm, turn], cols)

    low = right - right.astype(BF16).astype(F32)
    low_direction = direction - direction.astype(BF16).astype(F32)
    slope = slope_ref[...]
    lanes = lax.broadcasted_iota(jnp.int32, (cols, 128), 1)
    rows = lax.broadcasted_iota(jnp.int32, (cols, 128), 0)
    packed = jnp.zeros((cols, 128), F32)
    for slot, values in enumerate([
        direction * applied, low * total, low * kernel_ref[...], right * slope, right * slopes,
    ]):
        packed = jnp.where(lanes == rows + slot * cols, lane_sum(values), packed)
    rows = jnp.where(rows == 0, 5 * cols, 128)
    for slot, values in enumerate([
        direction * slope, direction * slopes, low_direction * kernel_ref[...], low_direction * total,
    ]):
        packed = jnp.where(lanes == rows + slot, lane_sum(values), packed)
    packed = jnp.sum(packed, axis=0, keepdims=True)
    for peer in range(message_ref.shape[0]):
        message_ref[peer, 0:1, :] = packed
        message_ref[peer, 1:2, :] = total[0:1, :]


def last_kernel(
    part_count, paired, points_total, scalars_ref, right_ref, direction_ref,
    residual_ref, applied_ref, columns_ref, products_ref, turned_ref, received_ref, *refs
):
    wides = refs[:part_count]
    solution_hbm, final_hbm, gradient_hbm, solution_ref, final_ref, gradient_ref, sems = refs[part_count:]
    cols, own = right_ref.shape
    amplitude = scalars_ref[1:2, 0:1]
    place = own_place()
    devices = received_ref.shape[0]

    chains = unrolled(devices, 4)

    def gather_sums(group, carried):
        return tuple(
            sums + received_ref[group * chains + chain, 0:1, :] for chain, sums in enumerate(carried)
        )

    sums = functools.reduce(
        jnp.add,
        lax.fori_loop(
            0, devices // chains, gather_sums, (jnp.zeros((1, 128), F32),) * chains,
            unroll=unrolled(devices // chains, 8),
        ),
    )
    step, norm_next, norm = [columns_ref[:, slot : slot + 1] for slot in range(3)]
    step_next = norm_next / from_lanes(sums, 0, cols)

    solution_ref[...] = step * right_ref[...] + step_next * direction_ref[...]
    copies = [
        pltpu.make_async_copy(solution_ref, solution_hbm, sems.at[0]),
        pltpu.make_async_copy(final_ref, final_hbm, sems.at[1]),
    ]
    copies[0].start()
    final_ref[...] = residual_ref[...] - step_next * applied_ref[...]
    copies[1].start()

    low_next, low_first, right_slope, right_slope_next = [
        from_lanes(sums, slot * cols, cols) for slot in range(1, 5)
    ]
    slope_cross, slope_square, low_second, low_square = [
        sums[:, 5 * cols + slot : 5 * cols + slot + 1] for slot in range(4)
    ]
    turn = columns_ref[:, 3:4]
    dots = turn * norm
    squares = norm_next + turn * dots
    steps, sides = wides[0].shape[:2]
    zero = jnp.zeros((cols, own), F32)
    row_zero = jnp.zeros((1, own), F32)
    sums = []
    for part in range(part_count):
        def one_pair(index, carried, part=part):
            carried = [list(sums) for sums in carried]
            block = part * steps + index
            for side in range(sides):
                vector = step * wides[part][index, side] + step_next * turned_ref[block, side]
                rounded = vector.astype(BF16).astype(F32)
                source = source_of(place, paired, steps, part, index, side)
                carried[0][side] = carried[0][side] + products_ref[block, side] * rounded
                carried[1][side] = carried[1][side] + received_ref[source, 1:2, :] * rounded[0:1, :]
            return tuple(tuple(sums) for sums in carried)

        start = ((zero,) * sides, (row_zero,) * sides)
        sums.append(lax.fori_loop(0, steps, one_pair, start, unroll=unrolled(steps, 4)))
    whole, first_row = [joined(parts) for parts in zip(*sums)]
    right_kernel = lane_sum(whole) + step * low_first + step_next * low_next
    first_step, second_step = step[0:1], step_next[0:1]
    direction_kernel = lane_sum(first_row) + first_step * low_second + second_step * low_square
    direction_slope = first_step * slope_cross + second_step * slope_square
    is_first = lax.broadcasted_iota(jnp.int32, (cols, 1), 0) == 0
    weight = jnp.where(is_first, 1.0, -1.0 / (cols - 1))
    for slot, (right_form, direction_form) in enumerate((
        (
            amplitude * (step * right_slope + step_next * right_slope_next),
            amplitude * direction_slope,
        ),
        (right_kernel, direction_kernel),
        (step * norm + step_next * dots, (step * dots + step_next * squares)[0:1]),
    )):
        form = jnp.where(is_first, step * right_form + step_next * direction_form, right_form)
        gradient_ref[slot] = jnp.sum(weight * form) * (0.5 / points_total)
    copies.append(pltpu.make_async_copy(gradient_ref, gradient_hbm, sems.at[2]))
    copies[2].start()
    for copy in copies:
        copy.wait()


SWAP = [(0, 1), (1, 0)]


def local(mesh_shape, points, right_side, lengthscale, outputscale, noise_level):
    axes = ("blk", "grp")
    feats, own = points.shape
    cols = right_side.shape[0]
    rows = feats + 2 * cols
    blocks = mesh_shape["blk"]
    devices = blocks * mesh_shape["grp"]
    paired = mesh_shape["grp"] == 2 and blocks >= 2 and blocks & (blocks - 1) == 0
    part_count = 2 if paired else 1
    steps = devices // (2 * part_count)
    params = pltpu.CompilerParams(vmem_limit_bytes=(4 << 20) + devices * (40 << 10))
    shape = pltpu.VMEM
    result = jax.ShapeDtypeStruct

    def near(*arrays):
        return [pltpu.with_memory_space_constraint(array, pltpu.VMEM) for array in arrays]

    call = functools.partial(pl.pallas_call, compiler_params=params)

    row_shape = shape((cols, own), F32)
    shard, own_points, own_right = call(
        pack_kernel,
        out_shape=(shape((rows, own), BF16), shape((feats, own), BF16), row_shape),
        in_specs=_hbm(2),
        out_specs=tuple(_vmem(3)),
        scratch_shapes=[pltpu.SemaphoreType.DMA((2,))],
        name="pack",
    )(*[pltpu.with_memory_space_constraint(array, pltpu.HBM) for array in (points, right_side)])
    shards = [shard]
    if paired:
        half = blocks // 2
        shards.append(lax.ppermute(shard, "blk", [(at, (at + half) % blocks) for at in range(blocks)]))
    peers = blocks // 2 if paired else devices
    message, scalars = call(
        fan_kernel,
        out_shape=(shape((peers, len(shards), rows, own), BF16), shape((8, 128), F32)),
        in_specs=[_smem()] * 3 + _vmem(len(shards)),
        out_specs=tuple(_vmem(2)),
        name="fan",
    )(lengthscale, outputscale, noise_level, *near(*shards))
    if paired:
        groups = [
            [2 * (side * half + (at ^ (at >> 1))) + core for at in range(half)]
            for side in range(2)
            for core in range(2)
        ]
        vectors = [lax.all_to_all(message, axes, 0, 0, tiled=True, axis_index_groups=groups)]
        vectors.append(lax.ppermute(vectors[0], "grp", SWAP))
    else:
        vectors = [lax.all_to_all(message, axes, 0, 0, tiled=True).reshape(steps, 2, rows, own)]

    tile_shape = shape((steps, own, 2 * own), BF16)
    wide_shape = shape((steps, 2, cols, own), F32)

    operands = []

    def kern_call(part, vector, *before):
        outs = [tile_shape, row_shape]
        if part == 0:
            outs = [shape((own, feats), BF16), shape((own, own), F32)] + outs
        with_message = part + 1 == part_count
        if with_message:
            outs.append(shape((devices, cols // part_count, own), F32))
            before = (*before, own_right)
        results = call(
            functools.partial(kern_kernel, part > 0, with_message),
            out_shape=tuple(outs),
            in_specs=_vmem(2 + len(operands or [vector]) + len(before)),
            out_specs=tuple(_vmem(len(outs))),
            name="kern",
        )(*near(scalars, *(operands or [own_points]), vector, *before))
        if part == 0:
            operands.extend(results[:2])
            results = results[2:]
        return results

    def dkern_call(vector, *before):
        return call(
            functools.partial(dkern_kernel, len(before) > 0),
            out_shape=(tile_shape, wide_shape, row_shape, row_shape),
            in_specs=_vmem(4 + len(before)),
            out_specs=tuple(_vmem(4)),
            name="dkern",
        )(*near(scalars, *operands, vector, *before))

    kerns = [kern_call(0, vectors[0])]
    dkerns = []
    if paired:
        dkerns.append(dkern_call(vectors[0]))
        vectors[1], *dkerns[0] = lax.optimization_barrier((vectors[1], *dkerns[0]))
        kerns.append(kern_call(1, vectors[1], kerns[0][1]))
    kernel_first, message = kerns[-1][1:]
    received = [lax.all_to_all(message, axes, 0, 0, tiled=True)]
    if paired:
        received[0], vectors[1] = lax.optimization_barrier((received[0], vectors[1]))
        received.append(lax.ppermute(received[0], "grp", SWAP))
        dkerns.append(dkern_call(vectors[1], dkerns[0][2]))
    else:
        dkerns.append(dkern_call(vectors[0]))
    kerns = [tiles for tiles, *rest in kerns]
    slope_first = dkerns[-1][2]
    dkerns, wides, norms = [[outs[slot] for outs in dkerns] for slot in (0, 1, 3)]

    both_shape = shape((devices // 2, 2, cols, own), F32)
    message, direction, residual, applied, columns, products, turned = call(
        functools.partial(second_kernel, part_count, paired),
        out_shape=(
            shape((devices, 2, own), F32), row_shape, row_shape, row_shape, shape((cols, 128), F32),
            both_shape, both_shape,
        ),
        in_specs=_vmem(4 + 5 * part_count),
        out_specs=tuple(_vmem(7)),
        name="second",
    )(
        *near(scalars, own_right, kernel_first, slope_first, *kerns, *dkerns, *wides, *norms, *received),
    )
    received = lax.all_to_all(message, axes, 0, 0, tiled=True)

    solution, final, gradient = call(
        functools.partial(last_kernel, part_count, paired, float(own * devices)),
        out_shape=(result((cols, own), F32), result((cols, own), F32), result((3,), F32)),
        in_specs=_vmem(9 + part_count),
        out_specs=tuple(_hbm(3)),
        scratch_shapes=[
            pltpu.VMEM((cols, own), F32),
            pltpu.VMEM((cols, own), F32),
            pltpu.SMEM((3,), F32),
            pltpu.SemaphoreType.DMA((3,)),
        ],
        name="last",
    )(
        *near(scalars, own_right, direction, residual, applied, columns, products, turned, received, *wides),
    )
    return solution, final, gradient


def solution(mesh):
    whole = P(None, ("blk", "grp"))
    return jax.shard_map(
        functools.partial(local, dict(mesh.shape)),
        mesh=mesh,
        in_specs=(whole, whole, P(), P(), P()),
        out_specs=(whole, whole, P()),
        check_vma=False,
    )
```
